256 devices in a mesh: row: 4 (over y_lo, core), col: 64 (over x, y_hi, z).
Axes of the slice: x: 4, y: 4 (y_hi: 2, y_lo: 2; y = y_hi * 2 + y_lo), z: 8, core: 2. Of those that a mesh axis runs over, the one named last changes fastest.
Arguments:
- tensor: bfloat16 [128, 3072, 4096], P(None, 'col', 'row'), may hold values from -6 to 6
- first_factor: bfloat16 [64, 4096], P(None, ('row', 'col')), may hold values from -0.453125 to 0.453125
- second_factor: bfloat16 [64, 3072], P(None, 'col'), may hold values from -0.5232237 to 0.5232237
Outputs:
- frames: float32 [64, 128], replicated
- mode_one: float32 [64, 4096], P(None, ('row', 'col'))
The draws below stay inside these ranges and needn't reach their ends.
All inputs are finite; a program needn't handle non-finite values.
Results may differ from the reference program's by a relative error of at most 0.004.
Values may be sent and summed in bfloat16 or wider, within the bound.
A program may use at most 128 MiB of HBM per device.

```python
import jax
import jax.numpy as jnp
from jax import lax

R = 64
K = 128
I = 4096
J = 3072


def factor_values(key, components, length):
    key_spread, key_noise, key_common = jax.random.split(key, 3)
    position = jnp.arange(length, dtype=jnp.float32) / length
    rising = jnp.exp(jnp.log(3.0) * position)
    spread = jnp.exp(jax.random.uniform(key_spread, (length,), jnp.float32, 0.0, jnp.log(10.0)))
    noise = jnp.clip(jax.random.normal(key_noise, (components, length), jnp.float32), -4.0, 4.0)
    common = 0.6 * jnp.clip(jax.random.normal(key_common, (length,), jnp.float32), -4.0, 4.0)
    values = (rising * spread)[None, :] * (noise + common[None, :]) / (8.0 * jnp.sqrt(jnp.float32(length)))
    return values.astype(jnp.bfloat16)


def draw_first_factor(key, part):
    return factor_values(jax.random.fold_in(key, 11), R, I)


def draw_second_factor(key, part):
    return factor_values(jax.random.fold_in(key, 23), R, J)


def raised(values, rng, source, target, shards_of, factor):
    def block_of(axis_at):
        return (jnp.arange(values.shape[axis_at]) // (values.shape[axis_at] // shards_of)).reshape((-1,) + (1,) * (values.ndim - 1 - axis_at))

    near = jax.random.permutation(rng, shards_of)[block_of(target)]
    second = (block_of(target) + shards_of // 2) % shards_of
    return jnp.where((block_of(source) == near) | (block_of(source) == second), factor * values, values)


def block_levels(rng, extent, cuts, least, top_value):
    gain, own = 1.0, jax.random.fold_in(rng, 6)
    for dim, shards_of in cuts:
        heights = jnp.exp(jax.random.uniform(jax.random.fold_in(own, dim), (shards_of,), jnp.float32, least / len(cuts), top_value / len(cuts)))
        gain = gain * jnp.repeat(heights, extent[dim] // shards_of).reshape([-1 if axis == dim else 1 for axis in range(len(extent))])
    return gain


def gaussian_with(stream_key, dims, scale, bound, shards, heavy, kind=jnp.bfloat16):
    entries = scale * jax.random.normal(stream_key, dims, jnp.float32)
    if shards:
        entries = entries * block_levels(stream_key, dims, shards, -0.22, 0.18)
    return jnp.clip(raised(entries, jax.random.fold_in(stream_key, 3), *heavy), -bound, bound).astype(kind)


def setup_inputs(seed: int = 0) -> dict:
    key_of = jax.random.split(jax.random.key(seed), 4)
    tensor = gaussian_with(key_of[0], (K, J, I), 0.35, 6.0, ((1, 64), (2, 4)), (1, 2, 64, 4.0))
    first_factor = draw_first_factor(jax.random.fold_in(key_of[3], 71), 0)
    second_factor = draw_second_factor(jax.random.fold_in(key_of[3], 71), 0)
    return {"tensor": tensor, "first_factor": first_factor, "second_factor": second_factor}


ridge_weight = 0.05

def ridge_solve(gram, right_side):
    order_size = gram.shape[0]
    factor_low = jnp.linalg.cholesky(gram + ridge_weight * jnp.eye(order_size, dtype=jnp.float32))
    middle = lax.linalg.triangular_solve(factor_low, right_side, left_side=True, lower=True)
    return lax.linalg.triangular_solve(factor_low, middle, left_side=True, lower=True, transpose_a=True)

def gram_of(factor):
    return jnp.dot(factor.astype(jnp.float32), factor.T.astype(jnp.float32), preferred_element_type=jnp.float32)

def mode_first_sum(tensor, frames, second):

    def step_frame(running, inputs):
        slab, frame_col = inputs
        weights = (frame_col[:, None] * second).astype(jnp.bfloat16)
        running = running + lax.dot_general(weights.astype(jnp.float32), slab.astype(jnp.float32), (((1,), (0,)), ((), ())), preferred_element_type=jnp.float32)
        return (running, None)
    start_sum = jnp.zeros((frames.shape[0], tensor.shape[2]), jnp.float32)
    result, _ = lax.scan(step_frame, start_sum, (tensor, frames.T))
    return result

def reference(tensor, first_factor, second_factor):
    gram_first = gram_of(first_factor)
    gram_second = gram_of(second_factor)
    second_values = second_factor.astype(jnp.float32)

    def frame_column(slab):
        projected = lax.dot_general(first_factor.astype(jnp.float32), slab.astype(jnp.float32), (((1,), (1,)), ((), ())), preferred_element_type=jnp.float32)
        return jnp.sum(projected * second_values, axis=1)
    frame_sum = lax.map(frame_column, tensor).T
    frames = ridge_solve(gram_first * gram_second, frame_sum)
    gram_frames = jnp.dot(frames, frames.T, precision=lax.Precision.HIGHEST)
    first_sum = mode_first_sum(tensor, frames, second_values)
    new_first = ridge_solve(gram_second * gram_frames, first_sum).astype(jnp.bfloat16)
    gram_new = gram_of(new_first)

    def step_second(running, inputs):
        slab, frame_col = inputs
        projected = lax.dot_general(new_first.astype(jnp.float32), slab.astype(jnp.float32), (((1,), (1,)), ((), ())), preferred_element_type=jnp.float32)
        return (running + projected * frame_col[:, None], None)
    start_second = jnp.zeros(second_values.shape, jnp.float32)
    second_sum, _ = lax.scan(step_second, start_second, (tensor, frames.T))
    new_second = ridge_solve(gram_new * gram_frames, second_sum)
    mode_one = mode_first_sum(tensor, frames, new_second)
    return (frames, mode_one)
```

```python
import functools

import jax
import jax.numpy as jnp
from jax import lax
from jax.experimental import pallas as pl
from jax.experimental.pallas import tpu as pltpu
from jax.sharding import PartitionSpec as P

ridge_weight = 0.05
MESH_ID = pl.DeviceIdType.MESH


def ridge_solve(gram, right_side):
    order_size = gram.shape[0]
    factor_low = jnp.linalg.cholesky(gram + ridge_weight * jnp.eye(order_size, dtype=jnp.float32))
    middle = lax.linalg.triangular_solve(factor_low, right_side, left_side=True, lower=True)
    return lax.linalg.triangular_solve(
        factor_low, middle, left_side=True, lower=True, transpose_a=True
    )


def gram_of(factor):
    return jnp.dot(factor, factor.T, preferred_element_type=jnp.float32)


def spread_product(frames, second):
    product = frames[:, :, None] * second[:, None, :]
    return product.astype(jnp.bfloat16).reshape(frames.shape[0], -1)


def _exchange_kernel(n, broadcast, reduce, send_ref, out_ref, recv, send_sems, recv_sems):
    me = lax.axis_index("col")
    row = lax.axis_index("row")

    def source(peer):
        return send_ref if broadcast else send_ref.at[peer]

    def descriptor(peer, slot):
        return pltpu.make_async_remote_copy(
            src_ref=source(peer),
            dst_ref=recv.at[slot],
            send_sem=send_sems.at[peer],
            recv_sem=recv_sems.at[slot],
            device_id=(row, peer),
            device_id_type=MESH_ID,
        )

    barrier = pltpu.get_barrier_semaphore()

    def greet(t, carry):
        peer = lax.rem(me + 1 + t, n)
        pl.semaphore_signal(barrier, inc=1, device_id=(row, peer), device_id_type=MESH_ID)
        return carry

    lax.fori_loop(0, n - 1, greet, 0)
    pl.semaphore_wait(barrier, n - 1)

    def start(t, carry):
        peer = lax.rem(me + 1 + t, n)
        descriptor(peer, me).start()
        return carry

    lax.fori_loop(0, n - 1, start, 0)

    def finish(t, carry):
        peer = lax.rem(me + 1 + t, n)
        copy = descriptor(peer, peer)
        copy.wait_send()
        copy.wait_recv()
        return carry

    lax.fori_loop(0, n - 1, finish, 0)
    recv[me] = source(me)[...]
    if reduce:
        out_ref[...] = jnp.sum(recv[...], axis=0)
    else:
        out_ref[...] = recv[...]


def col_exchange(send, n, broadcast, reduce, collective_id):
    piece = send.shape if broadcast else send.shape[1:]
    out_shape = piece if reduce else (n,) + tuple(piece)
    return pl.pallas_call(
        functools.partial(_exchange_kernel, n, broadcast, reduce),
        out_shape=jax.ShapeDtypeStruct(tuple(out_shape), send.dtype),
        in_specs=[pl.BlockSpec(memory_space=pltpu.VMEM)],
        out_specs=pl.BlockSpec(memory_space=pltpu.VMEM),
        scratch_shapes=[
            pltpu.VMEM((n,) + tuple(piece), send.dtype),
            pltpu.SemaphoreType.DMA((n,)),
            pltpu.SemaphoreType.DMA((n,)),
        ],
        compiler_params=pltpu.CompilerParams(collective_id=collective_id, has_side_effects=True),
    )(send)


def col_gather_t(piece, n):
    gathered = col_exchange(piece, n, broadcast=True, reduce=False, collective_id=0)
    return gathered.reshape(n * piece.shape[0], piece.shape[1])


def col_reduce_scatter_t(full_t, n, collective_id):
    width = full_t.shape[0] // n
    return col_exchange(
        full_t.reshape(n, width, full_t.shape[1]), n, broadcast=False, reduce=True,
        collective_id=collective_id,
    )


def local(tensor, first_factor, second_factor):
    frame_count, col_count, row_count = tensor.shape
    components = first_factor.shape[0]
    n = lax.axis_size("col")
    flattened = tensor.reshape(frame_count * col_count, row_count)
    second_values = second_factor.astype(jnp.float32)
    gram_first_part = gram_of(first_factor)
    gram_second_part = gram_of(second_factor) * (1.0 / lax.axis_size("row"))
    block_t = col_gather_t(first_factor.T, n)
    projected = lax.dot_general(
        block_t, flattened, (((0,), (1,)), ((), ())), preferred_element_type=jnp.float32
    )
    projected = projected.reshape(components, frame_count, col_count)
    frame_part = jnp.einsum("rkj,rj->rk", projected, second_values, precision=lax.Precision.HIGHEST)
    frame_sum, gram_first, gram_second = lax.psum(
        (frame_part, gram_first_part, gram_second_part), ("row", "col")
    )
    frames = ridge_solve(gram_first * gram_second, frame_sum)
    gram_frames = jnp.dot(frames, frames.T, precision=lax.Precision.HIGHEST)
    weights = spread_product(frames, second_values)
    full_part_t = lax.dot_general(
        flattened, weights, (((0,), (1,)), ((), ())), preferred_element_type=jnp.float32
    )
    first_sum_mine = col_reduce_scatter_t(full_part_t, n, 1).T
    new_first_mine = ridge_solve(gram_second * gram_frames, first_sum_mine).astype(jnp.bfloat16)
    new_block_t = col_gather_t(new_first_mine.T, n)
    gram_new_part = lax.dot_general(
        new_block_t, new_block_t, (((0,), (0,)), ((), ())), preferred_element_type=jnp.float32
    )
    projected_new = lax.dot_general(
        new_block_t, flattened, (((0,), (1,)), ((), ())), preferred_element_type=jnp.float32
    )
    projected_new = projected_new.reshape(components, frame_count, col_count)
    second_part = jnp.einsum("rkj,rk->rj", projected_new, frames, precision=lax.Precision.HIGHEST)
    second_sum, gram_new = lax.psum((second_part, gram_new_part), "row")
    new_second = ridge_solve(gram_new * gram_frames, second_sum)
    weights_next = spread_product(frames, new_second)
    full_next_t = lax.dot_general(
        flattened, weights_next, (((0,), (1,)), ((), ())), preferred_element_type=jnp.float32
    )
    mode_one = col_reduce_scatter_t(full_next_t, n, 2).T
    return (frames, mode_one)


def solution(mesh):
    return jax.shard_map(
        local,
        mesh=mesh,
        in_specs=(P(None, "col", "row"), P(None, ("row", "col")), P(None, "col")),
        out_specs=(P(), P(None, ("row", "col"))),
        check_vma=False,
    )
```

```python
import functools

import jax
import jax.numpy as jnp
from jax import lax
from jax.experimental import pallas as pl
from jax.experimental.pallas import tpu as pltpu
from jax.sharding import PartitionSpec as P

ridge_weight = 0.05
MESH_ID = pl.DeviceIdType.MESH


def ridge_solve(gram, right_side):
    order_size = gram.shape[0]
    factor_low = jnp.linalg.cholesky(gram + ridge_weight * jnp.eye(order_size, dtype=jnp.float32))
    middle = lax.linalg.triangular_solve(factor_low, right_side, left_side=True, lower=True)
    return lax.linalg.triangular_solve(
        factor_low, middle, left_side=True, lower=True, transpose_a=True
    )


def gram_of(factor):
    return jnp.dot(factor, factor.T, preferred_element_type=jnp.float32)


def project_columns(flattened, portion):
    return lax.dot_general(
        portion, flattened, (((1,), (1,)), ((), ())), preferred_element_type=jnp.float32
    )


def spread_product(frames, second):
    product = frames[:, :, None] * second[:, None, :]
    return product.astype(jnp.bfloat16).reshape(frames.shape[0], -1)


def _exchange_kernel(n, mode, send_ref, out_ref, recv, send_sems, recv_sems, *extra):
    me = lax.axis_index("col")
    row = lax.axis_index("row")
    broadcast = mode == "gather"

    def exchange(source, landing, sends, recvs):
        def descriptor(peer, slot):
            return pltpu.make_async_remote_copy(
                src_ref=source(peer),
                dst_ref=landing.at[slot],
                send_sem=sends.at[peer],
                recv_sem=recvs.at[slot],
                device_id=(row, peer),
                device_id_type=MESH_ID,
            )

        def start(t, carry):
            peer = lax.rem(me + 1 + t, n)
            descriptor(peer, me).start()
            return carry

        lax.fori_loop(0, n - 1, start, 0)

        def finish(t, carry):
            peer = lax.rem(me + 1 + t, n)
            copy = descriptor(peer, peer)
            copy.wait_send()
            copy.wait_recv()
            return carry

        lax.fori_loop(0, n - 1, finish, 0)
        landing[me] = source(me)[...]

    barrier = pltpu.get_barrier_semaphore()

    def greet(t, carry):
        peer = lax.rem(me + 1 + t, n)
        pl.semaphore_signal(barrier, inc=1, device_id=(row, peer), device_id_type=MESH_ID)
        return carry

    lax.fori_loop(0, n - 1, greet, 0)
    pl.semaphore_wait(barrier, n - 1)
    exchange((lambda peer: send_ref) if broadcast else (lambda peer: send_ref.at[peer]), recv, send_sems, recv_sems)
    if mode == "gather":
        out_ref[...] = recv[...]
    elif mode == "scatter":
        out_ref[...] = jnp.sum(recv[...], axis=0)
    else:
        chunk, recv_back, back_send_sems, back_recv_sems = extra
        chunk[...] = jnp.sum(recv[...], axis=0)
        exchange(lambda peer: chunk, recv_back, back_send_sems, back_recv_sems)
        out_ref[...] = recv_back[...]


def col_exchange(send, n, mode, collective_id):
    piece = tuple(send.shape) if mode == "gather" else tuple(send.shape[1:])
    out_shape = piece if mode == "scatter" else (n,) + piece
    scratch = [
        pltpu.VMEM((n,) + piece, send.dtype),
        pltpu.SemaphoreType.DMA((n,)),
        pltpu.SemaphoreType.DMA((n,)),
    ]
    if mode == "allreduce":
        scratch += [
            pltpu.VMEM(piece, send.dtype),
            pltpu.VMEM((n,) + piece, send.dtype),
            pltpu.SemaphoreType.DMA((n,)),
            pltpu.SemaphoreType.DMA((n,)),
        ]
    return pl.pallas_call(
        functools.partial(_exchange_kernel, n, mode),
        out_shape=jax.ShapeDtypeStruct(out_shape, send.dtype),
        in_specs=[pl.BlockSpec(memory_space=pltpu.VMEM)],
        out_specs=pl.BlockSpec(memory_space=pltpu.VMEM),
        scratch_shapes=scratch,
        compiler_params=pltpu.CompilerParams(collective_id=collective_id, has_side_effects=True),
    )(send)


def col_gather(piece_t, n):
    gathered = col_exchange(piece_t, n, "gather", 0)
    return gathered.reshape(n * piece_t.shape[0], piece_t.shape[1]).T


def col_reduce_scatter(full, n, collective_id):
    width = full.shape[1] // n
    summed_t = col_exchange(full.T.reshape(n, width, full.shape[0]), n, "scatter", collective_id)
    return summed_t.T


def col_all_reduce(full, n, collective_id):
    width = full.shape[1] // n
    summed_t = col_exchange(full.T.reshape(n, width, full.shape[0]), n, "allreduce", collective_id)
    return summed_t.reshape(n * width, full.shape[0]).T


def local(tensor, first_factor, second_factor):
    frame_count, col_count, row_count = tensor.shape
    components = first_factor.shape[0]
    n = lax.axis_size("col")
    flattened = tensor.reshape(frame_count * col_count, row_count)
    second_values = second_factor.astype(jnp.float32)
    gram_first_part = gram_of(first_factor)
    gram_second_part = gram_of(second_factor)
    block = col_gather(first_factor.T, n)
    projected = project_columns(flattened, block)
    projected = projected.reshape(components, frame_count, col_count)
    frame_part = jnp.einsum("rkj,rj->rk", projected, second_values, precision=lax.Precision.HIGHEST)
    row_summed = lax.psum(jnp.concatenate([frame_part, gram_first_part], axis=1), "row")
    summed = col_all_reduce(jnp.concatenate([row_summed, gram_second_part], axis=1), n, 3)
    frame_sum = summed[:, :frame_count]
    gram_first = summed[:, frame_count:frame_count + components]
    gram_second = summed[:, frame_count + components:]
    frames = ridge_solve(gram_first * gram_second, frame_sum)
    gram_frames = jnp.dot(frames, frames.T, precision=lax.Precision.HIGHEST)
    weights = spread_product(frames, second_values)
    full_part = lax.dot_general(
        weights, flattened, (((1,), (0,)), ((), ())), preferred_element_type=jnp.float32
    )
    first_sum_mine = col_reduce_scatter(full_part, n, 1)
    new_first_mine = ridge_solve(gram_second * gram_frames, first_sum_mine).astype(jnp.bfloat16)
    new_block = col_gather(new_first_mine.T, n)
    gram_new_part = gram_of(new_block)
    projected_new = project_columns(flattened, new_block)
    projected_new = projected_new.reshape(components, frame_count, col_count)
    second_part = jnp.einsum("rkj,rk->rj", projected_new, frames, precision=lax.Precision.HIGHEST)
    second_sum, gram_new = lax.psum((second_part, gram_new_part), "row")
    new_second = ridge_solve(gram_new * gram_frames, second_sum)
    weights_next = spread_product(frames, new_second)
    full_next = lax.dot_general(
        weights_next, flattened, (((1,), (0,)), ((), ())), preferred_element_type=jnp.float32
    )
    mode_one = col_reduce_scatter(full_next, n, 2)
    return (frames, mode_one)


def solution(mesh):
    return jax.shard_map(
        local,
        mesh=mesh,
        in_specs=(P(None, "col", "row"), P(None, ("row", "col")), P(None, "col")),
        out_specs=(P(), P(None, ("row", "col"))),
        check_vma=False,
    )
```

```python
import functools

import jax
import jax.numpy as jnp
from jax import lax
from jax.experimental import pallas as pl
from jax.experimental.pallas import tpu as pltpu
from jax.sharding import PartitionSpec as P

ridge_weight = 0.05
MESH_ID = pl.DeviceIdType.MESH


def ridge_solve(gram, right_side):
    order_size = gram.shape[0]
    factor_low = jnp.linalg.cholesky(gram + ridge_weight * jnp.eye(order_size, dtype=jnp.float32))
    middle = lax.linalg.triangular_solve(factor_low, right_side, left_side=True, lower=True)
    return lax.linalg.triangular_solve(
        factor_low, middle, left_side=True, lower=True, transpose_a=True
    )


def gram_of(factor):
    return jnp.dot(factor, factor.T, preferred_element_type=jnp.float32)


STREAM_ROWS = 768


def _project_kernel(portion_ref, slab_ref, out_ref):
    out_ref[...] = lax.dot_general(
        portion_ref[...], slab_ref[...], (((1,), (1,)), ((), ())),
        preferred_element_type=jnp.float32,
    )


def project_columns(flattened, portion):
    cols, rows = flattened.shape
    components = portion.shape[0]
    return pl.pallas_call(
        _project_kernel,
        grid=(cols // STREAM_ROWS,),
        in_specs=[
            pl.BlockSpec((components, rows), lambda s: (0, 0)),
            pl.BlockSpec((STREAM_ROWS, rows), lambda s: (s, 0)),
        ],
        out_specs=pl.BlockSpec((components, STREAM_ROWS), lambda s: (0, s)),
        out_shape=jax.ShapeDtypeStruct((components, cols), jnp.float32),
        cost_estimate=pl.CostEstimate(
            flops=2 * components * cols * rows, transcendentals=0,
            bytes_accessed=2 * cols * rows + 4 * components * cols,
        ),
    )(portion, flattened)


def _accumulate_kernel(weights_ref, slab_ref, out_ref):
    @pl.when(pl.program_id(0) == 0)
    def _():
        out_ref[...] = jnp.zeros_like(out_ref)

    out_ref[...] += jnp.dot(weights_ref[...], slab_ref[...], preferred_element_type=jnp.float32)


def accumulate_rows(weights, flattened):
    cols, rows = flattened.shape
    components = weights.shape[0]
    return pl.pallas_call(
        _accumulate_kernel,
        grid=(cols // STREAM_ROWS,),
        in_specs=[
            pl.BlockSpec((components, STREAM_ROWS), lambda s: (0, s)),
            pl.BlockSpec((STREAM_ROWS, rows), lambda s: (s, 0)),
        ],
        out_specs=pl.BlockSpec((components, rows), lambda s: (0, 0)),
        out_shape=jax.ShapeDtypeStruct((components, rows), jnp.float32),
        cost_estimate=pl.CostEstimate(
            flops=2 * components * cols * rows, transcendentals=0,
            bytes_accessed=2 * cols * rows + 2 * components * cols,
        ),
    )(weights, flattened)


def spread_product(frames, second):
    product = frames[:, :, None] * second[:, None, :]
    return product.astype(jnp.bfloat16).reshape(frames.shape[0], -1)


def _exchange_kernel(n, mode, send_ref, out_ref, recv, send_sems, recv_sems, *extra):
    me = lax.axis_index("col")
    row = lax.axis_index("row")
    broadcast = mode == "gather"

    def exchange(source, landing, sends, recvs):
        def descriptor(peer, slot):
            return pltpu.make_async_remote_copy(
                src_ref=source(peer),
                dst_ref=landing.at[slot],
                send_sem=sends.at[peer],
                recv_sem=recvs.at[slot],
                device_id=(row, peer),
                device_id_type=MESH_ID,
            )

        def start(t, carry):
            peer = lax.rem(me + 1 + t, n)
            descriptor(peer, me).start()
            return carry

        lax.fori_loop(0, n - 1, start, 0)

        def finish(t, carry):
            peer = lax.rem(me + 1 + t, n)
            copy = descriptor(peer, peer)
            copy.wait_send()
            copy.wait_recv()
            return carry

        lax.fori_loop(0, n - 1, finish, 0)
        landing[me] = source(me)[...]

    barrier = pltpu.get_barrier_semaphore()

    def greet(t, carry):
        peer = lax.rem(me + 1 + t, n)
        pl.semaphore_signal(barrier, inc=1, device_id=(row, peer), device_id_type=MESH_ID)
        return carry

    lax.fori_loop(0, n - 1, greet, 0)
    pl.semaphore_wait(barrier, n - 1)
    exchange((lambda peer: send_ref) if broadcast else (lambda peer: send_ref.at[peer]), recv, send_sems, recv_sems)
    if mode == "gather":
        out_ref[...] = recv[...]
    elif mode == "scatter":
        out_ref[...] = jnp.sum(recv[...], axis=0)
    else:
        chunk, recv_back, back_send_sems, back_recv_sems = extra
        chunk[...] = jnp.sum(recv[...], axis=0)
        exchange(lambda peer: chunk, recv_back, back_send_sems, back_recv_sems)
        out_ref[...] = recv_back[...]


def col_exchange(send, n, mode, collective_id):
    piece = tuple(send.shape) if mode == "gather" else tuple(send.shape[1:])
    out_shape = piece if mode == "scatter" else (n,) + piece
    scratch = [
        pltpu.VMEM((n,) + piece, send.dtype),
        pltpu.SemaphoreType.DMA((n,)),
        pltpu.SemaphoreType.DMA((n,)),
    ]
    if mode == "allreduce":
        scratch += [
            pltpu.VMEM(piece, send.dtype),
            pltpu.VMEM((n,) + piece, send.dtype),
            pltpu.SemaphoreType.DMA((n,)),
            pltpu.SemaphoreType.DMA((n,)),
        ]
    return pl.pallas_call(
        functools.partial(_exchange_kernel, n, mode),
        out_shape=jax.ShapeDtypeStruct(out_shape, send.dtype),
        in_specs=[pl.BlockSpec(memory_space=pltpu.VMEM)],
        out_specs=pl.BlockSpec(memory_space=pltpu.VMEM),
        scratch_shapes=scratch,
        compiler_params=pltpu.CompilerParams(collective_id=collective_id, has_side_effects=True),
    )(send)


def col_gather(piece_t, n):
    gathered = col_exchange(piece_t, n, "gather", 0)
    return gathered.reshape(n * piece_t.shape[0], piece_t.shape[1]).T


def col_reduce_scatter(full, n, collective_id):
    width = full.shape[1] // n
    summed_t = col_exchange(full.T.reshape(n, width, full.shape[0]), n, "scatter", collective_id)
    return summed_t.T


def col_all_reduce(full, n, collective_id):
    width = full.shape[1] // n
    summed_t = col_exchange(full.T.reshape(n, width, full.shape[0]), n, "allreduce", collective_id)
    return summed_t.reshape(n * width, full.shape[0]).T


def local(tensor, first_factor, second_factor):
    frame_count, col_count, row_count = tensor.shape
    components = first_factor.shape[0]
    n = lax.axis_size("col")
    flattened = tensor.reshape(frame_count * col_count, row_count)
    second_values = second_factor.astype(jnp.float32)
    gram_first_part = gram_of(first_factor)
    gram_second_part = gram_of(second_factor)
    block = col_gather(first_factor.T, n)
    projected = project_columns(flattened, block)
    projected = projected.reshape(components, frame_count, col_count)
    frame_part = jnp.einsum("rkj,rj->rk", projected, second_values, precision=lax.Precision.HIGHEST)
    row_summed = lax.psum(jnp.concatenate([frame_part, gram_first_part], axis=1), "row")
    summed = col_all_reduce(jnp.concatenate([row_summed, gram_second_part], axis=1), n, 3)
    frame_sum = summed[:, :frame_count]
    gram_first = summed[:, frame_count:frame_count + components]
    gram_second = summed[:, frame_count + components:]
    frames = ridge_solve(gram_first * gram_second, frame_sum)
    gram_frames = jnp.dot(frames, frames.T, precision=lax.Precision.HIGHEST)
    weights = spread_product(frames, second_values)
    full_part = accumulate_rows(weights, flattened)
    first_sum_mine = col_reduce_scatter(full_part, n, 1)
    new_first_mine = ridge_solve(gram_second * gram_frames, first_sum_mine).astype(jnp.bfloat16)
    new_block = col_gather(new_first_mine.T, n)
    gram_new_part = gram_of(new_block)
    projected_new = project_columns(flattened, new_block)
    projected_new = projected_new.reshape(components, frame_count, col_count)
    second_part = jnp.einsum("rkj,rk->rj", projected_new, frames, precision=lax.Precision.HIGHEST)
    second_sum, gram_new = lax.psum((second_part, gram_new_part), "row")
    new_second = ridge_solve(gram_new * gram_frames, second_sum)
    weights_next = spread_product(frames, new_second)
    full_next = accumulate_rows(weights_next, flattened)
    mode_one = col_reduce_scatter(full_next, n, 2)
    return (frames, mode_one)


def solution(mesh):
    return jax.shard_map(
        local,
        mesh=mesh,
        in_specs=(P(None, "col", "row"), P(None, ("row", "col")), P(None, "col")),
        out_specs=(P(), P(None, ("row", "col"))),
        check_vma=False,
    )
```

```python
import functools

import jax
import jax.numpy as jnp
from jax import lax
from jax.experimental import pallas as pl
from jax.experimental.pallas import tpu as pltpu
from jax.sharding import PartitionSpec as P

ridge_weight = 0.05
MESH_ID = pl.DeviceIdType.MESH


def ridge_solve(gram, right_side):
    order_size = gram.shape[0]
    factor_low = jnp.linalg.cholesky(gram + ridge_weight * jnp.eye(order_size, dtype=jnp.float32))
    middle = lax.linalg.triangular_solve(factor_low, right_side, left_side=True, lower=True)
    return lax.linalg.triangular_solve(
        factor_low, middle, left_side=True, lower=True, transpose_a=True
    )


def gram_of(factor):
    return jnp.dot(factor, factor.T, preferred_element_type=jnp.float32)


STREAM_ROWS = 768


def _project_kernel(portion_ref, slab_ref, out_ref):
    out_ref[...] = lax.dot_general(
        portion_ref[...], slab_ref[...], (((1,), (1,)), ((), ())),
        preferred_element_type=jnp.float32,
    )


def project_columns(flattened, portion):
    cols, rows = flattened.shape
    components = portion.shape[0]
    return pl.pallas_call(
        _project_kernel,
        grid=(cols // STREAM_ROWS,),
        in_specs=[
            pl.BlockSpec((components, rows), lambda s: (0, 0)),
            pl.BlockSpec((STREAM_ROWS, rows), lambda s: (s, 0)),
        ],
        out_specs=pl.BlockSpec((components, STREAM_ROWS), lambda s: (0, s)),
        out_shape=jax.ShapeDtypeStruct((components, cols), jnp.float32),
        cost_estimate=pl.CostEstimate(
            flops=2 * components * cols * rows, transcendentals=0,
            bytes_accessed=2 * cols * rows + 4 * components * cols,
        ),
    )(portion, flattened)


def _accumulate_kernel(weights_ref, slab_ref, out_ref):
    @pl.when(pl.program_id(0) == 0)
    def _():
        out_ref[...] = jnp.zeros_like(out_ref)

    out_ref[...] += jnp.dot(weights_ref[...], slab_ref[...], preferred_element_type=jnp.float32)


def accumulate_rows(weights, flattened):
    cols, rows = flattened.shape
    components = weights.shape[0]
    return pl.pallas_call(
        _accumulate_kernel,
        grid=(cols // STREAM_ROWS,),
        in_specs=[
            pl.BlockSpec((components, STREAM_ROWS), lambda s: (0, s)),
            pl.BlockSpec((STREAM_ROWS, rows), lambda s: (s, 0)),
        ],
        out_specs=pl.BlockSpec((components, rows), lambda s: (0, 0)),
        out_shape=jax.ShapeDtypeStruct((components, rows), jnp.float32),
        cost_estimate=pl.CostEstimate(
            flops=2 * components * cols * rows, transcendentals=0,
            bytes_accessed=2 * cols * rows + 2 * components * cols,
        ),
    )(weights, flattened)


def spread_product(frames, second):
    product = frames[:, :, None] * second[:, None, :]
    return product.astype(jnp.bfloat16).reshape(frames.shape[0], -1)


def _exchange_kernel(n, mode, send_ref, out_ref, recv, send_sems, recv_sems, *extra):
    me = lax.axis_index("col")
    row = lax.axis_index("row")
    broadcast = mode == "gather"

    def exchange(source, landing, sends, recvs):
        def descriptor(peer, slot):
            return pltpu.make_async_remote_copy(
                src_ref=source(peer),
                dst_ref=landing.at[slot],
                send_sem=sends.at[peer],
                recv_sem=recvs.at[slot],
                device_id=(row, peer),
                device_id_type=MESH_ID,
            )

        def start(t, carry):
            peer = lax.rem(me + 1 + t, n)
            descriptor(peer, me).start()
            return carry

        lax.fori_loop(0, n - 1, start, 0)

        def finish(t, carry):
            peer = lax.rem(me + 1 + t, n)
            copy = descriptor(peer, peer)
            copy.wait_send()
            copy.wait_recv()
            return carry

        lax.fori_loop(0, n - 1, finish, 0)
        landing[me] = source(me)[...]

    exchange((lambda peer: send_ref) if broadcast else (lambda peer: send_ref.at[peer]), recv, send_sems, recv_sems)
    if mode == "gather":
        out_ref[...] = recv[...]
    elif mode == "scatter":
        out_ref[...] = jnp.sum(recv[...], axis=0)
    else:
        chunk, recv_back, back_send_sems, back_recv_sems = extra
        chunk[...] = jnp.sum(recv[...], axis=0)
        exchange(lambda peer: chunk, recv_back, back_send_sems, back_recv_sems)
        out_ref[...] = recv_back[...]


def col_exchange(send, n, mode, collective_id):
    piece = tuple(send.shape) if mode == "gather" else tuple(send.shape[1:])
    out_shape = piece if mode == "scatter" else (n,) + piece
    scratch = [
        pltpu.VMEM((n,) + piece, send.dtype),
        pltpu.SemaphoreType.DMA((n,)),
        pltpu.SemaphoreType.DMA((n,)),
    ]
    if mode == "allreduce":
        scratch += [
            pltpu.VMEM(piece, send.dtype),
            pltpu.VMEM((n,) + piece, send.dtype),
            pltpu.SemaphoreType.DMA((n,)),
            pltpu.SemaphoreType.DMA((n,)),
        ]
    return pl.pallas_call(
        functools.partial(_exchange_kernel, n, mode),
        out_shape=jax.ShapeDtypeStruct(out_shape, send.dtype),
        in_specs=[pl.BlockSpec(memory_space=pltpu.VMEM)],
        out_specs=pl.BlockSpec(memory_space=pltpu.VMEM),
        scratch_shapes=scratch,
        compiler_params=pltpu.CompilerParams(has_side_effects=True),
    )(send)


def col_gather(piece_t, n):
    gathered = col_exchange(piece_t, n, "gather", 0)
    return gathered.reshape(n * piece_t.shape[0], piece_t.shape[1]).T


def col_reduce_scatter(full, n, collective_id):
    width = full.shape[1] // n
    summed_t = col_exchange(full.T.reshape(n, width, full.shape[0]), n, "scatter", collective_id)
    return summed_t.T


def col_all_reduce(full, n, collective_id):
    width = full.shape[1] // n
    summed_t = col_exchange(full.T.reshape(n, width, full.shape[0]), n, "allreduce", collective_id)
    return summed_t.reshape(n * width, full.shape[0]).T


def local(tensor, first_factor, second_factor):
    frame_count, col_count, row_count = tensor.shape
    components = first_factor.shape[0]
    n = lax.axis_size("col")
    flattened = tensor.reshape(frame_count * col_count, row_count)
    second_values = second_factor.astype(jnp.float32)
    gram_first_part = gram_of(first_factor)
    gram_second_part = gram_of(second_factor)
    block = col_gather(first_factor.T, n)
    projected = project_columns(flattened, block)
    projected = projected.reshape(components, frame_count, col_count)
    frame_part = jnp.einsum("rkj,rj->rk", projected, second_values, precision=lax.Precision.HIGHEST)
    row_summed = lax.psum(jnp.concatenate([frame_part, gram_first_part], axis=1), "row")
    summed = col_all_reduce(jnp.concatenate([row_summed, gram_second_part], axis=1), n, 3)
    frame_sum = summed[:, :frame_count]
    gram_first = summed[:, frame_count:frame_count + components]
    gram_second = summed[:, frame_count + components:]
    frames = ridge_solve(gram_first * gram_second, frame_sum)
    gram_frames = jnp.dot(frames, frames.T, precision=lax.Precision.HIGHEST)
    weights = spread_product(frames, second_values)
    full_part = accumulate_rows(weights, flattened)
    first_sum_mine = col_reduce_scatter(full_part, n, 1)
    new_first_mine = ridge_solve(gram_second * gram_frames, first_sum_mine).astype(jnp.bfloat16)
    new_block = col_gather(new_first_mine.T, n)
    gram_new_part = gram_of(new_block)
    projected_new = project_columns(flattened, new_block)
    projected_new = projected_new.reshape(components, frame_count, col_count)
    second_part = jnp.einsum("rkj,rk->rj", projected_new, frames, precision=lax.Precision.HIGHEST)
    second_sum, gram_new = lax.psum((second_part, gram_new_part), "row")
    new_second = ridge_solve(gram_new * gram_frames, second_sum)
    weights_next = spread_product(frames, new_second)
    full_next = accumulate_rows(weights_next, flattened)
    mode_one = col_reduce_scatter(full_next, n, 2)
    return (frames, mode_one)


def solution(mesh):
    return jax.shard_map(
        local,
        mesh=mesh,
        in_specs=(P(None, "col", "row"), P(None, ("row", "col")), P(None, "col")),
        out_specs=(P(), P(None, ("row", "col"))),
        check_vma=False,
    )
```

```python
import functools

import jax
import jax.numpy as jnp
from jax import lax
from jax.experimental import pallas as pl
from jax.experimental.pallas import tpu as pltpu
from jax.sharding import PartitionSpec as P

ridge_weight = 0.05
MESH_ID = pl.DeviceIdType.MESH


def ridge_solve(gram, right_side):
    order_size = gram.shape[0]
    factor_low = jnp.linalg.cholesky(gram + ridge_weight * jnp.eye(order_size, dtype=jnp.float32))
    middle = lax.linalg.triangular_solve(factor_low, right_side, left_side=True, lower=True)
    return lax.linalg.triangular_solve(
        factor_low, middle, left_side=True, lower=True, transpose_a=True
    )


def gram_of(factor):
    return jnp.dot(factor, factor.T, preferred_element_type=jnp.float32)


STREAM_FRAMES = 16


def _frame_kernel(block_t_ref, second_t_ref, slab_ref, out_ref):
    frames, width, rows = slab_ref.shape
    projected = jnp.dot(
        slab_ref[...].reshape(frames * width, rows), block_t_ref[...],
        preferred_element_type=jnp.float32,
    ).reshape(frames, width, block_t_ref.shape[1])
    out_ref[...] = jnp.sum(projected * second_t_ref[...][None], axis=1)


def _second_kernel(block_t_ref, frames_t_ref, slab_ref, out_ref):
    frames, width, rows = slab_ref.shape

    @pl.when(pl.program_id(0) == 0)
    def _():
        out_ref[...] = jnp.zeros_like(out_ref)

    projected = jnp.dot(
        slab_ref[...].reshape(frames * width, rows), block_t_ref[...],
        preferred_element_type=jnp.float32,
    ).reshape(frames, width, block_t_ref.shape[1])
    out_ref[...] += jnp.sum(projected * frames_t_ref[...][:, None, :], axis=0)


def _slab_spec(width, rows):
    return pl.BlockSpec((STREAM_FRAMES, width, rows), lambda s: (s, 0, 0))


def _whole(shape):
    return pl.BlockSpec(shape, lambda s: (0,) * len(shape))


def frame_pass(tensor, block_t, second_t):
    frame_count, width, rows = tensor.shape
    components = block_t.shape[1]
    return pl.pallas_call(
        _frame_kernel,
        grid=(frame_count // STREAM_FRAMES,),
        in_specs=[_whole(block_t.shape), _whole(second_t.shape), _slab_spec(width, rows)],
        out_specs=pl.BlockSpec((STREAM_FRAMES, components), lambda s: (s, 0)),
        out_shape=jax.ShapeDtypeStruct((frame_count, components), jnp.float32),
        cost_estimate=pl.CostEstimate(
            flops=2 * components * frame_count * width * rows, transcendentals=0,
            bytes_accessed=2 * frame_count * width * rows,
        ),
    )(block_t, second_t, tensor)


def second_pass(tensor, block_t, frames_t):
    frame_count, width, rows = tensor.shape
    components = block_t.shape[1]
    return pl.pallas_call(
        _second_kernel,
        grid=(frame_count // STREAM_FRAMES,),
        in_specs=[
            _whole(block_t.shape),
            pl.BlockSpec((STREAM_FRAMES, components), lambda s: (s, 0)),
            _slab_spec(width, rows),
        ],
        out_specs=_whole((width, components)),
        out_shape=jax.ShapeDtypeStruct((width, components), jnp.float32),
        cost_estimate=pl.CostEstimate(
            flops=2 * components * frame_count * width * rows, transcendentals=0,
            bytes_accessed=2 * frame_count * width * rows,
        ),
    )(block_t, frames_t, tensor)


def _accumulate_kernel(frames_ref, tiled_ref, slab_ref, out_ref):
    frames, width, rows = slab_ref.shape
    step = pl.program_id(0)

    @pl.when(step == 0)
    def _():
        out_ref[...] = jnp.zeros_like(out_ref)

    frame_count = frames_ref.shape[1]
    span = frames * width
    which = lax.broadcasted_iota(jnp.int32, (frame_count, span), 0) - step * frames
    column = lax.broadcasted_iota(jnp.int32, (frame_count, span), 1)
    expand = ((column >= which * width) & (column < which * width + width)).astype(jnp.bfloat16)
    rest = frames_ref[...]
    repeated = jnp.zeros((frames_ref.shape[0], span), jnp.float32)
    for _ in range(3):
        piece = rest.astype(jnp.bfloat16)
        rest = rest - piece.astype(jnp.float32)
        repeated = repeated + jnp.dot(piece, expand, preferred_element_type=jnp.float32)
    weights = (repeated * tiled_ref[...]).astype(jnp.bfloat16)
    out_ref[...] += jnp.dot(
        weights, slab_ref[...].reshape(span, rows), preferred_element_type=jnp.float32
    )


def accumulate_pass(tensor, frames, second):
    frame_count, width, rows = tensor.shape
    components = frames.shape[0]
    tiled = jnp.tile(second, (1, STREAM_FRAMES))
    return pl.pallas_call(
        _accumulate_kernel,
        grid=(frame_count // STREAM_FRAMES,),
        in_specs=[_whole(frames.shape), _whole(tiled.shape), _slab_spec(width, rows)],
        out_specs=_whole((components, rows)),
        out_shape=jax.ShapeDtypeStruct((components, rows), jnp.float32),
        cost_estimate=pl.CostEstimate(
            flops=2 * components * frame_count * width * rows, transcendentals=0,
            bytes_accessed=2 * frame_count * width * rows,
        ),
    )(frames, tiled, tensor)


def _exchange_kernel(n, mode, send_ref, out_ref, recv, send_sems, recv_sems, *extra):
    me = lax.axis_index("col")
    row = lax.axis_index("row")
    broadcast = mode == "gather"

    def exchange(source, landing, sends, recvs):
        def descriptor(peer, slot):
            return pltpu.make_async_remote_copy(
                src_ref=source(peer),
                dst_ref=landing.at[slot],
                send_sem=sends.at[peer],
                recv_sem=recvs.at[slot],
                device_id=(row, peer),
                device_id_type=MESH_ID,
            )

        def start(t, carry):
            peer = lax.rem(me + 1 + t, n)
            descriptor(peer, me).start()
            return carry

        lax.fori_loop(0, n - 1, start, 0)

        def finish(t, carry):
            peer = lax.rem(me + 1 + t, n)
            copy = descriptor(peer, peer)
            copy.wait_send()
            copy.wait_recv()
            return carry

        lax.fori_loop(0, n - 1, finish, 0)
        landing[me] = source(me)[...]

    barrier = pltpu.get_barrier_semaphore()

    def greet(t, carry):
        peer = lax.rem(me + 1 + t, n)
        pl.semaphore_signal(barrier, inc=1, device_id=(row, peer), device_id_type=MESH_ID)
        return carry

    lax.fori_loop(0, n - 1, greet, 0)
    pl.semaphore_wait(barrier, n - 1)
    exchange((lambda peer: send_ref) if broadcast else (lambda peer: send_ref.at[peer]), recv, send_sems, recv_sems)
    if mode == "gather":
        out_ref[...] = recv[...]
    elif mode == "scatter":
        out_ref[...] = jnp.sum(recv[...], axis=0)
    else:
        chunk, recv_back, back_send_sems, back_recv_sems = extra
        chunk[...] = jnp.sum(recv[...], axis=0)
        exchange(lambda peer: chunk, recv_back, back_send_sems, back_recv_sems)
        out_ref[...] = recv_back[...]


def col_exchange(send, n, mode, collective_id):
    piece = tuple(send.shape) if mode == "gather" else tuple(send.shape[1:])
    out_shape = piece if mode == "scatter" else (n,) + piece
    scratch = [
        pltpu.VMEM((n,) + piece, send.dtype),
        pltpu.SemaphoreType.DMA((n,)),
        pltpu.SemaphoreType.DMA((n,)),
    ]
    if mode == "allreduce":
        scratch += [
            pltpu.VMEM(piece, send.dtype),
            pltpu.VMEM((n,) + piece, send.dtype),
            pltpu.SemaphoreType.DMA((n,)),
            pltpu.SemaphoreType.DMA((n,)),
        ]
    return pl.pallas_call(
        functools.partial(_exchange_kernel, n, mode),
        out_shape=jax.ShapeDtypeStruct(out_shape, send.dtype),
        in_specs=[pl.BlockSpec(memory_space=pltpu.VMEM)],
        out_specs=pl.BlockSpec(memory_space=pltpu.VMEM),
        scratch_shapes=scratch,
        compiler_params=pltpu.CompilerParams(collective_id=collective_id, has_side_effects=True),
    )(send)


def col_gather_t(piece_t, n):
    gathered = col_exchange(piece_t, n, "gather", 0)
    return gathered.reshape(n * piece_t.shape[0], piece_t.shape[1])


def col_reduce_scatter(full, n, collective_id):
    width = full.shape[1] // n
    summed_t = col_exchange(full.T.reshape(n, width, full.shape[0]), n, "scatter", collective_id)
    return summed_t.T


def col_all_reduce(full, n, collective_id):
    width = full.shape[1] // n
    summed_t = col_exchange(full.T.reshape(n, width, full.shape[0]), n, "allreduce", collective_id)
    return summed_t.reshape(n * width, full.shape[0]).T


def local(tensor, first_factor, second_factor):
    frame_count, col_count, row_count = tensor.shape
    components = first_factor.shape[0]
    n = lax.axis_size("col")
    second_values = second_factor.astype(jnp.float32)
    gram_first_part = gram_of(first_factor)
    gram_second_part = gram_of(second_factor)
    block_t = col_gather_t(first_factor.T, n)
    frame_part = frame_pass(tensor, block_t, second_values.T).T
    row_summed = lax.psum(jnp.concatenate([frame_part, gram_first_part], axis=1), "row")
    summed = col_all_reduce(jnp.concatenate([row_summed, gram_second_part], axis=1), n, 3)
    frame_sum = summed[:, :frame_count]
    gram_first = summed[:, frame_count:frame_count + components]
    gram_second = summed[:, frame_count + components:]
    frames = ridge_solve(gram_first * gram_second, frame_sum)
    gram_frames = jnp.dot(frames, frames.T, precision=lax.Precision.HIGHEST)
    full_part = accumulate_pass(tensor, frames, second_values)
    first_sum_mine = col_reduce_scatter(full_part, n, 1)
    new_first_mine = ridge_solve(gram_second * gram_frames, first_sum_mine).astype(jnp.bfloat16)
    new_block_t = col_gather_t(new_first_mine.T, n)
    gram_new_part = lax.dot_general(
        new_block_t, new_block_t, (((0,), (0,)), ((), ())), preferred_element_type=jnp.float32
    )
    second_part = second_pass(tensor, new_block_t, frames.T).T
    second_sum, gram_new = lax.psum((second_part, gram_new_part), "row")
    new_second = ridge_solve(gram_new * gram_frames, second_sum)
    full_next = accumulate_pass(tensor, frames, new_second)
    mode_one = col_reduce_scatter(full_next, n, 2)
    return (frames, mode_one)


def solution(mesh):
    return jax.shard_map(
        local,
        mesh=mesh,
        in_specs=(P(None, "col", "row"), P(None, ("row", "col")), P(None, "col")),
        out_specs=(P(), P(None, ("row", "col"))),
        check_vma=False,
    )
```

```python
import functools

import jax
import jax.numpy as jnp
from jax import lax
from jax.experimental import pallas as pl
from jax.experimental.pallas import tpu as pltpu
from jax.sharding import PartitionSpec as P

ridge_weight = 0.05
MESH_ID = pl.DeviceIdType.MESH


def ridge_solve(gram, right_side):
    order_size = gram.shape[0]
    factor_low = jnp.linalg.cholesky(gram + ridge_weight * jnp.eye(order_size, dtype=jnp.float32))
    middle = lax.linalg.triangular_solve(factor_low, right_side, left_side=True, lower=True)
    return lax.linalg.triangular_solve(
        factor_low, middle, left_side=True, lower=True, transpose_a=True
    )


def gram_of(factor):
    return jnp.dot(factor, factor.T, preferred_element_type=jnp.float32)


STREAM_FRAMES = 16


def _frame_kernel(block_t_ref, second_t_ref, slab_ref, out_ref):
    frames, width, rows = slab_ref.shape
    projected = jnp.dot(
        slab_ref[...].reshape(frames * width, rows), block_t_ref[...],
        preferred_element_type=jnp.float32,
    ).reshape(frames, width, block_t_ref.shape[1])
    out_ref[...] = jnp.sum(projected * second_t_ref[...][None], axis=1)


def _second_kernel(block_t_ref, frames_t_ref, slab_ref, out_ref):
    frames, width, rows = slab_ref.shape

    @pl.when(pl.program_id(0) == 0)
    def _():
        out_ref[...] = jnp.zeros_like(out_ref)

    projected = jnp.dot(
        slab_ref[...].reshape(frames * width, rows), block_t_ref[...],
        preferred_element_type=jnp.float32,
    ).reshape(frames, width, block_t_ref.shape[1])
    out_ref[...] += jnp.sum(projected * frames_t_ref[...][:, None, :], axis=0)


def _slab_spec(width, rows):
    return pl.BlockSpec((STREAM_FRAMES, width, rows), lambda s: (s, 0, 0))


def _whole(shape):
    return pl.BlockSpec(shape, lambda s: (0,) * len(shape))


def frame_pass(tensor, block_t, second_t):
    frame_count, width, rows = tensor.shape
    components = block_t.shape[1]
    return pl.pallas_call(
        _frame_kernel,
        grid=(frame_count // STREAM_FRAMES,),
        in_specs=[_whole(block_t.shape), _whole(second_t.shape), _slab_spec(width, rows)],
        out_specs=pl.BlockSpec((STREAM_FRAMES, components), lambda s: (s, 0)),
        out_shape=jax.ShapeDtypeStruct((frame_count, components), jnp.float32),
        cost_estimate=pl.CostEstimate(
            flops=2 * components * frame_count * width * rows, transcendentals=0,
            bytes_accessed=2 * frame_count * width * rows,
        ),
    )(block_t, second_t, tensor)


def second_pass(tensor, block_t, frames_t):
    frame_count, width, rows = tensor.shape
    components = block_t.shape[1]
    return pl.pallas_call(
        _second_kernel,
        grid=(frame_count // STREAM_FRAMES,),
        in_specs=[
            _whole(block_t.shape),
            pl.BlockSpec((STREAM_FRAMES, components), lambda s: (s, 0)),
            _slab_spec(width, rows),
        ],
        out_specs=_whole((width, components)),
        out_shape=jax.ShapeDtypeStruct((width, components), jnp.float32),
        cost_estimate=pl.CostEstimate(
            flops=2 * components * frame_count * width * rows, transcendentals=0,
            bytes_accessed=2 * frame_count * width * rows,
        ),
    )(block_t, frames_t, tensor)


def _accumulate_kernel(frames_ref, tiled_ref, slab_ref, out_ref):
    frames, width, rows = slab_ref.shape
    step = pl.program_id(0)

    @pl.when(step == 0)
    def _():
        out_ref[...] = jnp.zeros_like(out_ref)

    frame_count = frames_ref.shape[1]
    span = frames * width
    which = lax.broadcasted_iota(jnp.int32, (frame_count, span), 0) - step * frames
    column = lax.broadcasted_iota(jnp.int32, (frame_count, span), 1)
    expand = ((column >= which * width) & (column < which * width + width)).astype(jnp.bfloat16)
    rest = frames_ref[...]
    repeated = jnp.zeros((frames_ref.shape[0], span), jnp.float32)
    for _ in range(3):
        piece = rest.astype(jnp.bfloat16)
        rest = rest - piece.astype(jnp.float32)
        repeated = repeated + jnp.dot(piece, expand, preferred_element_type=jnp.float32)
    weights = (repeated * tiled_ref[...]).astype(jnp.bfloat16)
    out_ref[...] += jnp.dot(
        weights, slab_ref[...].reshape(span, rows), preferred_element_type=jnp.float32
    )


def accumulate_pass(tensor, frames, second):
    frame_count, width, rows = tensor.shape
    components = frames.shape[0]
    tiled = jnp.tile(second, (1, STREAM_FRAMES))
    return pl.pallas_call(
        _accumulate_kernel,
        grid=(frame_count // STREAM_FRAMES,),
        in_specs=[_whole(frames.shape), _whole(tiled.shape), _slab_spec(width, rows)],
        out_specs=_whole((components, rows)),
        out_shape=jax.ShapeDtypeStruct((components, rows), jnp.float32),
        cost_estimate=pl.CostEstimate(
            flops=2 * components * frame_count * width * rows, transcendentals=0,
            bytes_accessed=2 * frame_count * width * rows,
        ),
    )(frames, tiled, tensor)


def _exchange_kernel(n, rows, mode, send_ref, out_ref, recv, send_sems, recv_sems, *extra):
    me = lax.axis_index("col")
    row = lax.axis_index("row")

    def exchange(count, mine, device, source, landing, sends, recvs):
        def descriptor(peer, slot):
            return pltpu.make_async_remote_copy(
                src_ref=source(peer),
                dst_ref=landing.at[slot],
                send_sem=sends.at[peer],
                recv_sem=recvs.at[slot],
                device_id=device(peer),
                device_id_type=MESH_ID,
            )

        def start(t, carry):
            peer = lax.rem(mine + 1 + t, count)
            descriptor(peer, mine).start()
            return carry

        lax.fori_loop(0, count - 1, start, 0)

        def finish(t, carry):
            peer = lax.rem(mine + 1 + t, count)
            copy = descriptor(peer, peer)
            copy.wait_send()
            copy.wait_recv()
            return carry

        lax.fori_loop(0, count - 1, finish, 0)
        landing[mine] = source(mine)[...]

    def along_col(peer):
        return (row, peer)

    def along_row(peer):
        return (peer, me)

    barrier = pltpu.get_barrier_semaphore()
    greeted = 0
    for count, mine, device in ((n, me, along_col), (rows, row, along_row)):
        if (count == n) == (mode == "rowsum") and not (mode == "allreduce" and count == rows):
            continue

        def greet(t, carry, count=count, mine=mine, device=device):
            peer = lax.rem(mine + 1 + t, count)
            pl.semaphore_signal(barrier, inc=1, device_id=device(peer), device_id_type=MESH_ID)
            return carry

        lax.fori_loop(0, count - 1, greet, 0)
        greeted += count - 1
    pl.semaphore_wait(barrier, greeted)

    if mode == "rowsum":
        exchange(rows, row, along_row, lambda peer: send_ref, recv, send_sems, recv_sems)
        out_ref[...] = jnp.sum(recv[...], axis=0)
        return
    broadcast = mode == "gather"
    exchange(
        n, me, along_col, (lambda peer: send_ref) if broadcast else (lambda peer: send_ref.at[peer]),
        recv, send_sems, recv_sems,
    )
    if mode == "gather":
        out_ref[...] = recv[...]
    elif mode == "scatter":
        out_ref[...] = jnp.sum(recv[...], axis=0)
    else:
        (chunk, row_recv, row_send_sems, row_recv_sems, total,
         recv_back, back_send_sems, back_recv_sems) = extra
        chunk[...] = jnp.sum(recv[...], axis=0)
        exchange(rows, row, along_row, lambda peer: chunk, row_recv, row_send_sems, row_recv_sems)
        total[...] = jnp.sum(row_recv[...], axis=0)
        exchange(n, me, along_col, lambda peer: total, recv_back, back_send_sems, back_recv_sems)
        out_ref[...] = recv_back[...]


def col_exchange(send, n, mode, collective_id):
    rows = lax.axis_size("row")
    piece = tuple(send.shape) if mode in ("gather", "rowsum") else tuple(send.shape[1:])
    slots = rows if mode == "rowsum" else n
    out_shape = piece if mode in ("scatter", "rowsum") else (n,) + piece
    scratch = [
        pltpu.VMEM((slots,) + piece, send.dtype),
        pltpu.SemaphoreType.DMA((slots,)),
        pltpu.SemaphoreType.DMA((slots,)),
    ]
    if mode == "allreduce":
        scratch += [
            pltpu.VMEM(piece, send.dtype),
            pltpu.VMEM((rows,) + piece, send.dtype),
            pltpu.SemaphoreType.DMA((rows,)),
            pltpu.SemaphoreType.DMA((rows,)),
            pltpu.VMEM(piece, send.dtype),
            pltpu.VMEM((n,) + piece, send.dtype),
            pltpu.SemaphoreType.DMA((n,)),
            pltpu.SemaphoreType.DMA((n,)),
        ]
    return pl.pallas_call(
        functools.partial(_exchange_kernel, n, rows, mode),
        out_shape=jax.ShapeDtypeStruct(out_shape, send.dtype),
        in_specs=[pl.BlockSpec(memory_space=pltpu.VMEM)],
        out_specs=pl.BlockSpec(memory_space=pltpu.VMEM),
        scratch_shapes=scratch,
        compiler_params=pltpu.CompilerParams(collective_id=collective_id, has_side_effects=True),
    )(send)


def col_gather_t(piece_t, n):
    gathered = col_exchange(piece_t, n, "gather", 0)
    return gathered.reshape(n * piece_t.shape[0], piece_t.shape[1])


def col_reduce_scatter(full, n, collective_id):
    width = full.shape[1] // n
    summed_t = col_exchange(full.T.reshape(n, width, full.shape[0]), n, "scatter", collective_id)
    return summed_t.T


def all_reduce(full, n, collective_id):
    width = full.shape[1] // n
    summed_t = col_exchange(full.T.reshape(n, width, full.shape[0]), n, "allreduce", collective_id)
    return summed_t.reshape(n * width, full.shape[0]).T


def row_sum(piece, n, collective_id):
    return col_exchange(piece, n, "rowsum", collective_id)


def local(tensor, first_factor, second_factor):
    frame_count, col_count, row_count = tensor.shape
    components = first_factor.shape[0]
    n = lax.axis_size("col")
    second_values = second_factor.astype(jnp.float32)
    gram_first_part = gram_of(first_factor)
    gram_second_part = gram_of(second_factor)
    block_t = col_gather_t(first_factor.T, n)
    frame_part = frame_pass(tensor, block_t, second_values.T).T
    scaled_second = gram_second_part * (1.0 / lax.axis_size("row"))
    summed = all_reduce(jnp.concatenate([frame_part, gram_first_part, scaled_second], axis=1), n, 3)
    frame_sum = summed[:, :frame_count]
    gram_first = summed[:, frame_count:frame_count + components]
    gram_second = summed[:, frame_count + components:]
    frames = ridge_solve(gram_first * gram_second, frame_sum)
    gram_frames = jnp.dot(frames, frames.T, precision=lax.Precision.HIGHEST)
    full_part = accumulate_pass(tensor, frames, second_values)
    first_sum_mine = col_reduce_scatter(full_part, n, 1)
    new_first_mine = ridge_solve(gram_second * gram_frames, first_sum_mine).astype(jnp.bfloat16)
    new_block_t = col_gather_t(new_first_mine.T, n)
    gram_new_part = lax.dot_general(
        new_block_t, new_block_t, (((0,), (0,)), ((), ())), preferred_element_type=jnp.float32
    )
    second_part_t = second_pass(tensor, new_block_t, frames.T)
    summed_new = row_sum(jnp.concatenate([second_part_t, gram_new_part], axis=0), n, 4)
    second_sum = summed_new[:col_count].T
    gram_new = summed_new[col_count:]
    new_second = ridge_solve(gram_new * gram_frames, second_sum)
    full_next = accumulate_pass(tensor, frames, new_second)
    mode_one = col_reduce_scatter(full_next, n, 2)
    return (frames, mode_one)


def solution(mesh):
    return jax.shard_map(
        local,
        mesh=mesh,
        in_specs=(P(None, "col", "row"), P(None, ("row", "col")), P(None, "col")),
        out_specs=(P(), P(None, ("row", "col"))),
        check_vma=False,
    )
```

```python
import functools

import jax
import jax.numpy as jnp
from jax import lax
from jax.experimental import pallas as pl
from jax.experimental.pallas import tpu as pltpu
from jax.sharding import PartitionSpec as P

ridge_weight = 0.05
MESH_ID = pl.DeviceIdType.MESH


def ridge_solve(gram, right_side):
    order_size = gram.shape[0]
    factor_low = jnp.linalg.cholesky(gram + ridge_weight * jnp.eye(order_size, dtype=jnp.float32))
    middle = lax.linalg.triangular_solve(factor_low, right_side, left_side=True, lower=True)
    return lax.linalg.triangular_solve(
        factor_low, middle, left_side=True, lower=True, transpose_a=True
    )


def gram_of(factor):
    return jnp.dot(factor, factor.T, preferred_element_type=jnp.float32)


STREAM_FRAMES = 16


def _frame_kernel(block_t_ref, second_t_ref, slab_ref, out_ref):
    frames, width, rows = slab_ref.shape
    projected = jnp.dot(
        slab_ref[...].reshape(frames * width, rows), block_t_ref[...],
        preferred_element_type=jnp.float32,
    ).reshape(frames, width, block_t_ref.shape[1])
    out_ref[...] = jnp.sum(projected * second_t_ref[...][None], axis=1)


def _second_kernel(block_t_ref, frames_t_ref, slab_ref, out_ref):
    frames, width, rows = slab_ref.shape

    @pl.when(pl.program_id(0) == 0)
    def _():
        out_ref[...] = jnp.zeros_like(out_ref)

    projected = jnp.dot(
        slab_ref[...].reshape(frames * width, rows), block_t_ref[...],
        preferred_element_type=jnp.float32,
    ).reshape(frames, width, block_t_ref.shape[1])
    out_ref[...] += jnp.sum(projected * frames_t_ref[...][:, None, :], axis=0)


def _slab_spec(width, rows):
    return pl.BlockSpec((STREAM_FRAMES, width, rows), lambda s: (s, 0, 0))


def _whole(shape):
    return pl.BlockSpec(shape, lambda s: (0,) * len(shape))


def frame_pass(tensor, block_t, second_t):
    frame_count, width, rows = tensor.shape
    components = block_t.shape[1]
    return pl.pallas_call(
        _frame_kernel,
        grid=(frame_count // STREAM_FRAMES,),
        in_specs=[_whole(block_t.shape), _whole(second_t.shape), _slab_spec(width, rows)],
        out_specs=pl.BlockSpec((STREAM_FRAMES, components), lambda s: (s, 0)),
        out_shape=jax.ShapeDtypeStruct((frame_count, components), jnp.float32),
        cost_estimate=pl.CostEstimate(
            flops=2 * components * frame_count * width * rows, transcendentals=0,
            bytes_accessed=2 * frame_count * width * rows,
        ),
    )(block_t, second_t, tensor)


def second_pass(tensor, block_t, frames_t):
    frame_count, width, rows = tensor.shape
    components = block_t.shape[1]
    return pl.pallas_call(
        _second_kernel,
        grid=(frame_count // STREAM_FRAMES,),
        in_specs=[
            _whole(block_t.shape),
            pl.BlockSpec((STREAM_FRAMES, components), lambda s: (s, 0)),
            _slab_spec(width, rows),
        ],
        out_specs=_whole((width, components)),
        out_shape=jax.ShapeDtypeStruct((width, components), jnp.float32),
        cost_estimate=pl.CostEstimate(
            flops=2 * components * frame_count * width * rows, transcendentals=0,
            bytes_accessed=2 * frame_count * width * rows,
        ),
    )(block_t, frames_t, tensor)


def _accumulate_kernel(frames_ref, tiled_ref, slab_ref, out_ref):
    frames, width, rows = slab_ref.shape
    step = pl.program_id(0)

    @pl.when(step == 0)
    def _():
        out_ref[...] = jnp.zeros_like(out_ref)

    frame_count = frames_ref.shape[1]
    span = frames * width
    which = lax.broadcasted_iota(jnp.int32, (frame_count, span), 0) - step * frames
    column = lax.broadcasted_iota(jnp.int32, (frame_count, span), 1)
    expand = ((column >= which * width) & (column < which * width + width)).astype(jnp.bfloat16)
    rest = frames_ref[...]
    repeated = jnp.zeros((frames_ref.shape[0], span), jnp.float32)
    for _ in range(3):
        piece = rest.astype(jnp.bfloat16)
        rest = rest - piece.astype(jnp.float32)
        repeated = repeated + jnp.dot(piece, expand, preferred_element_type=jnp.float32)
    weights = (repeated * tiled_ref[...]).astype(jnp.bfloat16)
    out_ref[...] += jnp.dot(
        weights, slab_ref[...].reshape(span, rows), preferred_element_type=jnp.float32
    )


def accumulate_pass(tensor, frames, second):
    frame_count, width, rows = tensor.shape
    components = frames.shape[0]
    tiled = jnp.tile(second, (1, STREAM_FRAMES))
    return pl.pallas_call(
        _accumulate_kernel,
        grid=(frame_count // STREAM_FRAMES,),
        in_specs=[_whole(frames.shape), _whole(tiled.shape), _slab_spec(width, rows)],
        out_specs=_whole((components, rows)),
        out_shape=jax.ShapeDtypeStruct((components, rows), jnp.float32),
        cost_estimate=pl.CostEstimate(
            flops=2 * components * frame_count * width * rows, transcendentals=0,
            bytes_accessed=2 * frame_count * width * rows,
        ),
    )(frames, tiled, tensor)


def _split(n):
    inner = next(d for d in (8, 4, 2, 1) if n % d == 0 and d * d <= n)
    return inner, n // inner


def _exchange_kernel(n, rows, mode, send_ref, out_ref, *scratch):
    me = lax.axis_index("col")
    row = lax.axis_index("row")
    inner, outer = _split(n)
    low = lax.rem(me, inner)
    high = me // inner

    def in_low(peer):
        return (row, high * inner + peer)

    def in_high(peer):
        return (row, peer * inner + low)

    def in_row(peer):
        return (peer, me)

    def exchange(count, mine, device, source, landing, sends, recvs):
        def descriptor(peer, slot):
            return pltpu.make_async_remote_copy(
                src_ref=source(peer),
                dst_ref=landing.at[slot],
                send_sem=sends.at[peer],
                recv_sem=recvs.at[slot],
                device_id=device(peer),
                device_id_type=MESH_ID,
            )

        def start(t, carry):
            peer = lax.rem(mine + 1 + t, count)
            descriptor(peer, mine).start()
            return carry

        lax.fori_loop(0, count - 1, start, 0)

        def finish(t, carry):
            peer = lax.rem(mine + 1 + t, count)
            copy = descriptor(peer, peer)
            copy.wait_send()
            copy.wait_recv()
            return carry

        lax.fori_loop(0, count - 1, finish, 0)
        landing[mine] = source(mine)[...]

    if mode == "rowsum":
        groups = [(rows, row, in_row)]
    else:
        groups = [(inner, low, in_low), (outer, high, in_high)]
        if mode == "allreduce":
            groups.append((rows, row, in_row))
    barrier = pltpu.get_barrier_semaphore()
    for count, mine, device in groups:
        def greet(t, carry, count=count, mine=mine, device=device):
            peer = lax.rem(mine + 1 + t, count)
            pl.semaphore_signal(barrier, inc=1, device_id=device(peer), device_id_type=MESH_ID)
            return carry

        lax.fori_loop(0, count - 1, greet, 0)
    pl.semaphore_wait(barrier, sum(count - 1 for count, _, _ in groups))

    scratch = list(scratch)

    def take(k):
        taken = scratch[:k]
        del scratch[:k]
        return taken

    def gather(piece_ref):
        bundle, s1, r1 = take(3)
        exchange(outer, high, in_high, lambda peer: piece_ref, bundle, s1, r1)
        everything, s2, r2 = take(3)
        exchange(inner, low, in_low, lambda peer: bundle, everything, s2, r2)
        out_ref[...] = everything[...]

    if mode == "rowsum":
        landing, s1, r1 = take(3)
        exchange(rows, row, in_row, lambda peer: send_ref, landing, s1, r1)
        out_ref[...] = jnp.sum(landing[...], axis=0)
        return
    if mode == "gather":
        gather(send_ref)
        return
    landing, s1, r1, partial = take(4)
    exchange(inner, low, in_low, lambda peer: send_ref.at[peer], landing, s1, r1)
    partial[...] = jnp.sum(landing[...], axis=0)
    landing2, s2, r2 = take(3)
    exchange(outer, high, in_high, lambda peer: partial.at[peer], landing2, s2, r2)
    if mode == "scatter":
        out_ref[...] = jnp.sum(landing2[...], axis=0)
        return
    chunk, row_landing, s3, r3, total = take(5)
    chunk[...] = jnp.sum(landing2[...], axis=0)
    exchange(rows, row, in_row, lambda peer: chunk, row_landing, s3, r3)
    total[...] = jnp.sum(row_landing[...], axis=0)
    gather(total)


def col_exchange(send, n, mode, collective_id):
    rows = lax.axis_size("row")
    inner, outer = _split(n)
    dtype = send.dtype

    def stage(count, piece):
        return [
            pltpu.VMEM((count,) + piece, dtype),
            pltpu.SemaphoreType.DMA((count,)),
            pltpu.SemaphoreType.DMA((count,)),
        ]

    if mode == "rowsum":
        piece = tuple(send.shape)
        out_shape = piece
        scratch = stage(rows, piece)
    elif mode == "gather":
        piece = tuple(send.shape)
        out_shape = (inner, outer) + piece
        scratch = stage(outer, piece) + stage(inner, (outer,) + piece)
    else:
        piece = tuple(send.shape[2:])
        out_shape = piece if mode == "scatter" else (inner, outer) + piece
        scratch = stage(inner, (outer,) + piece) + [pltpu.VMEM((outer,) + piece, dtype)]
        scratch += stage(outer, piece)
        if mode == "allreduce":
            scratch += [pltpu.VMEM(piece, dtype)] + stage(rows, piece) + [pltpu.VMEM(piece, dtype)]
            scratch += stage(outer, piece) + stage(inner, (outer,) + piece)
    return pl.pallas_call(
        functools.partial(_exchange_kernel, n, rows, mode),
        out_shape=jax.ShapeDtypeStruct(out_shape, dtype),
        in_specs=[pl.BlockSpec(memory_space=pltpu.VMEM)],
        out_specs=pl.BlockSpec(memory_space=pltpu.VMEM),
        scratch_shapes=scratch,
        compiler_params=pltpu.CompilerParams(collective_id=collective_id, has_side_effects=True),
    )(send)


def _chunk_order(chunks, n):
    inner, outer = _split(n)
    return chunks.reshape((outer, inner) + chunks.shape[1:]).swapaxes(0, 1)


def _col_order(gathered, n):
    return gathered.swapaxes(0, 1).reshape((n,) + gathered.shape[2:])


def col_gather_t(piece_t, n):
    gathered = _col_order(col_exchange(piece_t, n, "gather", 0), n)
    return gathered.reshape(n * piece_t.shape[0], piece_t.shape[1])


def col_reduce_scatter(full, n, collective_id):
    width = full.shape[1] // n
    chunks = _chunk_order(full.T.reshape(n, width, full.shape[0]), n)
    return col_exchange(chunks, n, "scatter", collective_id).T


def all_reduce(full, n, collective_id):
    width = full.shape[1] // n
    chunks = _chunk_order(full.T.reshape(n, width, full.shape[0]), n)
    summed_t = _col_order(col_exchange(chunks, n, "allreduce", collective_id), n)
    return summed_t.reshape(n * width, full.shape[0]).T


def row_sum(piece, n, collective_id):
    return col_exchange(piece, n, "rowsum", collective_id)


def local(tensor, first_factor, second_factor):
    frame_count, col_count, row_count = tensor.shape
    components = first_factor.shape[0]
    n = lax.axis_size("col")
    second_values = second_factor.astype(jnp.float32)
    gram_first_part = gram_of(first_factor)
    gram_second_part = gram_of(second_factor)
    block_t = col_gather_t(first_factor.T, n)
    frame_part = frame_pass(tensor, block_t, second_values.T).T
    scaled_second = gram_second_part * (1.0 / lax.axis_size("row"))
    summed = all_reduce(jnp.concatenate([frame_part, gram_first_part, scaled_second], axis=1), n, 3)
    frame_sum = summed[:, :frame_count]
    gram_first = summed[:, frame_count:frame_count + components]
    gram_second = summed[:, frame_count + components:]
    frames = ridge_solve(gram_first * gram_second, frame_sum)
    gram_frames = jnp.dot(frames, frames.T, precision=lax.Precision.HIGHEST)
    full_part = accumulate_pass(tensor, frames, second_values)
    first_sum_mine = col_reduce_scatter(full_part, n, 1)
    new_first_mine = ridge_solve(gram_second * gram_frames, first_sum_mine).astype(jnp.bfloat16)
    new_block_t = col_gather_t(new_first_mine.T, n)
    gram_new_part = lax.dot_general(
        new_block_t, new_block_t, (((0,), (0,)), ((), ())), preferred_element_type=jnp.float32
    )
    second_part_t = second_pass(tensor, new_block_t, frames.T)
    summed_new = row_sum(jnp.concatenate([second_part_t, gram_new_part], axis=0), n, 4)
    second_sum = summed_new[:col_count].T
    gram_new = summed_new[col_count:]
    new_second = ridge_solve(gram_new * gram_frames, second_sum)
    full_next = accumulate_pass(tensor, frames, new_second)
    mode_one = col_reduce_scatter(full_next, n, 2)
    return (frames, mode_one)


def solution(mesh):
    return jax.shard_map(
        local,
        mesh=mesh,
        in_specs=(P(None, "col", "row"), P(None, ("row", "col")), P(None, "col")),
        out_specs=(P(), P(None, ("row", "col"))),
        check_vma=False,
    )
```

```python
import functools

import jax
import jax.numpy as jnp
from jax import lax
from jax.experimental import pallas as pl
from jax.experimental.pallas import tpu as pltpu
from jax.sharding import PartitionSpec as P

ridge_weight = 0.05
MESH_ID = pl.DeviceIdType.MESH


def ridge_solve(gram, right_side):
    order_size = gram.shape[0]
    factor_low = jnp.linalg.cholesky(gram + ridge_weight * jnp.eye(order_size, dtype=jnp.float32))
    middle = lax.linalg.triangular_solve(factor_low, right_side, left_side=True, lower=True)
    return lax.linalg.triangular_solve(
        factor_low, middle, left_side=True, lower=True, transpose_a=True
    )


def gram_of(factor):
    return jnp.dot(factor, factor.T, preferred_element_type=jnp.float32)


STREAM_FRAMES = 16


def _frame_kernel(block_t_ref, second_t_ref, slab_ref, out_ref):
    frames, width, rows = slab_ref.shape
    projected = jnp.dot(
        slab_ref[...].reshape(frames * width, rows), block_t_ref[...],
        preferred_element_type=jnp.float32,
    ).reshape(frames, width, block_t_ref.shape[1])
    out_ref[...] = jnp.sum(projected * second_t_ref[...][None], axis=1)


def _second_kernel(block_t_ref, frames_t_ref, slab_ref, out_ref):
    frames, width, rows = slab_ref.shape

    @pl.when(pl.program_id(0) == 0)
    def _():
        out_ref[...] = jnp.zeros_like(out_ref)

    projected = jnp.dot(
        slab_ref[...].reshape(frames * width, rows), block_t_ref[...],
        preferred_element_type=jnp.float32,
    ).reshape(frames, width, block_t_ref.shape[1])
    out_ref[...] += jnp.sum(projected * frames_t_ref[...][:, None, :], axis=0)


def _slab_spec(width, rows):
    return pl.BlockSpec((STREAM_FRAMES, width, rows), lambda s: (s, 0, 0))


def _whole(shape):
    return pl.BlockSpec(shape, lambda s: (0,) * len(shape))


def frame_pass(tensor, block_t, second_t):
    frame_count, width, rows = tensor.shape
    components = block_t.shape[1]
    return pl.pallas_call(
        _frame_kernel,
        grid=(frame_count // STREAM_FRAMES,),
        in_specs=[_whole(block_t.shape), _whole(second_t.shape), _slab_spec(width, rows)],
        out_specs=pl.BlockSpec((STREAM_FRAMES, components), lambda s: (s, 0)),
        out_shape=jax.ShapeDtypeStruct((frame_count, components), jnp.float32),
        cost_estimate=pl.CostEstimate(
            flops=2 * components * frame_count * width * rows, transcendentals=0,
            bytes_accessed=2 * frame_count * width * rows,
        ),
    )(block_t, second_t, tensor)


def second_pass(tensor, block_t, frames_t):
    frame_count, width, rows = tensor.shape
    components = block_t.shape[1]
    return pl.pallas_call(
        _second_kernel,
        grid=(frame_count // STREAM_FRAMES,),
        in_specs=[
            _whole(block_t.shape),
            pl.BlockSpec((STREAM_FRAMES, components), lambda s: (s, 0)),
            _slab_spec(width, rows),
        ],
        out_specs=_whole((width, components)),
        out_shape=jax.ShapeDtypeStruct((width, components), jnp.float32),
        cost_estimate=pl.CostEstimate(
            flops=2 * components * frame_count * width * rows, transcendentals=0,
            bytes_accessed=2 * frame_count * width * rows,
        ),
    )(block_t, frames_t, tensor)


def _accumulate_kernel(frames_ref, tiled_ref, slab_ref, out_ref):
    frames, width, rows = slab_ref.shape
    step = pl.program_id(0)

    @pl.when(step == 0)
    def _():
        out_ref[...] = jnp.zeros_like(out_ref)

    frame_count = frames_ref.shape[1]
    span = frames * width
    which = lax.broadcasted_iota(jnp.int32, (frame_count, span), 0) - step * frames
    column = lax.broadcasted_iota(jnp.int32, (frame_count, span), 1)
    expand = ((column >= which * width) & (column < which * width + width)).astype(jnp.bfloat16)
    rest = frames_ref[...]
    repeated = jnp.zeros((frames_ref.shape[0], span), jnp.float32)
    for _ in range(3):
        piece = rest.astype(jnp.bfloat16)
        rest = rest - piece.astype(jnp.float32)
        repeated = repeated + jnp.dot(piece, expand, preferred_element_type=jnp.float32)
    weights = (repeated * tiled_ref[...]).astype(jnp.bfloat16)
    out_ref[...] += jnp.dot(
        weights, slab_ref[...].reshape(span, rows), preferred_element_type=jnp.float32
    )


def accumulate_pass(tensor, frames, second):
    frame_count, width, rows = tensor.shape
    components = frames.shape[0]
    tiled = jnp.tile(second, (1, STREAM_FRAMES))
    return pl.pallas_call(
        _accumulate_kernel,
        grid=(frame_count // STREAM_FRAMES,),
        in_specs=[_whole(frames.shape), _whole(tiled.shape), _slab_spec(width, rows)],
        out_specs=_whole((components, rows)),
        out_shape=jax.ShapeDtypeStruct((components, rows), jnp.float32),
        cost_estimate=pl.CostEstimate(
            flops=2 * components * frame_count * width * rows, transcendentals=0,
            bytes_accessed=2 * frame_count * width * rows,
        ),
    )(frames, tiled, tensor)


def _split(n):
    inner = next(d for d in (8, 4, 2, 1) if n % d == 0 and d * d <= n)
    return inner, n // inner


def _exchange_kernel(n, rows, mode, send_ref, out_ref, *scratch):
    me = lax.axis_index("col")
    row = lax.axis_index("row")
    inner, outer = _split(n)
    low = lax.rem(me, inner)
    high = me // inner

    def in_low(peer):
        return (row, high * inner + peer)

    def in_high(peer):
        return (row, peer * inner + low)

    def in_row(peer):
        return (peer, me)

    def exchange(count, mine, device, source, landing, sends, recvs):
        def descriptor(peer, slot):
            return pltpu.make_async_remote_copy(
                src_ref=source(peer),
                dst_ref=landing.at[slot],
                send_sem=sends.at[peer],
                recv_sem=recvs.at[slot],
                device_id=device(peer),
                device_id_type=MESH_ID,
            )

        def start(t, carry):
            peer = lax.rem(mine + 1 + t, count)
            descriptor(peer, mine).start()
            return carry

        lax.fori_loop(0, count - 1, start, 0)

        def finish(t, carry):
            peer = lax.rem(mine + 1 + t, count)
            copy = descriptor(peer, peer)
            copy.wait_send()
            copy.wait_recv()
            return carry

        lax.fori_loop(0, count - 1, finish, 0)
        landing[mine] = source(mine)[...]

    if mode == "rowsum":
        groups = [(rows, row, in_row)]
    else:
        groups = [(inner, low, in_low), (outer, high, in_high)]
        if mode == "allreduce":
            groups.append((rows, row, in_row))
    barrier = pltpu.get_barrier_semaphore()
    for count, mine, device in groups:
        def greet(t, carry, count=count, mine=mine, device=device):
            peer = lax.rem(mine + 1 + t, count)
            pl.semaphore_signal(barrier, inc=1, device_id=device(peer), device_id_type=MESH_ID)
            return carry

        lax.fori_loop(0, count - 1, greet, 0)
    pl.semaphore_wait(barrier, sum(count - 1 for count, _, _ in groups))

    scratch = list(scratch)

    def take(k):
        taken = scratch[:k]
        del scratch[:k]
        return taken

    def gather(piece_ref):
        bundle, s1, r1 = take(3)
        exchange(inner, low, in_low, lambda peer: piece_ref, bundle, s1, r1)
        everything, s2, r2 = take(3)
        exchange(outer, high, in_high, lambda peer: bundle, everything, s2, r2)
        out_ref[...] = everything[...]

    if mode == "rowsum":
        landing, s1, r1 = take(3)
        exchange(rows, row, in_row, lambda peer: send_ref, landing, s1, r1)
        out_ref[...] = jnp.sum(landing[...], axis=0)
        return
    if mode == "gather":
        gather(send_ref)
        return
    landing, s1, r1, partial = take(4)
    exchange(outer, high, in_high, lambda peer: send_ref.at[peer], landing, s1, r1)
    partial[...] = jnp.sum(landing[...], axis=0)
    landing2, s2, r2 = take(3)
    exchange(inner, low, in_low, lambda peer: partial.at[peer], landing2, s2, r2)
    if mode == "scatter":
        out_ref[...] = jnp.sum(landing2[...], axis=0)
        return
    chunk, row_landing, s3, r3, total = take(5)
    chunk[...] = jnp.sum(landing2[...], axis=0)
    exchange(rows, row, in_row, lambda peer: chunk, row_landing, s3, r3)
    total[...] = jnp.sum(row_landing[...], axis=0)
    gather(total)


def col_exchange(send, n, mode, collective_id):
    rows = lax.axis_size("row")
    inner, outer = _split(n)
    dtype = send.dtype

    def stage(count, piece):
        return [
            pltpu.VMEM((count,) + piece, dtype),
            pltpu.SemaphoreType.DMA((count,)),
            pltpu.SemaphoreType.DMA((count,)),
        ]

    if mode == "rowsum":
        piece = tuple(send.shape)
        out_shape = piece
        scratch = stage(rows, piece)
    elif mode == "gather":
        piece = tuple(send.shape)
        out_shape = (outer, inner) + piece
        scratch = stage(inner, piece) + stage(outer, (inner,) + piece)
    else:
        piece = tuple(send.shape[2:])
        out_shape = piece if mode == "scatter" else (outer, inner) + piece
        scratch = stage(outer, (inner,) + piece) + [pltpu.VMEM((inner,) + piece, dtype)]
        scratch += stage(inner, piece)
        if mode == "allreduce":
            scratch += [pltpu.VMEM(piece, dtype)] + stage(rows, piece) + [pltpu.VMEM(piece, dtype)]
            scratch += stage(inner, piece) + stage(outer, (inner,) + piece)
    return pl.pallas_call(
        functools.partial(_exchange_kernel, n, rows, mode),
        out_shape=jax.ShapeDtypeStruct(out_shape, dtype),
        in_specs=[pl.BlockSpec(memory_space=pltpu.VMEM)],
        out_specs=pl.BlockSpec(memory_space=pltpu.VMEM),
        scratch_shapes=scratch,
        compiler_params=pltpu.CompilerParams(collective_id=collective_id, has_side_effects=True),
    )(send)


def _chunk_order(chunks, n):
    inner, outer = _split(n)
    return chunks.reshape((outer, inner) + chunks.shape[1:])


def _col_order(gathered, n):
    return gathered.reshape((n,) + gathered.shape[2:])


def col_gather_t(piece_t, n):
    gathered = _col_order(col_exchange(piece_t, n, "gather", 0), n)
    return gathered.reshape(n * piece_t.shape[0], piece_t.shape[1])


def col_reduce_scatter(full, n, collective_id):
    width = full.shape[1] // n
    chunks = _chunk_order(full.T.reshape(n, width, full.shape[0]), n)
    return col_exchange(chunks, n, "scatter", collective_id).T


def all_reduce(full, n, collective_id):
    width = full.shape[1] // n
    chunks = _chunk_order(full.T.reshape(n, width, full.shape[0]), n)
    summed_t = _col_order(col_exchange(chunks, n, "allreduce", collective_id), n)
    return summed_t.reshape(n * width, full.shape[0]).T


def row_sum(piece, n, collective_id):
    return col_exchange(piece, n, "rowsum", collective_id)


def local(tensor, first_factor, second_factor):
    frame_count, col_count, row_count = tensor.shape
    components = first_factor.shape[0]
    n = lax.axis_size("col")
    second_values = second_factor.astype(jnp.float32)
    gram_first_part = gram_of(first_factor)
    gram_second_part = gram_of(second_factor)
    block_t = col_gather_t(first_factor.T, n)
    frame_part = frame_pass(tensor, block_t, second_values.T).T
    scaled_second = gram_second_part * (1.0 / lax.axis_size("row"))
    summed = all_reduce(jnp.concatenate([frame_part, gram_first_part, scaled_second], axis=1), n, 3)
    frame_sum = summed[:, :frame_count]
    gram_first = summed[:, frame_count:frame_count + components]
    gram_second = summed[:, frame_count + components:]
    frames = ridge_solve(gram_first * gram_second, frame_sum)
    gram_frames = jnp.dot(frames, frames.T, precision=lax.Precision.HIGHEST)
    full_part = accumulate_pass(tensor, frames, second_values)
    first_sum_mine = col_reduce_scatter(full_part, n, 1)
    new_first_mine = ridge_solve(gram_second * gram_frames, first_sum_mine).astype(jnp.bfloat16)
    new_block_t = col_gather_t(new_first_mine.T, n)
    gram_new_part = lax.dot_general(
        new_block_t, new_block_t, (((0,), (0,)), ((), ())), preferred_element_type=jnp.float32
    )
    second_part_t = second_pass(tensor, new_block_t, frames.T)
    summed_new = row_sum(jnp.concatenate([second_part_t, gram_new_part], axis=0), n, 4)
    second_sum = summed_new[:col_count].T
    gram_new = summed_new[col_count:]
    new_second = ridge_solve(gram_new * gram_frames, second_sum)
    full_next = accumulate_pass(tensor, frames, new_second)
    mode_one = col_reduce_scatter(full_next, n, 2)
    return (frames, mode_one)


def solution(mesh):
    return jax.shard_map(
        local,
        mesh=mesh,
        in_specs=(P(None, "col", "row"), P(None, ("row", "col")), P(None, "col")),
        out_specs=(P(), P(None, ("row", "col"))),
        check_vma=False,
    )
```

```python
import functools

import jax
import jax.numpy as jnp
from jax import lax
from jax.experimental import pallas as pl
from jax.experimental.pallas import tpu as pltpu
from jax.sharding import PartitionSpec as P

ridge_weight = 0.05
MESH_ID = pl.DeviceIdType.MESH


def ridge_solve(gram, right_side):
    order_size = gram.shape[0]
    factor_low = jnp.linalg.cholesky(gram + ridge_weight * jnp.eye(order_size, dtype=jnp.float32))
    middle = lax.linalg.triangular_solve(factor_low, right_side, left_side=True, lower=True)
    return lax.linalg.triangular_solve(
        factor_low, middle, left_side=True, lower=True, transpose_a=True
    )


def gram_of(factor):
    return jnp.dot(factor, factor.T, preferred_element_type=jnp.float32)


STREAM_FRAMES = 32


def _frame_kernel(block_t_ref, second_t_ref, slab_ref, out_ref):
    frames, width, rows = slab_ref.shape
    projected = jnp.dot(
        slab_ref[...].reshape(frames * width, rows), block_t_ref[...],
        preferred_element_type=jnp.float32,
    ).reshape(frames, width, block_t_ref.shape[1])
    out_ref[...] = jnp.sum(projected * second_t_ref[...][None], axis=1)


def _second_kernel(block_t_ref, frames_t_ref, slab_ref, out_ref):
    frames, width, rows = slab_ref.shape

    @pl.when(pl.program_id(0) == 0)
    def _():
        out_ref[...] = jnp.zeros_like(out_ref)

    projected = jnp.dot(
        slab_ref[...].reshape(frames * width, rows), block_t_ref[...],
        preferred_element_type=jnp.float32,
    ).reshape(frames, width, block_t_ref.shape[1])
    out_ref[...] += jnp.sum(projected * frames_t_ref[...][:, None, :], axis=0)


def _slab_spec(width, rows):
    return pl.BlockSpec((STREAM_FRAMES, width, rows), lambda s: (s, 0, 0))


def _whole(shape):
    return pl.BlockSpec(shape, lambda s: (0,) * len(shape))


def frame_pass(tensor, block_t, second_t):
    frame_count, width, rows = tensor.shape
    components = block_t.shape[1]
    return pl.pallas_call(
        _frame_kernel,
        grid=(frame_count // STREAM_FRAMES,),
        in_specs=[_whole(block_t.shape), _whole(second_t.shape), _slab_spec(width, rows)],
        out_specs=pl.BlockSpec((STREAM_FRAMES, components), lambda s: (s, 0)),
        out_shape=jax.ShapeDtypeStruct((frame_count, components), jnp.float32),
        cost_estimate=pl.CostEstimate(
            flops=2 * components * frame_count * width * rows, transcendentals=0,
            bytes_accessed=2 * frame_count * width * rows,
        ),
    )(block_t, second_t, tensor)


def second_pass(tensor, block_t, frames_t):
    frame_count, width, rows = tensor.shape
    components = block_t.shape[1]
    return pl.pallas_call(
        _second_kernel,
        grid=(frame_count // STREAM_FRAMES,),
        in_specs=[
            _whole(block_t.shape),
            pl.BlockSpec((STREAM_FRAMES, components), lambda s: (s, 0)),
            _slab_spec(width, rows),
        ],
        out_specs=_whole((width, components)),
        out_shape=jax.ShapeDtypeStruct((width, components), jnp.float32),
        cost_estimate=pl.CostEstimate(
            flops=2 * components * frame_count * width * rows, transcendentals=0,
            bytes_accessed=2 * frame_count * width * rows,
        ),
    )(block_t, frames_t, tensor)


def _accumulate_kernel(frames_ref, tiled_ref, slab_ref, out_ref):
    frames, width, rows = slab_ref.shape
    step = pl.program_id(0)

    @pl.when(step == 0)
    def _():
        out_ref[...] = jnp.zeros_like(out_ref)

    frame_count = frames_ref.shape[1]
    span = frames * width
    which = lax.broadcasted_iota(jnp.int32, (frame_count, span), 0) - step * frames
    column = lax.broadcasted_iota(jnp.int32, (frame_count, span), 1)
    expand = ((column >= which * width) & (column < which * width + width)).astype(jnp.bfloat16)
    rest = frames_ref[...]
    repeated = jnp.zeros((frames_ref.shape[0], span), jnp.float32)
    for _ in range(3):
        piece = rest.astype(jnp.bfloat16)
        rest = rest - piece.astype(jnp.float32)
        repeated = repeated + jnp.dot(piece, expand, preferred_element_type=jnp.float32)
    weights = (repeated * tiled_ref[...]).astype(jnp.bfloat16)
    out_ref[...] += jnp.dot(
        weights, slab_ref[...].reshape(span, rows), preferred_element_type=jnp.float32
    )


def accumulate_pass(tensor, frames, second):
    frame_count, width, rows = tensor.shape
    components = frames.shape[0]
    tiled = jnp.tile(second, (1, STREAM_FRAMES))
    return pl.pallas_call(
        _accumulate_kernel,
        grid=(frame_count // STREAM_FRAMES,),
        in_specs=[_whole(frames.shape), _whole(tiled.shape), _slab_spec(width, rows)],
        out_specs=_whole((components, rows)),
        out_shape=jax.ShapeDtypeStruct((components, rows), jnp.float32),
        cost_estimate=pl.CostEstimate(
            flops=2 * components * frame_count * width * rows, transcendentals=0,
            bytes_accessed=2 * frame_count * width * rows,
        ),
    )(frames, tiled, tensor)


def _split(n):
    inner = next(d for d in (8, 4, 2, 1) if n % d == 0 and d * d <= n)
    return inner, n // inner


def _exchange_kernel(n, rows, mode, send_ref, out_ref, *scratch):
    me = lax.axis_index("col")
    row = lax.axis_index("row")
    inner, outer = _split(n)
    low = lax.rem(me, inner)
    high = me // inner

    def in_low(peer):
        return (row, high * inner + peer)

    def in_high(peer):
        return (row, peer * inner + low)

    def in_row(peer):
        return (peer, me)

    def exchange(count, mine, device, source, landing, sends, recvs):
        def descriptor(peer, slot):
            return pltpu.make_async_remote_copy(
                src_ref=source(peer),
                dst_ref=landing.at[slot],
                send_sem=sends.at[peer],
                recv_sem=recvs.at[slot],
                device_id=device(peer),
                device_id_type=MESH_ID,
            )

        def start(t, carry):
            peer = lax.rem(mine + 1 + t, count)
            descriptor(peer, mine).start()
            return carry

        lax.fori_loop(0, count - 1, start, 0)

        def finish(t, carry):
            peer = lax.rem(mine + 1 + t, count)
            copy = descriptor(peer, peer)
            copy.wait_send()
            copy.wait_recv()
            return carry

        lax.fori_loop(0, count - 1, finish, 0)
        landing[mine] = source(mine)[...]

    if mode == "rowsum":
        groups = [(rows, row, in_row)]
    else:
        groups = [(inner, low, in_low), (outer, high, in_high)]
        if mode == "allreduce":
            groups.append((rows, row, in_row))
    barrier = pltpu.get_barrier_semaphore()
    for count, mine, device in groups:
        def greet(t, carry, count=count, mine=mine, device=device):
            peer = lax.rem(mine + 1 + t, count)
            pl.semaphore_signal(barrier, inc=1, device_id=device(peer), device_id_type=MESH_ID)
            return carry

        lax.fori_loop(0, count - 1, greet, 0)
    pl.semaphore_wait(barrier, sum(count - 1 for count, _, _ in groups))

    scratch = list(scratch)

    def take(k):
        taken = scratch[:k]
        del scratch[:k]
        return taken

    def gather(piece_ref):
        bundle, s1, r1 = take(3)
        exchange(inner, low, in_low, lambda peer: piece_ref, bundle, s1, r1)
        everything, s2, r2 = take(3)
        exchange(outer, high, in_high, lambda peer: bundle, everything, s2, r2)
        out_ref[...] = everything[...]

    if mode == "rowsum":
        landing, s1, r1 = take(3)
        exchange(rows, row, in_row, lambda peer: send_ref, landing, s1, r1)
        out_ref[...] = jnp.sum(landing[...], axis=0)
        return
    if mode == "gather":
        gather(send_ref)
        return
    landing, s1, r1, partial = take(4)
    exchange(outer, high, in_high, lambda peer: send_ref.at[peer], landing, s1, r1)
    partial[...] = jnp.sum(landing[...], axis=0)
    landing2, s2, r2 = take(3)
    exchange(inner, low, in_low, lambda peer: partial.at[peer], landing2, s2, r2)
    if mode == "scatter":
        out_ref[...] = jnp.sum(landing2[...], axis=0)
        return
    chunk, row_landing, s3, r3, total = take(5)
    chunk[...] = jnp.sum(landing2[...], axis=0)
    exchange(rows, row, in_row, lambda peer: chunk, row_landing, s3, r3)
    total[...] = jnp.sum(row_landing[...], axis=0)
    gather(total)


def col_exchange(send, n, mode, collective_id):
    rows = lax.axis_size("row")
    inner, outer = _split(n)
    dtype = send.dtype

    def stage(count, piece):
        return [
            pltpu.VMEM((count,) + piece, dtype),
            pltpu.SemaphoreType.DMA((count,)),
            pltpu.SemaphoreType.DMA((count,)),
        ]

    if mode == "rowsum":
        piece = tuple(send.shape)
        out_shape = piece
        scratch = stage(rows, piece)
    elif mode == "gather":
        piece = tuple(send.shape)
        out_shape = (outer, inner) + piece
        scratch = stage(inner, piece) + stage(outer, (inner,) + piece)
    else:
        piece = tuple(send.shape[2:])
        out_shape = piece if mode == "scatter" else (outer, inner) + piece
        scratch = stage(outer, (inner,) + piece) + [pltpu.VMEM((inner,) + piece, dtype)]
        scratch += stage(inner, piece)
        if mode == "allreduce":
            scratch += [pltpu.VMEM(piece, dtype)] + stage(rows, piece) + [pltpu.VMEM(piece, dtype)]
            scratch += stage(inner, piece) + stage(outer, (inner,) + piece)
    return pl.pallas_call(
        functools.partial(_exchange_kernel, n, rows, mode),
        out_shape=jax.ShapeDtypeStruct(out_shape, dtype),
        in_specs=[pl.BlockSpec(memory_space=pltpu.VMEM)],
        out_specs=pl.BlockSpec(memory_space=pltpu.VMEM),
        scratch_shapes=scratch,
        compiler_params=pltpu.CompilerParams(collective_id=collective_id, has_side_effects=True),
    )(send)


def _chunk_order(chunks, n):
    inner, outer = _split(n)
    return chunks.reshape((outer, inner) + chunks.shape[1:])


def _col_order(gathered, n):
    return gathered.reshape((n,) + gathered.shape[2:])


def col_gather_t(piece_t, n):
    gathered = _col_order(col_exchange(piece_t, n, "gather", 0), n)
    return gathered.reshape(n * piece_t.shape[0], piece_t.shape[1])


def col_reduce_scatter(full, n, collective_id):
    width = full.shape[1] // n
    chunks = _chunk_order(full.T.reshape(n, width, full.shape[0]), n)
    return col_exchange(chunks, n, "scatter", collective_id).T


def all_reduce(full, n, collective_id):
    width = full.shape[1] // n
    chunks = _chunk_order(full.T.reshape(n, width, full.shape[0]), n)
    summed_t = _col_order(col_exchange(chunks, n, "allreduce", collective_id), n)
    return summed_t.reshape(n * width, full.shape[0]).T


def row_sum(piece, n, collective_id):
    return col_exchange(piece, n, "rowsum", collective_id)


def local(tensor, first_factor, second_factor):
    frame_count, col_count, row_count = tensor.shape
    components = first_factor.shape[0]
    n = lax.axis_size("col")
    second_values = second_factor.astype(jnp.float32)
    gram_first_part = gram_of(first_factor)
    gram_second_part = gram_of(second_factor)
    block_t = col_gather_t(first_factor.T, n)
    frame_part = frame_pass(tensor, block_t, second_values.T).T
    scaled_second = gram_second_part * (1.0 / lax.axis_size("row"))
    summed = all_reduce(jnp.concatenate([frame_part, gram_first_part, scaled_second], axis=1), n, 3)
    frame_sum = summed[:, :frame_count]
    gram_first = summed[:, frame_count:frame_count + components]
    gram_second = summed[:, frame_count + components:]
    frames = ridge_solve(gram_first * gram_second, frame_sum)
    gram_frames = jnp.dot(frames, frames.T, precision=lax.Precision.HIGHEST)
    full_part = accumulate_pass(tensor, frames, second_values)
    first_sum_mine = col_reduce_scatter(full_part, n, 1)
    new_first_mine = ridge_solve(gram_second * gram_frames, first_sum_mine).astype(jnp.bfloat16)
    new_block_t = col_gather_t(new_first_mine.T, n)
    gram_new_part = lax.dot_general(
        new_block_t, new_block_t, (((0,), (0,)), ((), ())), preferred_element_type=jnp.float32
    )
    second_part_t = second_pass(tensor, new_block_t, frames.T)
    summed_new = row_sum(jnp.concatenate([second_part_t, gram_new_part], axis=0), n, 4)
    second_sum = summed_new[:col_count].T
    gram_new = summed_new[col_count:]
    new_second = ridge_solve(gram_new * gram_frames, second_sum)
    full_next = accumulate_pass(tensor, frames, new_second)
    mode_one = col_reduce_scatter(full_next, n, 2)
    return (frames, mode_one)


def solution(mesh):
    return jax.shard_map(
        local,
        mesh=mesh,
        in_specs=(P(None, "col", "row"), P(None, ("row", "col")), P(None, "col")),
        out_specs=(P(), P(None, ("row", "col"))),
        check_vma=False,
    )
```

```python
import functools

import jax
import jax.numpy as jnp
from jax import lax
from jax.experimental import pallas as pl
from jax.experimental.pallas import tpu as pltpu
from jax.sharding import PartitionSpec as P

ridge_weight = 0.05
MESH_ID = pl.DeviceIdType.MESH


def ridge_solve(gram, right_side):
    order_size = gram.shape[0]
    factor_low = jnp.linalg.cholesky(gram + ridge_weight * jnp.eye(order_size, dtype=jnp.float32))
    middle = lax.linalg.triangular_solve(factor_low, right_side, left_side=True, lower=True)
    return lax.linalg.triangular_solve(
        factor_low, middle, left_side=True, lower=True, transpose_a=True
    )


def gram_of(factor):
    return jnp.dot(factor, factor.T, preferred_element_type=jnp.float32)


STREAM_FRAMES = 32


def _frame_kernel(block_t_ref, second_t_ref, slab_ref, out_ref):
    frames, width, rows = slab_ref.shape
    projected = jnp.dot(
        slab_ref[...].reshape(frames * width, rows), block_t_ref[...],
        preferred_element_type=jnp.float32,
    ).reshape(frames, width, block_t_ref.shape[1])
    out_ref[...] = jnp.sum(projected * second_t_ref[...][None], axis=1)


def _second_kernel(block_t_ref, frames_t_ref, slab_ref, out_ref):
    frames, width, rows = slab_ref.shape

    @pl.when(pl.program_id(0) == 0)
    def _():
        out_ref[...] = jnp.zeros_like(out_ref)

    projected = jnp.dot(
        slab_ref[...].reshape(frames * width, rows), block_t_ref[...],
        preferred_element_type=jnp.float32,
    ).reshape(frames, width, block_t_ref.shape[1])
    out_ref[...] += jnp.sum(projected * frames_t_ref[...][:, None, :], axis=0)


def _slab_spec(width, rows):
    return pl.BlockSpec((STREAM_FRAMES, width, rows), lambda s: (s, 0, 0))


def _whole(shape):
    return pl.BlockSpec(shape, lambda s: (0,) * len(shape))


def frame_pass(tensor, block_t, second_t):
    frame_count, width, rows = tensor.shape
    components = block_t.shape[1]
    return pl.pallas_call(
        _frame_kernel,
        grid=(frame_count // STREAM_FRAMES,),
        in_specs=[_whole(block_t.shape), _whole(second_t.shape), _slab_spec(width, rows)],
        out_specs=pl.BlockSpec((STREAM_FRAMES, components), lambda s: (s, 0)),
        out_shape=jax.ShapeDtypeStruct((frame_count, components), jnp.float32),
        cost_estimate=pl.CostEstimate(
            flops=2 * components * frame_count * width * rows, transcendentals=0,
            bytes_accessed=2 * frame_count * width * rows,
        ),
    )(block_t, second_t, tensor)


def second_pass(tensor, block_t, frames_t):
    frame_count, width, rows = tensor.shape
    components = block_t.shape[1]
    return pl.pallas_call(
        _second_kernel,
        grid=(frame_count // STREAM_FRAMES,),
        in_specs=[
            _whole(block_t.shape),
            pl.BlockSpec((STREAM_FRAMES, components), lambda s: (s, 0)),
            _slab_spec(width, rows),
        ],
        out_specs=_whole((width, components)),
        out_shape=jax.ShapeDtypeStruct((width, components), jnp.float32),
        cost_estimate=pl.CostEstimate(
            flops=2 * components * frame_count * width * rows, transcendentals=0,
            bytes_accessed=2 * frame_count * width * rows,
        ),
    )(block_t, frames_t, tensor)


def _accumulate_kernel(frames_ref, tiled_ref, slab_ref, out_ref):
    frames, width, rows = slab_ref.shape
    step = pl.program_id(0)

    @pl.when(step == 0)
    def _():
        out_ref[...] = jnp.zeros_like(out_ref)

    frame_count = frames_ref.shape[1]
    span = frames * width
    which = lax.broadcasted_iota(jnp.int32, (frame_count, span), 0) - step * frames
    column = lax.broadcasted_iota(jnp.int32, (frame_count, span), 1)
    expand = ((column >= which * width) & (column < which * width + width)).astype(jnp.bfloat16)
    rest = frames_ref[...]
    repeated = jnp.zeros((frames_ref.shape[0], span), jnp.float32)
    for _ in range(3):
        piece = rest.astype(jnp.bfloat16)
        rest = rest - piece.astype(jnp.float32)
        repeated = repeated + jnp.dot(piece, expand, preferred_element_type=jnp.float32)
    weights = (repeated * tiled_ref[...]).astype(jnp.bfloat16)
    out_ref[...] += jnp.dot(
        weights, slab_ref[...].reshape(span, rows), preferred_element_type=jnp.float32
    )


def accumulate_pass(tensor, frames, second):
    frame_count, width, rows = tensor.shape
    components = frames.shape[0]
    tiled = jnp.tile(second, (1, STREAM_FRAMES))
    return pl.pallas_call(
        _accumulate_kernel,
        grid=(frame_count // STREAM_FRAMES,),
        in_specs=[_whole(frames.shape), _whole(tiled.shape), _slab_spec(width, rows)],
        out_specs=_whole((components, rows)),
        out_shape=jax.ShapeDtypeStruct((components, rows), jnp.float32),
        cost_estimate=pl.CostEstimate(
            flops=2 * components * frame_count * width * rows, transcendentals=0,
            bytes_accessed=2 * frame_count * width * rows,
        ),
    )(frames, tiled, tensor)


def _split(n):
    inner = next(d for d in (8, 4, 2, 1) if n % d == 0 and d * d <= n)
    return inner, n // inner


def _exchange_kernel(n, rows, mode, send_ref, out_ref, *scratch):
    me = lax.axis_index("col")
    row = lax.axis_index("row")
    inner, outer = _split(n)
    low = lax.rem(me, inner)
    high = me // inner

    def in_low(peer):
        return (row, high * inner + peer)

    def in_high(peer):
        return (row, peer * inner + low)

    def in_row(peer):
        return (peer, me)

    def exchange(count, mine, device, source, landing, sends, recvs):
        def descriptor(peer, slot):
            return pltpu.make_async_remote_copy(
                src_ref=source(peer),
                dst_ref=landing.at[slot],
                send_sem=sends.at[peer],
                recv_sem=recvs.at[slot],
                device_id=device(peer),
                device_id_type=MESH_ID,
            )

        def start(t, carry):
            peer = lax.rem(mine + 1 + t, count)
            descriptor(peer, mine).start()
            return carry

        lax.fori_loop(0, count - 1, start, 0)

        def finish(t, carry):
            peer = lax.rem(mine + 1 + t, count)
            copy = descriptor(peer, peer)
            copy.wait_send()
            copy.wait_recv()
            return carry

        lax.fori_loop(0, count - 1, finish, 0)
        landing[mine] = source(mine)[...]

    if mode == "rowsum":
        groups = [(rows, row, in_row)]
    else:
        groups = [(inner, low, in_low), (outer, high, in_high)]
        if mode == "allreduce":
            groups.append((rows, row, in_row))
    barrier = pltpu.get_barrier_semaphore()
    for count, mine, device in groups:
        def greet(t, carry, count=count, mine=mine, device=device):
            peer = lax.rem(mine + 1 + t, count)
            pl.semaphore_signal(barrier, inc=1, device_id=device(peer), device_id_type=MESH_ID)
            return carry

        lax.fori_loop(0, count - 1, greet, 0)
    pl.semaphore_wait(barrier, sum(count - 1 for count, _, _ in groups))

    scratch = list(scratch)

    def take(k):
        taken = scratch[:k]
        del scratch[:k]
        return taken

    def gather(piece_ref):
        bundle, s1, r1 = take(3)
        exchange(inner, low, in_low, lambda peer: piece_ref, bundle, s1, r1)
        everything, s2, r2 = take(3)
        exchange(outer, high, in_high, lambda peer: bundle, everything, s2, r2)
        out_ref[...] = everything[...]

    if mode == "rowsum":
        landing, s1, r1 = take(3)
        exchange(rows, row, in_row, lambda peer: send_ref, landing, s1, r1)
        out_ref[...] = jnp.sum(landing[...], axis=0)
        return
    if mode == "gather":
        gather(send_ref)
        return
    landing, s1, r1, partial = take(4)
    exchange(outer, high, in_high, lambda peer: send_ref.at[peer], landing, s1, r1)
    partial[...] = jnp.sum(landing[...], axis=0)
    if mode == "scatter":
        landing2, s2, r2 = take(3)
        exchange(inner, low, in_low, lambda peer: partial.at[peer], landing2, s2, r2)
        out_ref[...] = jnp.sum(landing2[...], axis=0)
        return
    landing2, s2, r2, bundle = take(4)
    exchange(inner, low, in_low, lambda peer: partial, landing2, s2, r2)
    bundle[...] = jnp.sum(landing2[...], axis=0)
    row_landing, s3, r3, total = take(4)
    exchange(rows, row, in_row, lambda peer: bundle, row_landing, s3, r3)
    total[...] = jnp.sum(row_landing[...], axis=0)
    everything, s4, r4 = take(3)
    exchange(outer, high, in_high, lambda peer: total, everything, s4, r4)
    out_ref[...] = everything[...]


def col_exchange(send, n, mode, collective_id):
    rows = lax.axis_size("row")
    inner, outer = _split(n)
    dtype = send.dtype

    def stage(count, piece):
        return [
            pltpu.VMEM((count,) + piece, dtype),
            pltpu.SemaphoreType.DMA((count,)),
            pltpu.SemaphoreType.DMA((count,)),
        ]

    if mode == "rowsum":
        piece = tuple(send.shape)
        out_shape = piece
        scratch = stage(rows, piece)
    elif mode == "gather":
        piece = tuple(send.shape)
        out_shape = (outer, inner) + piece
        scratch = stage(inner, piece) + stage(outer, (inner,) + piece)
    else:
        piece = tuple(send.shape[2:])
        out_shape = piece if mode == "scatter" else (outer, inner) + piece
        bundle = (inner,) + piece
        scratch = stage(outer, bundle) + [pltpu.VMEM(bundle, dtype)]
        if mode == "scatter":
            scratch += stage(inner, piece)
        else:
            scratch += stage(inner, bundle) + [pltpu.VMEM(bundle, dtype)]
            scratch += stage(rows, bundle) + [pltpu.VMEM(bundle, dtype)]
            scratch += stage(outer, bundle)
    return pl.pallas_call(
        functools.partial(_exchange_kernel, n, rows, mode),
        out_shape=jax.ShapeDtypeStruct(out_shape, dtype),
        in_specs=[pl.BlockSpec(memory_space=pltpu.VMEM)],
        out_specs=pl.BlockSpec(memory_space=pltpu.VMEM),
        scratch_shapes=scratch,
        compiler_params=pltpu.CompilerParams(collective_id=collective_id, has_side_effects=True),
    )(send)


def _chunk_order(chunks, n):
    inner, outer = _split(n)
    return chunks.reshape((outer, inner) + chunks.shape[1:])


def _col_order(gathered, n):
    return gathered.reshape((n,) + gathered.shape[2:])


def col_gather_t(piece_t, n):
    gathered = _col_order(col_exchange(piece_t, n, "gather", 0), n)
    return gathered.reshape(n * piece_t.shape[0], piece_t.shape[1])


def col_reduce_scatter(full, n, collective_id):
    width = full.shape[1] // n
    chunks = _chunk_order(full.T.reshape(n, width, full.shape[0]), n)
    return col_exchange(chunks, n, "scatter", collective_id).T


def all_reduce(full, n, collective_id):
    width = full.shape[1] // n
    chunks = _chunk_order(full.T.reshape(n, width, full.shape[0]), n)
    summed_t = _col_order(col_exchange(chunks, n, "allreduce", collective_id), n)
    return summed_t.reshape(n * width, full.shape[0]).T


def row_sum(piece, n, collective_id):
    return col_exchange(piece, n, "rowsum", collective_id)


def local(tensor, first_factor, second_factor):
    frame_count, col_count, row_count = tensor.shape
    components = first_factor.shape[0]
    n = lax.axis_size("col")
    second_values = second_factor.astype(jnp.float32)
    gram_first_part = gram_of(first_factor)
    gram_second_part = gram_of(second_factor)
    block_t = col_gather_t(first_factor.T, n)
    frame_part = frame_pass(tensor, block_t, second_values.T).T
    scaled_second = gram_second_part * (1.0 / lax.axis_size("row"))
    summed = all_reduce(jnp.concatenate([frame_part, gram_first_part, scaled_second], axis=1), n, 3)
    frame_sum = summed[:, :frame_count]
    gram_first = summed[:, frame_count:frame_count + components]
    gram_second = summed[:, frame_count + components:]
    frames = ridge_solve(gram_first * gram_second, frame_sum)
    gram_frames = jnp.dot(frames, frames.T, precision=lax.Precision.HIGHEST)
    full_part = accumulate_pass(tensor, frames, second_values)
    first_sum_mine = col_reduce_scatter(full_part, n, 1)
    new_first_mine = ridge_solve(gram_second * gram_frames, first_sum_mine).astype(jnp.bfloat16)
    new_block_t = col_gather_t(new_first_mine.T, n)
    gram_new_part = lax.dot_general(
        new_block_t, new_block_t, (((0,), (0,)), ((), ())), preferred_element_type=jnp.float32
    )
    second_part_t = second_pass(tensor, new_block_t, frames.T)
    summed_new = row_sum(jnp.concatenate([second_part_t, gram_new_part], axis=0), n, 4)
    second_sum = summed_new[:col_count].T
    gram_new = summed_new[col_count:]
    new_second = ridge_solve(gram_new * gram_frames, second_sum)
    full_next = accumulate_pass(tensor, frames, new_second)
    mode_one = col_reduce_scatter(full_next, n, 2)
    return (frames, mode_one)


def solution(mesh):
    return jax.shard_map(
        local,
        mesh=mesh,
        in_specs=(P(None, "col", "row"), P(None, ("row", "col")), P(None, "col")),
        out_specs=(P(), P(None, ("row", "col"))),
        check_vma=False,
    )
```

```python
import functools

import jax
import jax.numpy as jnp
from jax import lax
from jax.experimental import pallas as pl
from jax.experimental.pallas import tpu as pltpu
from jax.sharding import PartitionSpec as P

ridge_weight = 0.05
MESH_ID = pl.DeviceIdType.MESH


def ridge_solve(gram, right_side):
    order_size = gram.shape[0]
    factor_low = jnp.linalg.cholesky(gram + ridge_weight * jnp.eye(order_size, dtype=jnp.float32))
    middle = lax.linalg.triangular_solve(factor_low, right_side, left_side=True, lower=True)
    return lax.linalg.triangular_solve(
        factor_low, middle, left_side=True, lower=True, transpose_a=True
    )


def gram_of(factor):
    return jnp.dot(factor, factor.T, preferred_element_type=jnp.float32)


STREAM_FRAMES = 32


def _frame_kernel(block_t_ref, second_t_ref, slab_ref, out_ref):
    frames, width, rows = slab_ref.shape
    projected = jnp.dot(
        slab_ref[...].reshape(frames * width, rows), block_t_ref[...],
        preferred_element_type=jnp.float32,
    ).reshape(frames, width, block_t_ref.shape[1])
    out_ref[...] = jnp.sum(projected * second_t_ref[...][None], axis=1)


def _second_kernel(block_t_ref, frames_t_ref, slab_ref, out_ref):
    frames, width, rows = slab_ref.shape

    @pl.when(pl.program_id(0) == 0)
    def _():
        out_ref[...] = jnp.zeros_like(out_ref)

    projected = jnp.dot(
        slab_ref[...].reshape(frames * width, rows), block_t_ref[...],
        preferred_element_type=jnp.float32,
    ).reshape(frames, width, block_t_ref.shape[1])
    out_ref[...] += jnp.sum(projected * frames_t_ref[...][:, None, :], axis=0)


def _slab_spec(width, rows):
    return pl.BlockSpec((STREAM_FRAMES, width, rows), lambda s: (s, 0, 0))


def _whole(shape):
    return pl.BlockSpec(shape, lambda s: (0,) * len(shape))


def frame_pass(tensor, block_t, second_t):
    frame_count, width, rows = tensor.shape
    components = block_t.shape[1]
    return pl.pallas_call(
        _frame_kernel,
        grid=(frame_count // STREAM_FRAMES,),
        in_specs=[_whole(block_t.shape), _whole(second_t.shape), _slab_spec(width, rows)],
        out_specs=pl.BlockSpec((STREAM_FRAMES, components), lambda s: (s, 0)),
        out_shape=jax.ShapeDtypeStruct((frame_count, components), jnp.float32),
        cost_estimate=pl.CostEstimate(
            flops=2 * components * frame_count * width * rows, transcendentals=0,
            bytes_accessed=2 * frame_count * width * rows,
        ),
    )(block_t, second_t, tensor)


def second_pass(tensor, block_t, frames_t):
    frame_count, width, rows = tensor.shape
    components = block_t.shape[1]
    return pl.pallas_call(
        _second_kernel,
        grid=(frame_count // STREAM_FRAMES,),
        in_specs=[
            _whole(block_t.shape),
            pl.BlockSpec((STREAM_FRAMES, components), lambda s: (s, 0)),
            _slab_spec(width, rows),
        ],
        out_specs=_whole((width, components)),
        out_shape=jax.ShapeDtypeStruct((width, components), jnp.float32),
        cost_estimate=pl.CostEstimate(
            flops=2 * components * frame_count * width * rows, transcendentals=0,
            bytes_accessed=2 * frame_count * width * rows,
        ),
    )(block_t, frames_t, tensor)


def _accumulate_kernel(frames_ref, tiled_ref, slab_ref, out_ref):
    frames, width, rows = slab_ref.shape
    step = pl.program_id(0)

    @pl.when(step == 0)
    def _():
        out_ref[...] = jnp.zeros_like(out_ref)

    frame_count = frames_ref.shape[1]
    span = frames * width
    which = lax.broadcasted_iota(jnp.int32, (frame_count, span), 0) - step * frames
    column = lax.broadcasted_iota(jnp.int32, (frame_count, span), 1)
    expand = ((column >= which * width) & (column < which * width + width)).astype(jnp.bfloat16)
    rest = frames_ref[...]
    repeated = jnp.zeros((frames_ref.shape[0], span), jnp.float32)
    for _ in range(3):
        piece = rest.astype(jnp.bfloat16)
        rest = rest - piece.astype(jnp.float32)
        repeated = repeated + jnp.dot(piece, expand, preferred_element_type=jnp.float32)
    weights = (repeated * tiled_ref[...]).astype(jnp.bfloat16)
    out_ref[...] += jnp.dot(
        weights, slab_ref[...].reshape(span, rows), preferred_element_type=jnp.float32
    )


def accumulate_pass(tensor, frames, second):
    frame_count, width, rows = tensor.shape
    components = frames.shape[0]
    tiled = jnp.tile(second, (1, STREAM_FRAMES))
    return pl.pallas_call(
        _accumulate_kernel,
        grid=(frame_count // STREAM_FRAMES,),
        in_specs=[_whole(frames.shape), _whole(tiled.shape), _slab_spec(width, rows)],
        out_specs=_whole((components, rows)),
        out_shape=jax.ShapeDtypeStruct((components, rows), jnp.float32),
        cost_estimate=pl.CostEstimate(
            flops=2 * components * frame_count * width * rows, transcendentals=0,
            bytes_accessed=2 * frame_count * width * rows,
        ),
    )(frames, tiled, tensor)


def _split(n):
    inner = next(d for d in (8, 4, 2, 1) if n % d == 0 and d * d <= n)
    return inner, n // inner


def _exchange_kernel(n, rows, mode, *refs):
    if mode == "solve":
        send_ref, op_ref, out_ref = refs[:3]
        scratch = refs[3:]
    else:
        send_ref, out_ref = refs[:2]
        scratch = refs[2:]
    me = lax.axis_index("col")
    row = lax.axis_index("row")
    inner, outer = _split(n)
    low = lax.rem(me, inner)
    high = me // inner

    def in_low(peer):
        return (row, high * inner + peer)

    def in_high(peer):
        return (row, peer * inner + low)

    def in_row(peer):
        return (peer, me)

    def exchange(count, mine, device, source, landing, sends, recvs):
        def descriptor(peer, slot):
            return pltpu.make_async_remote_copy(
                src_ref=source(peer),
                dst_ref=landing.at[slot],
                send_sem=sends.at[peer],
                recv_sem=recvs.at[slot],
                device_id=device(peer),
                device_id_type=MESH_ID,
            )

        def start(t, carry):
            peer = lax.rem(mine + 1 + t, count)
            descriptor(peer, mine).start()
            return carry

        lax.fori_loop(0, count - 1, start, 0)

        def finish(t, carry):
            peer = lax.rem(mine + 1 + t, count)
            copy = descriptor(peer, peer)
            copy.wait_send()
            copy.wait_recv()
            return carry

        lax.fori_loop(0, count - 1, finish, 0)
        landing[mine] = source(mine)[...]

    if mode == "rowsum":
        groups = [(rows, row, in_row)]
    else:
        groups = [(inner, low, in_low), (outer, high, in_high)]
        if mode == "allreduce":
            groups.append((rows, row, in_row))
    barrier = pltpu.get_barrier_semaphore()
    for count, mine, device in groups:
        def greet(t, carry, count=count, mine=mine, device=device):
            peer = lax.rem(mine + 1 + t, count)
            pl.semaphore_signal(barrier, inc=1, device_id=device(peer), device_id_type=MESH_ID)
            return carry

        lax.fori_loop(0, count - 1, greet, 0)
    pl.semaphore_wait(barrier, sum(count - 1 for count, _, _ in groups))

    scratch = list(scratch)

    def take(k):
        taken = scratch[:k]
        del scratch[:k]
        return taken

    def gather(piece_ref):
        bundle, s1, r1 = take(3)
        exchange(inner, low, in_low, lambda peer: piece_ref, bundle, s1, r1)
        everything, s2, r2 = take(3)
        exchange(outer, high, in_high, lambda peer: bundle, everything, s2, r2)
        out_ref[...] = everything[...]

    if mode == "rowsum":
        landing, s1, r1 = take(3)
        exchange(rows, row, in_row, lambda peer: send_ref, landing, s1, r1)
        out_ref[...] = jnp.sum(landing[...], axis=0)
        return
    if mode == "gather":
        gather(send_ref)
        return
    landing, s1, r1, partial = take(4)
    exchange(outer, high, in_high, lambda peer: send_ref.at[peer], landing, s1, r1)
    partial[...] = jnp.sum(landing[...], axis=0)
    if mode == "scatter":
        landing2, s2, r2 = take(3)
        exchange(inner, low, in_low, lambda peer: partial.at[peer], landing2, s2, r2)
        out_ref[...] = jnp.sum(landing2[...], axis=0)
        return
    if mode == "solve":
        landing2, s2, r2, solved = take(4)
        exchange(inner, low, in_low, lambda peer: partial.at[peer], landing2, s2, r2)
        chunk = jnp.sum(landing2[...], axis=0)
        solved[...] = jnp.dot(
            chunk, op_ref[...], precision=lax.Precision.HIGHEST, preferred_element_type=jnp.float32
        ).astype(solved.dtype)
        gather(solved)
        return
    landing2, s2, r2, bundle = take(4)
    exchange(inner, low, in_low, lambda peer: partial, landing2, s2, r2)
    bundle[...] = jnp.sum(landing2[...], axis=0)
    row_landing, s3, r3, total = take(4)
    exchange(rows, row, in_row, lambda peer: bundle, row_landing, s3, r3)
    total[...] = jnp.sum(row_landing[...], axis=0)
    everything, s4, r4 = take(3)
    exchange(outer, high, in_high, lambda peer: total, everything, s4, r4)
    out_ref[...] = everything[...]


def col_exchange(send, n, mode, collective_id, op=None, out_dtype=None):
    rows = lax.axis_size("row")
    inner, outer = _split(n)
    dtype = send.dtype

    def stage(count, piece, kind=dtype):
        return [
            pltpu.VMEM((count,) + piece, kind),
            pltpu.SemaphoreType.DMA((count,)),
            pltpu.SemaphoreType.DMA((count,)),
        ]

    if mode == "rowsum":
        piece = tuple(send.shape)
        out_shape = piece
        scratch = stage(rows, piece)
    elif mode == "gather":
        piece = tuple(send.shape)
        out_shape = (outer, inner) + piece
        scratch = stage(inner, piece) + stage(outer, (inner,) + piece)
    else:
        piece = tuple(send.shape[2:])
        out_shape = piece if mode == "scatter" else (outer, inner) + piece
        bundle = (inner,) + piece
        scratch = stage(outer, bundle) + [pltpu.VMEM(bundle, dtype)]
        if mode == "scatter":
            scratch += stage(inner, piece)
        elif mode == "solve":
            out_shape = (outer, inner) + piece
            scratch += stage(inner, piece) + [pltpu.VMEM(piece, out_dtype)]
            scratch += stage(inner, piece, out_dtype) + stage(outer, (inner,) + piece, out_dtype)
        else:
            scratch += stage(inner, bundle) + [pltpu.VMEM(bundle, dtype)]
            scratch += stage(rows, bundle) + [pltpu.VMEM(bundle, dtype)]
            scratch += stage(outer, bundle)
    operands = (send,) if op is None else (send, op)
    return pl.pallas_call(
        functools.partial(_exchange_kernel, n, rows, mode),
        out_shape=jax.ShapeDtypeStruct(out_shape, out_dtype or dtype),
        in_specs=[pl.BlockSpec(memory_space=pltpu.VMEM)] * len(operands),
        out_specs=pl.BlockSpec(memory_space=pltpu.VMEM),
        scratch_shapes=scratch,
        compiler_params=pltpu.CompilerParams(collective_id=collective_id, has_side_effects=True),
    )(*operands)


def _chunk_order(chunks, n):
    inner, outer = _split(n)
    return chunks.reshape((outer, inner) + chunks.shape[1:])


def _col_order(gathered, n):
    return gathered.reshape((n,) + gathered.shape[2:])


def col_gather_t(piece_t, n):
    gathered = _col_order(col_exchange(piece_t, n, "gather", 0), n)
    return gathered.reshape(n * piece_t.shape[0], piece_t.shape[1])


def col_reduce_scatter(full, n, collective_id):
    width = full.shape[1] // n
    chunks = _chunk_order(full.T.reshape(n, width, full.shape[0]), n)
    return col_exchange(chunks, n, "scatter", collective_id).T


def all_reduce(full, n, collective_id):
    width = full.shape[1] // n
    chunks = _chunk_order(full.T.reshape(n, width, full.shape[0]), n)
    summed_t = _col_order(col_exchange(chunks, n, "allreduce", collective_id), n)
    return summed_t.reshape(n * width, full.shape[0]).T


def solve_and_gather_t(full, operator_t, n, collective_id):
    width = full.shape[1] // n
    chunks = _chunk_order(full.T.reshape(n, width, full.shape[0]), n)
    gathered = col_exchange(
        chunks, n, "solve", collective_id, op=operator_t, out_dtype=jnp.bfloat16
    )
    return gathered.reshape(n * width, full.shape[0])


def row_sum(piece, n, collective_id):
    return col_exchange(piece, n, "rowsum", collective_id)


def local(tensor, first_factor, second_factor):
    frame_count, col_count, row_count = tensor.shape
    components = first_factor.shape[0]
    n = lax.axis_size("col")
    second_values = second_factor.astype(jnp.float32)
    gram_first_part = gram_of(first_factor)
    gram_second_part = gram_of(second_factor)
    block_t = col_gather_t(first_factor.T, n)
    frame_part = frame_pass(tensor, block_t, second_values.T).T
    scaled_second = gram_second_part * (1.0 / lax.axis_size("row"))
    summed = all_reduce(jnp.concatenate([frame_part, gram_first_part, scaled_second], axis=1), n, 3)
    frame_sum = summed[:, :frame_count]
    gram_first = summed[:, frame_count:frame_count + components]
    gram_second = summed[:, frame_count + components:]
    frames = ridge_solve(gram_first * gram_second, frame_sum)
    gram_frames = jnp.dot(frames, frames.T, precision=lax.Precision.HIGHEST)
    full_part = accumulate_pass(tensor, frames, second_values)
    inverse = ridge_solve(gram_second * gram_frames, jnp.eye(components, dtype=jnp.float32))
    new_block_t = solve_and_gather_t(full_part, inverse.T, n, 1)
    gram_new_part = lax.dot_general(
        new_block_t, new_block_t, (((0,), (0,)), ((), ())), preferred_element_type=jnp.float32
    )
    second_part_t = second_pass(tensor, new_block_t, frames.T)
    summed_new = row_sum(jnp.concatenate([second_part_t, gram_new_part], axis=0), n, 4)
    second_sum = summed_new[:col_count].T
    gram_new = summed_new[col_count:]
    new_second = ridge_solve(gram_new * gram_frames, second_sum)
    full_next = accumulate_pass(tensor, frames, new_second)
    mode_one = col_reduce_scatter(full_next, n, 2)
    return (frames, mode_one)


def solution(mesh):
    return jax.shard_map(
        local,
        mesh=mesh,
        in_specs=(P(None, "col", "row"), P(None, ("row", "col")), P(None, "col")),
        out_specs=(P(), P(None, ("row", "col"))),
        check_vma=False,
    )
```

```python
import functools

import jax
import jax.numpy as jnp
from jax import lax
from jax.experimental import pallas as pl
from jax.experimental.pallas import tpu as pltpu
from jax.sharding import PartitionSpec as P

ridge_weight = 0.05
MESH_ID = pl.DeviceIdType.MESH


def ridge_solve(gram, right_side):
    order_size = gram.shape[0]
    factor_low = jnp.linalg.cholesky(gram + ridge_weight * jnp.eye(order_size, dtype=jnp.float32))
    middle = lax.linalg.triangular_solve(factor_low, right_side, left_side=True, lower=True)
    return lax.linalg.triangular_solve(
        factor_low, middle, left_side=True, lower=True, transpose_a=True
    )


def gram_of(factor):
    return jnp.dot(factor, factor.T, preferred_element_type=jnp.float32)


STREAM_FRAMES = 32


def _frame_kernel(block_t_ref, second_t_ref, slab_ref, out_ref):
    frames, width, rows = slab_ref.shape
    projected = jnp.dot(
        slab_ref[...].reshape(frames * width, rows), block_t_ref[...],
        preferred_element_type=jnp.float32,
    ).reshape(frames, width, block_t_ref.shape[1])
    out_ref[...] = jnp.sum(projected * second_t_ref[...][None], axis=1)


def _second_kernel(block_t_ref, frames_t_ref, slab_ref, out_ref):
    frames, width, rows = slab_ref.shape

    @pl.when(pl.program_id(0) == 0)
    def _():
        out_ref[...] = jnp.zeros_like(out_ref)

    projected = jnp.dot(
        slab_ref[...].reshape(frames * width, rows), block_t_ref[...],
        preferred_element_type=jnp.float32,
    ).reshape(frames, width, block_t_ref.shape[1])
    out_ref[...] += jnp.sum(projected * frames_t_ref[...][:, None, :], axis=0)


def _slab_spec(width, rows):
    return pl.BlockSpec((STREAM_FRAMES, width, rows), lambda s: (s, 0, 0))


def _whole(shape):
    return pl.BlockSpec(shape, lambda s: (0,) * len(shape))


def frame_pass(tensor, block_t, second_t):
    frame_count, width, rows = tensor.shape
    components = block_t.shape[1]
    return pl.pallas_call(
        _frame_kernel,
        grid=(frame_count // STREAM_FRAMES,),
        in_specs=[_whole(block_t.shape), _whole(second_t.shape), _slab_spec(width, rows)],
        out_specs=pl.BlockSpec((STREAM_FRAMES, components), lambda s: (s, 0)),
        out_shape=jax.ShapeDtypeStruct((frame_count, components), jnp.float32),
        cost_estimate=pl.CostEstimate(
            flops=2 * components * frame_count * width * rows, transcendentals=0,
            bytes_accessed=2 * frame_count * width * rows,
        ),
    )(block_t, second_t, tensor)


def second_pass(tensor, block_t, frames_t):
    frame_count, width, rows = tensor.shape
    components = block_t.shape[1]
    return pl.pallas_call(
        _second_kernel,
        grid=(frame_count // STREAM_FRAMES,),
        in_specs=[
            _whole(block_t.shape),
            pl.BlockSpec((STREAM_FRAMES, components), lambda s: (s, 0)),
            _slab_spec(width, rows),
        ],
        out_specs=_whole((width, components)),
        out_shape=jax.ShapeDtypeStruct((width, components), jnp.float32),
        cost_estimate=pl.CostEstimate(
            flops=2 * components * frame_count * width * rows, transcendentals=0,
            bytes_accessed=2 * frame_count * width * rows,
        ),
    )(block_t, frames_t, tensor)


def _accumulate_kernel(frames_ref, tiled_ref, slab_ref, out_ref, total_ref):
    frames, width, rows = slab_ref.shape
    step = pl.program_id(0)

    @pl.when(step == 0)
    def _():
        total_ref[...] = jnp.zeros_like(total_ref)

    frame_count = frames_ref.shape[1]
    span = frames * width
    which = lax.broadcasted_iota(jnp.int32, (frame_count, span), 0) - step * frames
    column = lax.broadcasted_iota(jnp.int32, (frame_count, span), 1)
    expand = ((column >= which * width) & (column < which * width + width)).astype(jnp.bfloat16)
    rest = frames_ref[...]
    repeated = jnp.zeros((frames_ref.shape[0], span), jnp.float32)
    for _ in range(3):
        piece = rest.astype(jnp.bfloat16)
        rest = rest - piece.astype(jnp.float32)
        repeated = repeated + jnp.dot(piece, expand, preferred_element_type=jnp.float32)
    weights = (repeated * tiled_ref[...]).astype(jnp.bfloat16)
    total_ref[...] += jnp.dot(
        weights, slab_ref[...].reshape(span, rows), preferred_element_type=jnp.float32
    )

    @pl.when(step == pl.num_programs(0) - 1)
    def _():
        out_ref[...] = total_ref[...].T


def accumulate_pass_t(tensor, frames, second):
    frame_count, width, rows = tensor.shape
    components = frames.shape[0]
    tiled = jnp.tile(second, (1, STREAM_FRAMES))
    return pl.pallas_call(
        _accumulate_kernel,
        grid=(frame_count // STREAM_FRAMES,),
        in_specs=[_whole(frames.shape), _whole(tiled.shape), _slab_spec(width, rows)],
        out_specs=_whole((rows, components)),
        out_shape=jax.ShapeDtypeStruct((rows, components), jnp.float32),
        scratch_shapes=[pltpu.VMEM((components, rows), jnp.float32)],
        cost_estimate=pl.CostEstimate(
            flops=2 * components * frame_count * width * rows, transcendentals=0,
            bytes_accessed=2 * frame_count * width * rows,
        ),
    )(frames, tiled, tensor)


def _split(n):
    inner = next(d for d in (8, 4, 2, 1) if n % d == 0 and d * d <= n)
    return inner, n // inner


def _exchange_kernel(n, rows, mode, *refs):
    if mode == "solve":
        send_ref, op_ref, out_ref = refs[:3]
        scratch = refs[3:]
    else:
        send_ref, out_ref = refs[:2]
        scratch = refs[2:]
    me = lax.axis_index("col")
    row = lax.axis_index("row")
    inner, outer = _split(n)
    low = lax.rem(me, inner)
    high = me // inner

    def in_low(peer):
        return (row, high * inner + peer)

    def in_high(peer):
        return (row, peer * inner + low)

    def in_row(peer):
        return (peer, me)

    def exchange(count, mine, device, source, landing, sends, recvs):
        def descriptor(peer, slot):
            return pltpu.make_async_remote_copy(
                src_ref=source(peer),
                dst_ref=landing.at[slot],
                send_sem=sends.at[peer],
                recv_sem=recvs.at[slot],
                device_id=device(peer),
                device_id_type=MESH_ID,
            )

        def start(t, carry):
            peer = lax.rem(mine + 1 + t, count)
            descriptor(peer, mine).start()
            return carry

        lax.fori_loop(0, count - 1, start, 0)

        def finish(t, carry):
            peer = lax.rem(mine + 1 + t, count)
            copy = descriptor(peer, peer)
            copy.wait_send()
            copy.wait_recv()
            return carry

        lax.fori_loop(0, count - 1, finish, 0)
        landing[mine] = source(mine)[...]

    if mode == "rowsum":
        groups = [(rows, row, in_row)]
    else:
        groups = [(inner, low, in_low), (outer, high, in_high)]
        if mode == "allreduce":
            groups.append((rows, row, in_row))
    barrier = pltpu.get_barrier_semaphore()
    for count, mine, device in groups:
        def greet(t, carry, count=count, mine=mine, device=device):
            peer = lax.rem(mine + 1 + t, count)
            pl.semaphore_signal(barrier, inc=1, device_id=device(peer), device_id_type=MESH_ID)
            return carry

        lax.fori_loop(0, count - 1, greet, 0)
    pl.semaphore_wait(barrier, sum(count - 1 for count, _, _ in groups))

    scratch = list(scratch)

    def take(k):
        taken = scratch[:k]
        del scratch[:k]
        return taken

    def gather(piece_ref):
        bundle, s1, r1 = take(3)
        exchange(inner, low, in_low, lambda peer: piece_ref, bundle, s1, r1)
        everything, s2, r2 = take(3)
        exchange(outer, high, in_high, lambda peer: bundle, everything, s2, r2)
        out_ref[...] = everything[...]

    if mode == "rowsum":
        landing, s1, r1 = take(3)
        exchange(rows, row, in_row, lambda peer: send_ref, landing, s1, r1)
        out_ref[...] = jnp.sum(landing[...], axis=0)
        return
    if mode == "gather":
        gather(send_ref)
        return
    landing, s1, r1, partial = take(4)
    exchange(outer, high, in_high, lambda peer: send_ref.at[peer], landing, s1, r1)
    partial[...] = jnp.sum(landing[...], axis=0)
    if mode == "scatter":
        landing2, s2, r2 = take(3)
        exchange(inner, low, in_low, lambda peer: partial.at[peer], landing2, s2, r2)
        out_ref[...] = jnp.sum(landing2[...], axis=0)
        return
    if mode == "solve":
        landing2, s2, r2, solved = take(4)
        exchange(inner, low, in_low, lambda peer: partial.at[peer], landing2, s2, r2)
        chunk = jnp.sum(landing2[...], axis=0)
        solved[...] = jnp.dot(
            chunk, op_ref[...], precision=lax.Precision.HIGHEST, preferred_element_type=jnp.float32
        ).astype(solved.dtype)
        gather(solved)
        return
    landing2, s2, r2, bundle = take(4)
    exchange(inner, low, in_low, lambda peer: partial, landing2, s2, r2)
    bundle[...] = jnp.sum(landing2[...], axis=0)
    row_landing, s3, r3, total = take(4)
    exchange(rows, row, in_row, lambda peer: bundle, row_landing, s3, r3)
    total[...] = jnp.sum(row_landing[...], axis=0)
    everything, s4, r4 = take(3)
    exchange(outer, high, in_high, lambda peer: total, everything, s4, r4)
    out_ref[...] = everything[...]


def col_exchange(send, n, mode, collective_id, op=None, out_dtype=None):
    rows = lax.axis_size("row")
    inner, outer = _split(n)
    dtype = send.dtype

    def stage(count, piece, kind=dtype):
        return [
            pltpu.VMEM((count,) + piece, kind),
            pltpu.SemaphoreType.DMA((count,)),
            pltpu.SemaphoreType.DMA((count,)),
        ]

    if mode == "rowsum":
        piece = tuple(send.shape)
        out_shape = piece
        scratch = stage(rows, piece)
    elif mode == "gather":
        piece = tuple(send.shape)
        out_shape = (outer, inner) + piece
        scratch = stage(inner, piece) + stage(outer, (inner,) + piece)
    else:
        piece = tuple(send.shape[2:])
        out_shape = piece if mode == "scatter" else (outer, inner) + piece
        bundle = (inner,) + piece
        scratch = stage(outer, bundle) + [pltpu.VMEM(bundle, dtype)]
        if mode == "scatter":
            scratch += stage(inner, piece)
        elif mode == "solve":
            out_shape = (outer, inner) + piece
            scratch += stage(inner, piece) + [pltpu.VMEM(piece, out_dtype)]
            scratch += stage(inner, piece, out_dtype) + stage(outer, (inner,) + piece, out_dtype)
        else:
            scratch += stage(inner, bundle) + [pltpu.VMEM(bundle, dtype)]
            scratch += stage(rows, bundle) + [pltpu.VMEM(bundle, dtype)]
            scratch += stage(outer, bundle)
    operands = (send,) if op is None else (send, op)
    return pl.pallas_call(
        functools.partial(_exchange_kernel, n, rows, mode),
        out_shape=jax.ShapeDtypeStruct(out_shape, out_dtype or dtype),
        in_specs=[pl.BlockSpec(memory_space=pltpu.VMEM)] * len(operands),
        out_specs=pl.BlockSpec(memory_space=pltpu.VMEM),
        scratch_shapes=scratch,
        compiler_params=pltpu.CompilerParams(collective_id=collective_id, has_side_effects=True),
    )(*operands)


def _chunk_order(chunks, n):
    inner, outer = _split(n)
    return chunks.reshape((outer, inner) + chunks.shape[1:])


def _col_order(gathered, n):
    return gathered.reshape((n,) + gathered.shape[2:])


def col_gather_t(piece_t, n):
    gathered = _col_order(col_exchange(piece_t, n, "gather", 0), n)
    return gathered.reshape(n * piece_t.shape[0], piece_t.shape[1])


def col_reduce_scatter(full_t, n, collective_id):
    width = full_t.shape[0] // n
    chunks = _chunk_order(full_t.reshape(n, width, full_t.shape[1]), n)
    return col_exchange(chunks, n, "scatter", collective_id).T


def all_reduce(full, n, collective_id):
    width = full.shape[1] // n
    chunks = _chunk_order(full.T.reshape(n, width, full.shape[0]), n)
    summed_t = _col_order(col_exchange(chunks, n, "allreduce", collective_id), n)
    return summed_t.reshape(n * width, full.shape[0]).T


def solve_and_gather_t(full_t, operator_t, n, collective_id):
    width = full_t.shape[0] // n
    chunks = _chunk_order(full_t.reshape(n, width, full_t.shape[1]), n)
    gathered = col_exchange(
        chunks, n, "solve", collective_id, op=operator_t, out_dtype=jnp.bfloat16
    )
    return gathered.reshape(n * width, full_t.shape[1])


def row_sum(piece, n, collective_id):
    return col_exchange(piece, n, "rowsum", collective_id)


def local(tensor, first_factor, second_factor):
    frame_count, col_count, row_count = tensor.shape
    components = first_factor.shape[0]
    n = lax.axis_size("col")
    second_values = second_factor.astype(jnp.float32)
    gram_first_part = gram_of(first_factor)
    gram_second_part = gram_of(second_factor)
    block_t = col_gather_t(first_factor.T, n)
    frame_part = frame_pass(tensor, block_t, second_values.T).T
    scaled_second = gram_second_part * (1.0 / lax.axis_size("row"))
    summed = all_reduce(jnp.concatenate([frame_part, gram_first_part, scaled_second], axis=1), n, 3)
    frame_sum = summed[:, :frame_count]
    gram_first = summed[:, frame_count:frame_count + components]
    gram_second = summed[:, frame_count + components:]
    frames = ridge_solve(gram_first * gram_second, frame_sum)
    gram_frames = jnp.dot(frames, frames.T, precision=lax.Precision.HIGHEST)
    full_part = accumulate_pass_t(tensor, frames, second_values)
    inverse = ridge_solve(gram_second * gram_frames, jnp.eye(components, dtype=jnp.float32))
    new_block_t = solve_and_gather_t(full_part, inverse.T, n, 1)
    gram_new_part = lax.dot_general(
        new_block_t, new_block_t, (((0,), (0,)), ((), ())), preferred_element_type=jnp.float32
    )
    second_part_t = second_pass(tensor, new_block_t, frames.T)
    summed_new = row_sum(jnp.concatenate([second_part_t, gram_new_part], axis=0), n, 4)
    second_sum = summed_new[:col_count].T
    gram_new = summed_new[col_count:]
    new_second = ridge_solve(gram_new * gram_frames, second_sum)
    full_next = accumulate_pass_t(tensor, frames, new_second)
    mode_one = col_reduce_scatter(full_next, n, 2)
    return (frames, mode_one)


def solution(mesh):
    return jax.shard_map(
        local,
        mesh=mesh,
        in_specs=(P(None, "col", "row"), P(None, ("row", "col")), P(None, "col")),
        out_specs=(P(), P(None, ("row", "col"))),
        check_vma=False,
    )
```

```python
import functools

import jax
import numpy as np
import jax.numpy as jnp
from jax import lax
from jax.experimental import pallas as pl
from jax.experimental.pallas import tpu as pltpu
from jax.sharding import PartitionSpec as P

ridge_weight = 0.05
MESH_ID = pl.DeviceIdType.MESH


def ridge_solve(gram, right_side):
    order_size = gram.shape[0]
    factor_low = jnp.linalg.cholesky(gram + ridge_weight * jnp.eye(order_size, dtype=jnp.float32))
    middle = lax.linalg.triangular_solve(factor_low, right_side, left_side=True, lower=True)
    return lax.linalg.triangular_solve(
        factor_low, middle, left_side=True, lower=True, transpose_a=True
    )


def gram_of(factor):
    return jnp.dot(factor, factor.T, preferred_element_type=jnp.float32)


STREAM_FRAMES = 32


def _frame_kernel(block_t_ref, second_t_ref, slab_ref, out_ref):
    frames, width, rows = slab_ref.shape
    projected = jnp.dot(
        slab_ref[...].reshape(frames * width, rows), block_t_ref[...],
        preferred_element_type=jnp.float32,
    ).reshape(frames, width, block_t_ref.shape[1])
    out_ref[...] = jnp.sum(projected * second_t_ref[...][None], axis=1)


def _second_kernel(block_t_ref, frames_t_ref, slab_ref, out_ref):
    frames, width, rows = slab_ref.shape

    @pl.when(pl.program_id(0) == 0)
    def _():
        out_ref[...] = jnp.zeros_like(out_ref)

    projected = jnp.dot(
        slab_ref[...].reshape(frames * width, rows), block_t_ref[...],
        preferred_element_type=jnp.float32,
    ).reshape(frames, width, block_t_ref.shape[1])
    out_ref[...] += jnp.sum(projected * frames_t_ref[...][:, None, :], axis=0)


def _slab_spec(width, rows):
    return pl.BlockSpec((STREAM_FRAMES, width, rows), lambda s: (s, 0, 0))


def _whole(shape):
    return pl.BlockSpec(shape, lambda s: (0,) * len(shape))


def frame_pass(tensor, block_t, second_t):
    frame_count, width, rows = tensor.shape
    components = block_t.shape[1]
    return pl.pallas_call(
        _frame_kernel,
        grid=(frame_count // STREAM_FRAMES,),
        in_specs=[_whole(block_t.shape), _whole(second_t.shape), _slab_spec(width, rows)],
        out_specs=pl.BlockSpec((STREAM_FRAMES, components), lambda s: (s, 0)),
        out_shape=jax.ShapeDtypeStruct((frame_count, components), jnp.float32),
        cost_estimate=pl.CostEstimate(
            flops=2 * components * frame_count * width * rows, transcendentals=0,
            bytes_accessed=2 * frame_count * width * rows,
        ),
    )(block_t, second_t, tensor)


def second_pass(tensor, block_t, frames_t):
    frame_count, width, rows = tensor.shape
    components = block_t.shape[1]
    return pl.pallas_call(
        _second_kernel,
        grid=(frame_count // STREAM_FRAMES,),
        in_specs=[
            _whole(block_t.shape),
            pl.BlockSpec((STREAM_FRAMES, components), lambda s: (s, 0)),
            _slab_spec(width, rows),
        ],
        out_specs=_whole((width, components)),
        out_shape=jax.ShapeDtypeStruct((width, components), jnp.float32),
        cost_estimate=pl.CostEstimate(
            flops=2 * components * frame_count * width * rows, transcendentals=0,
            bytes_accessed=2 * frame_count * width * rows,
        ),
    )(block_t, frames_t, tensor)


def _accumulate_kernel(frames_ref, second_ref, tile_ref, slab_ref, out_ref, total_ref):
    frames, width, rows = slab_ref.shape
    step = pl.program_id(0)

    @pl.when(step == 0)
    def _():
        total_ref[...] = jnp.zeros_like(total_ref)

    frame_count = frames_ref.shape[1]
    span = frames * width
    which = lax.broadcasted_iota(jnp.int32, (frame_count, span), 0) - step * frames
    column = lax.broadcasted_iota(jnp.int32, (frame_count, span), 1)
    expand = ((column >= which * width) & (column < which * width + width)).astype(jnp.bfloat16)
    def spread(values, selector):
        rest = values
        repeated = jnp.zeros((values.shape[0], span), jnp.float32)
        for _ in range(3):
            piece = rest.astype(jnp.bfloat16)
            rest = rest - piece.astype(jnp.float32)
            repeated = repeated + jnp.dot(piece, selector, preferred_element_type=jnp.float32)
        return repeated

    weights = (spread(frames_ref[...], expand) * spread(second_ref[...], tile_ref[...])).astype(
        jnp.bfloat16
    )
    total_ref[...] += jnp.dot(
        weights, slab_ref[...].reshape(span, rows), preferred_element_type=jnp.float32
    )

    @pl.when(step == pl.num_programs(0) - 1)
    def _():
        out_ref[...] = total_ref[...].T


def accumulate_pass_t(tensor, frames, second):
    frame_count, width, rows = tensor.shape
    components = frames.shape[0]
    tiler = jnp.asarray(np.tile(np.eye(width, dtype=np.float32), (1, STREAM_FRAMES)), jnp.bfloat16)
    return pl.pallas_call(
        _accumulate_kernel,
        grid=(frame_count // STREAM_FRAMES,),
        in_specs=[
            _whole(frames.shape), _whole(second.shape), _whole(tiler.shape),
            _slab_spec(width, rows),
        ],
        out_specs=_whole((rows, components)),
        out_shape=jax.ShapeDtypeStruct((rows, components), jnp.float32),
        scratch_shapes=[pltpu.VMEM((components, rows), jnp.float32)],
        cost_estimate=pl.CostEstimate(
            flops=2 * components * frame_count * width * rows, transcendentals=0,
            bytes_accessed=2 * frame_count * width * rows,
        ),
    )(frames, second, tiler, tensor)


def _split(n):
    inner = next(d for d in (8, 4, 2, 1) if n % d == 0 and d * d <= n)
    return inner, n // inner


def _exchange_kernel(n, rows, mode, *refs):
    if mode == "solve":
        send_ref, op_ref, out_ref = refs[:3]
        scratch = refs[3:]
    else:
        send_ref, out_ref = refs[:2]
        scratch = refs[2:]
    me = lax.axis_index("col")
    row = lax.axis_index("row")
    inner, outer = _split(n)
    low = lax.rem(me, inner)
    high = me // inner

    def in_low(peer):
        return (row, high * inner + peer)

    def in_high(peer):
        return (row, peer * inner + low)

    def in_row(peer):
        return (peer, me)

    def exchange(count, mine, device, source, landing, sends, recvs):
        def descriptor(peer, slot):
            return pltpu.make_async_remote_copy(
                src_ref=source(peer),
                dst_ref=landing.at[slot],
                send_sem=sends.at[peer],
                recv_sem=recvs.at[slot],
                device_id=device(peer),
                device_id_type=MESH_ID,
            )

        def start(t, carry):
            peer = lax.rem(mine + 1 + t, count)
            descriptor(peer, mine).start()
            return carry

        lax.fori_loop(0, count - 1, start, 0)

        def finish(t, carry):
            peer = lax.rem(mine + 1 + t, count)
            copy = descriptor(peer, peer)
            copy.wait_send()
            copy.wait_recv()
            return carry

        lax.fori_loop(0, count - 1, finish, 0)
        landing[mine] = source(mine)[...]

    if mode == "rowsum":
        groups = [(rows, row, in_row)]
    else:
        groups = [(inner, low, in_low), (outer, high, in_high)]
        if mode == "allreduce":
            groups.append((rows, row, in_row))
    barrier = pltpu.get_barrier_semaphore()
    for count, mine, device in groups:
        def greet(t, carry, count=count, mine=mine, device=device):
            peer = lax.rem(mine + 1 + t, count)
            pl.semaphore_signal(barrier, inc=1, device_id=device(peer), device_id_type=MESH_ID)
            return carry

        lax.fori_loop(0, count - 1, greet, 0)
    pl.semaphore_wait(barrier, sum(count - 1 for count, _, _ in groups))

    scratch = list(scratch)

    def take(k):
        taken = scratch[:k]
        del scratch[:k]
        return taken

    def gather(piece_ref):
        bundle, s1, r1 = take(3)
        exchange(inner, low, in_low, lambda peer: piece_ref, bundle, s1, r1)
        everything, s2, r2 = take(3)
        exchange(outer, high, in_high, lambda peer: bundle, everything, s2, r2)
        out_ref[...] = everything[...]

    if mode == "rowsum":
        landing, s1, r1 = take(3)
        exchange(rows, row, in_row, lambda peer: send_ref, landing, s1, r1)
        out_ref[...] = jnp.sum(landing[...], axis=0)
        return
    if mode == "gather":
        gather(send_ref)
        return
    landing, s1, r1, partial = take(4)
    exchange(outer, high, in_high, lambda peer: send_ref.at[peer], landing, s1, r1)
    partial[...] = jnp.sum(landing[...], axis=0)
    if mode == "scatter":
        landing2, s2, r2 = take(3)
        exchange(inner, low, in_low, lambda peer: partial.at[peer], landing2, s2, r2)
        out_ref[...] = jnp.sum(landing2[...], axis=0)
        return
    if mode == "solve":
        landing2, s2, r2, solved = take(4)
        exchange(inner, low, in_low, lambda peer: partial.at[peer], landing2, s2, r2)
        chunk = jnp.sum(landing2[...], axis=0)
        solved[...] = jnp.dot(
            chunk, op_ref[...], precision=lax.Precision.HIGHEST, preferred_element_type=jnp.float32
        ).astype(solved.dtype)
        gather(solved)
        return
    landing2, s2, r2, bundle = take(4)
    exchange(inner, low, in_low, lambda peer: partial, landing2, s2, r2)
    bundle[...] = jnp.sum(landing2[...], axis=0)
    row_landing, s3, r3, total = take(4)
    exchange(rows, row, in_row, lambda peer: bundle, row_landing, s3, r3)
    total[...] = jnp.sum(row_landing[...], axis=0)
    everything, s4, r4 = take(3)
    exchange(outer, high, in_high, lambda peer: total, everything, s4, r4)
    out_ref[...] = everything[...]


def col_exchange(send, n, mode, collective_id, op=None, out_dtype=None):
    rows = lax.axis_size("row")
    inner, outer = _split(n)
    dtype = send.dtype

    def stage(count, piece, kind=dtype):
        return [
            pltpu.VMEM((count,) + piece, kind),
            pltpu.SemaphoreType.DMA((count,)),
            pltpu.SemaphoreType.DMA((count,)),
        ]

    if mode == "rowsum":
        piece = tuple(send.shape)
        out_shape = piece
        scratch = stage(rows, piece)
    elif mode == "gather":
        piece = tuple(send.shape)
        out_shape = (outer, inner) + piece
        scratch = stage(inner, piece) + stage(outer, (inner,) + piece)
    else:
        piece = tuple(send.shape[2:])
        out_shape = piece if mode == "scatter" else (outer, inner) + piece
        bundle = (inner,) + piece
        scratch = stage(outer, bundle) + [pltpu.VMEM(bundle, dtype)]
        if mode == "scatter":
            scratch += stage(inner, piece)
        elif mode == "solve":
            out_shape = (outer, inner) + piece
            scratch += stage(inner, piece) + [pltpu.VMEM(piece, out_dtype)]
            scratch += stage(inner, piece, out_dtype) + stage(outer, (inner,) + piece, out_dtype)
        else:
            scratch += stage(inner, bundle) + [pltpu.VMEM(bundle, dtype)]
            scratch += stage(rows, bundle) + [pltpu.VMEM(bundle, dtype)]
            scratch += stage(outer, bundle)
    operands = (send,) if op is None else (send, op)
    return pl.pallas_call(
        functools.partial(_exchange_kernel, n, rows, mode),
        out_shape=jax.ShapeDtypeStruct(out_shape, out_dtype or dtype),
        in_specs=[pl.BlockSpec(memory_space=pltpu.VMEM)] * len(operands),
        out_specs=pl.BlockSpec(memory_space=pltpu.VMEM),
        scratch_shapes=scratch,
        compiler_params=pltpu.CompilerParams(collective_id=collective_id, has_side_effects=True),
    )(*operands)


def _chunk_order(chunks, n):
    inner, outer = _split(n)
    return chunks.reshape((outer, inner) + chunks.shape[1:])


def _col_order(gathered, n):
    return gathered.reshape((n,) + gathered.shape[2:])


def col_gather_t(piece_t, n):
    gathered = _col_order(col_exchange(piece_t, n, "gather", 0), n)
    return gathered.reshape(n * piece_t.shape[0], piece_t.shape[1])


def col_reduce_scatter(full_t, n, collective_id):
    width = full_t.shape[0] // n
    chunks = _chunk_order(full_t.reshape(n, width, full_t.shape[1]), n)
    return col_exchange(chunks, n, "scatter", collective_id).T


def all_reduce(full, n, collective_id):
    width = full.shape[1] // n
    chunks = _chunk_order(full.T.reshape(n, width, full.shape[0]), n)
    summed_t = _col_order(col_exchange(chunks, n, "allreduce", collective_id), n)
    return summed_t.reshape(n * width, full.shape[0]).T


def solve_and_gather_t(full_t, operator_t, n, collective_id):
    width = full_t.shape[0] // n
    chunks = _chunk_order(full_t.reshape(n, width, full_t.shape[1]), n)
    gathered = col_exchange(
        chunks, n, "solve", collective_id, op=operator_t, out_dtype=jnp.bfloat16
    )
    return gathered.reshape(n * width, full_t.shape[1])


def row_sum(piece, n, collective_id):
    return col_exchange(piece, n, "rowsum", collective_id)


def local(tensor, first_factor, second_factor):
    frame_count, col_count, row_count = tensor.shape
    components = first_factor.shape[0]
    n = lax.axis_size("col")
    second_values = second_factor.astype(jnp.float32)
    gram_first_part = gram_of(first_factor)
    gram_second_part = gram_of(second_factor)
    block_t = col_gather_t(first_factor.T, n)
    frame_part = frame_pass(tensor, block_t, second_values.T).T
    scaled_second = gram_second_part * (1.0 / lax.axis_size("row"))
    summed = all_reduce(jnp.concatenate([frame_part, gram_first_part, scaled_second], axis=1), n, 3)
    frame_sum = summed[:, :frame_count]
    gram_first = summed[:, frame_count:frame_count + components]
    gram_second = summed[:, frame_count + components:]
    frames = ridge_solve(gram_first * gram_second, frame_sum)
    gram_frames = jnp.dot(frames, frames.T, precision=lax.Precision.HIGHEST)
    full_part = accumulate_pass_t(tensor, frames, second_values)
    inverse = ridge_solve(gram_second * gram_frames, jnp.eye(components, dtype=jnp.float32))
    new_block_t = solve_and_gather_t(full_part, inverse.T, n, 1)
    gram_new_part = lax.dot_general(
        new_block_t, new_block_t, (((0,), (0,)), ((), ())), preferred_element_type=jnp.float32
    )
    second_part_t = second_pass(tensor, new_block_t, frames.T)
    summed_new = row_sum(jnp.concatenate([second_part_t, gram_new_part], axis=0), n, 4)
    second_sum = summed_new[:col_count].T
    gram_new = summed_new[col_count:]
    new_second = ridge_solve(gram_new * gram_frames, second_sum)
    full_next = accumulate_pass_t(tensor, frames, new_second)
    mode_one = col_reduce_scatter(full_next, n, 2)
    return (frames, mode_one)


def solution(mesh):
    return jax.shard_map(
        local,
        mesh=mesh,
        in_specs=(P(None, "col", "row"), P(None, ("row", "col")), P(None, "col")),
        out_specs=(P(), P(None, ("row", "col"))),
        check_vma=False,
    )
```

```python
import functools

import jax
import jax.numpy as jnp
from jax import lax
from jax.experimental import pallas as pl
from jax.experimental.pallas import tpu as pltpu
from jax.sharding import PartitionSpec as P

ridge_weight = 0.05
MESH_ID = pl.DeviceIdType.MESH


def ridge_solve(gram, right_side):
    order_size = gram.shape[0]
    factor_low = jnp.linalg.cholesky(gram + ridge_weight * jnp.eye(order_size, dtype=jnp.float32))
    middle = lax.linalg.triangular_solve(factor_low, right_side, left_side=True, lower=True)
    return lax.linalg.triangular_solve(
        factor_low, middle, left_side=True, lower=True, transpose_a=True
    )


def gram_of(factor):
    return jnp.dot(factor, factor.T, preferred_element_type=jnp.float32)


STREAM_FRAMES = 32
PROJECT_FRAMES = 64


def _frame_kernel(block_t_ref, second_t_ref, slab_ref, out_ref):
    frames, width, rows = slab_ref.shape
    projected = jnp.dot(
        slab_ref[...].reshape(frames * width, rows), block_t_ref[...],
        preferred_element_type=jnp.float32,
    ).reshape(frames, width, block_t_ref.shape[1])
    out_ref[...] = jnp.sum(projected * second_t_ref[...][None], axis=1)


def _second_kernel(block_t_ref, frames_t_ref, slab_ref, out_ref):
    frames, width, rows = slab_ref.shape

    @pl.when(pl.program_id(0) == 0)
    def _():
        out_ref[...] = jnp.zeros_like(out_ref)

    projected = jnp.dot(
        slab_ref[...].reshape(frames * width, rows), block_t_ref[...],
        preferred_element_type=jnp.float32,
    ).reshape(frames, width, block_t_ref.shape[1])
    out_ref[...] += jnp.sum(projected * frames_t_ref[...][:, None, :], axis=0)


def _slab_spec(width, rows, frames=STREAM_FRAMES):
    return pl.BlockSpec((frames, width, rows), lambda s: (s, 0, 0))


def _whole(shape):
    return pl.BlockSpec(shape, lambda s: (0,) * len(shape))


def frame_pass(tensor, block_t, second_t):
    frame_count, width, rows = tensor.shape
    components = block_t.shape[1]
    return pl.pallas_call(
        _frame_kernel,
        grid=(frame_count // PROJECT_FRAMES,),
        in_specs=[
            _whole(block_t.shape), _whole(second_t.shape), _slab_spec(width, rows, PROJECT_FRAMES)
        ],
        out_specs=pl.BlockSpec((PROJECT_FRAMES, components), lambda s: (s, 0)),
        out_shape=jax.ShapeDtypeStruct((frame_count, components), jnp.float32),
        cost_estimate=pl.CostEstimate(
            flops=2 * components * frame_count * width * rows, transcendentals=0,
            bytes_accessed=2 * frame_count * width * rows,
        ),
    )(block_t, second_t, tensor)


def second_pass(tensor, block_t, frames_t):
    frame_count, width, rows = tensor.shape
    components = block_t.shape[1]
    return pl.pallas_call(
        _second_kernel,
        grid=(frame_count // PROJECT_FRAMES,),
        in_specs=[
            _whole(block_t.shape),
            pl.BlockSpec((PROJECT_FRAMES, components), lambda s: (s, 0)),
            _slab_spec(width, rows, PROJECT_FRAMES),
        ],
        out_specs=_whole((width, components)),
        out_shape=jax.ShapeDtypeStruct((width, components), jnp.float32),
        cost_estimate=pl.CostEstimate(
            flops=2 * components * frame_count * width * rows, transcendentals=0,
            bytes_accessed=2 * frame_count * width * rows,
        ),
    )(block_t, frames_t, tensor)


def _accumulate_kernel(frames_ref, tiled_ref, slab_ref, out_ref, total_ref):
    frames, width, rows = slab_ref.shape
    step = pl.program_id(0)

    @pl.when(step == 0)
    def _():
        total_ref[...] = jnp.zeros_like(total_ref)

    frame_count = frames_ref.shape[1]
    span = frames * width
    which = lax.broadcasted_iota(jnp.int32, (frame_count, span), 0) - step * frames
    column = lax.broadcasted_iota(jnp.int32, (frame_count, span), 1)
    expand = ((column >= which * width) & (column < which * width + width)).astype(jnp.bfloat16)
    rest = frames_ref[...]
    repeated = jnp.zeros((frames_ref.shape[0], span), jnp.float32)
    for _ in range(3):
        piece = rest.astype(jnp.bfloat16)
        rest = rest - piece.astype(jnp.float32)
        repeated = repeated + jnp.dot(piece, expand, preferred_element_type=jnp.float32)
    weights = (repeated * tiled_ref[...]).astype(jnp.bfloat16)
    total_ref[...] += jnp.dot(
        weights, slab_ref[...].reshape(span, rows), preferred_element_type=jnp.float32
    )

    @pl.when(step == pl.num_programs(0) - 1)
    def _():
        out_ref[...] = total_ref[...].T


def accumulate_pass_t(tensor, frames, second):
    frame_count, width, rows = tensor.shape
    components = frames.shape[0]
    tiled = jnp.tile(second, (1, STREAM_FRAMES))
    return pl.pallas_call(
        _accumulate_kernel,
        grid=(frame_count // STREAM_FRAMES,),
        in_specs=[_whole(frames.shape), _whole(tiled.shape), _slab_spec(width, rows)],
        out_specs=_whole((rows, components)),
        out_shape=jax.ShapeDtypeStruct((rows, components), jnp.float32),
        scratch_shapes=[pltpu.VMEM((components, rows), jnp.float32)],
        cost_estimate=pl.CostEstimate(
            flops=2 * components * frame_count * width * rows, transcendentals=0,
            bytes_accessed=2 * frame_count * width * rows,
        ),
    )(frames, tiled, tensor)


def _split(n):
    inner = next(d for d in (8, 4, 2, 1) if n % d == 0 and d * d <= n)
    return inner, n // inner


def _exchange_kernel(n, rows, mode, *refs):
    if mode == "solve":
        send_ref, op_ref, out_ref = refs[:3]
        scratch = refs[3:]
    else:
        send_ref, out_ref = refs[:2]
        scratch = refs[2:]
    me = lax.axis_index("col")
    row = lax.axis_index("row")
    inner, outer = _split(n)
    low = lax.rem(me, inner)
    high = me // inner

    def in_low(peer):
        return (row, high * inner + peer)

    def in_high(peer):
        return (row, peer * inner + low)

    def in_row(peer):
        return (peer, me)

    def exchange(count, mine, device, source, landing, sends, recvs):
        def descriptor(peer, slot):
            return pltpu.make_async_remote_copy(
                src_ref=source(peer),
                dst_ref=landing.at[slot],
                send_sem=sends.at[peer],
                recv_sem=recvs.at[slot],
                device_id=device(peer),
                device_id_type=MESH_ID,
            )

        def start(t, carry):
            peer = lax.rem(mine + 1 + t, count)
            descriptor(peer, mine).start()
            return carry

        lax.fori_loop(0, count - 1, start, 0)

        def finish(t, carry):
            peer = lax.rem(mine + 1 + t, count)
            copy = descriptor(peer, peer)
            copy.wait_send()
            copy.wait_recv()
            return carry

        lax.fori_loop(0, count - 1, finish, 0)
        landing[mine] = source(mine)[...]

    if mode == "rowsum":
        groups = [(rows, row, in_row)]
    else:
        groups = [(inner, low, in_low), (outer, high, in_high)]
        if mode == "allreduce":
            groups.append((rows, row, in_row))
    barrier = pltpu.get_barrier_semaphore()
    for count, mine, device in groups:
        def greet(t, carry, count=count, mine=mine, device=device):
            peer = lax.rem(mine + 1 + t, count)
            pl.semaphore_signal(barrier, inc=1, device_id=device(peer), device_id_type=MESH_ID)
            return carry

        lax.fori_loop(0, count - 1, greet, 0)
    pl.semaphore_wait(barrier, sum(count - 1 for count, _, _ in groups))

    scratch = list(scratch)

    def take(k):
        taken = scratch[:k]
        del scratch[:k]
        return taken

    def gather(piece_ref):
        bundle, s1, r1 = take(3)
        exchange(inner, low, in_low, lambda peer: piece_ref, bundle, s1, r1)
        everything, s2, r2 = take(3)
        exchange(outer, high, in_high, lambda peer: bundle, everything, s2, r2)
        out_ref[...] = everything[...]

    if mode == "rowsum":
        landing, s1, r1 = take(3)
        exchange(rows, row, in_row, lambda peer: send_ref, landing, s1, r1)
        out_ref[...] = jnp.sum(landing[...], axis=0)
        return
    if mode == "gather":
        gather(send_ref)
        return
    landing, s1, r1, partial = take(4)
    exchange(outer, high, in_high, lambda peer: send_ref.at[peer], landing, s1, r1)
    partial[...] = jnp.sum(landing[...], axis=0)
    if mode == "scatter":
        landing2, s2, r2 = take(3)
        exchange(inner, low, in_low, lambda peer: partial.at[peer], landing2, s2, r2)
        out_ref[...] = jnp.sum(landing2[...], axis=0)
        return
    if mode == "solve":
        landing2, s2, r2, solved = take(4)
        exchange(inner, low, in_low, lambda peer: partial.at[peer], landing2, s2, r2)
        chunk = jnp.sum(landing2[...], axis=0)
        solved[...] = jnp.dot(
            chunk, op_ref[...], precision=lax.Precision.HIGHEST, preferred_element_type=jnp.float32
        ).astype(solved.dtype)
        gather(solved)
        return
    landing2, s2, r2, bundle = take(4)
    exchange(inner, low, in_low, lambda peer: partial, landing2, s2, r2)
    bundle[...] = jnp.sum(landing2[...], axis=0)
    row_landing, s3, r3, total = take(4)
    exchange(rows, row, in_row, lambda peer: bundle, row_landing, s3, r3)
    total[...] = jnp.sum(row_landing[...], axis=0)
    everything, s4, r4 = take(3)
    exchange(outer, high, in_high, lambda peer: total, everything, s4, r4)
    out_ref[...] = everything[...]


def col_exchange(send, n, mode, collective_id, op=None, out_dtype=None):
    rows = lax.axis_size("row")
    inner, outer = _split(n)
    dtype = send.dtype

    def stage(count, piece, kind=dtype):
        return [
            pltpu.VMEM((count,) + piece, kind),
            pltpu.SemaphoreType.DMA((count,)),
            pltpu.SemaphoreType.DMA((count,)),
        ]

    if mode == "rowsum":
        piece = tuple(send.shape)
        out_shape = piece
        scratch = stage(rows, piece)
    elif mode == "gather":
        piece = tuple(send.shape)
        out_shape = (outer, inner) + piece
        scratch = stage(inner, piece) + stage(outer, (inner,) + piece)
    else:
        piece = tuple(send.shape[2:])
        out_shape = piece if mode == "scatter" else (outer, inner) + piece
        bundle = (inner,) + piece
        scratch = stage(outer, bundle) + [pltpu.VMEM(bundle, dtype)]
        if mode == "scatter":
            scratch += stage(inner, piece)
        elif mode == "solve":
            out_shape = (outer, inner) + piece
            scratch += stage(inner, piece) + [pltpu.VMEM(piece, out_dtype)]
            scratch += stage(inner, piece, out_dtype) + stage(outer, (inner,) + piece, out_dtype)
        else:
            scratch += stage(inner, bundle) + [pltpu.VMEM(bundle, dtype)]
            scratch += stage(rows, bundle) + [pltpu.VMEM(bundle, dtype)]
            scratch += stage(outer, bundle)
    operands = (send,) if op is None else (send, op)
    return pl.pallas_call(
        functools.partial(_exchange_kernel, n, rows, mode),
        out_shape=jax.ShapeDtypeStruct(out_shape, out_dtype or dtype),
        in_specs=[pl.BlockSpec(memory_space=pltpu.VMEM)] * len(operands),
        out_specs=pl.BlockSpec(memory_space=pltpu.VMEM),
        scratch_shapes=scratch,
        compiler_params=pltpu.CompilerParams(collective_id=collective_id, has_side_effects=True),
    )(*operands)


def _chunk_order(chunks, n):
    inner, outer = _split(n)
    return chunks.reshape((outer, inner) + chunks.shape[1:])


def _col_order(gathered, n):
    return gathered.reshape((n,) + gathered.shape[2:])


def col_gather_t(piece_t, n):
    gathered = _col_order(col_exchange(piece_t, n, "gather", 0), n)
    return gathered.reshape(n * piece_t.shape[0], piece_t.shape[1])


def col_reduce_scatter(full_t, n, collective_id):
    width = full_t.shape[0] // n
    chunks = _chunk_order(full_t.reshape(n, width, full_t.shape[1]), n)
    return col_exchange(chunks, n, "scatter", collective_id).T


def all_reduce(full, n, collective_id):
    width = full.shape[1] // n
    chunks = _chunk_order(full.T.reshape(n, width, full.shape[0]), n)
    summed_t = _col_order(col_exchange(chunks, n, "allreduce", collective_id), n)
    return summed_t.reshape(n * width, full.shape[0]).T


def solve_and_gather_t(full_t, operator_t, n, collective_id):
    width = full_t.shape[0] // n
    chunks = _chunk_order(full_t.reshape(n, width, full_t.shape[1]), n)
    gathered = col_exchange(
        chunks, n, "solve", collective_id, op=operator_t, out_dtype=jnp.bfloat16
    )
    return gathered.reshape(n * width, full_t.shape[1])


def row_sum(piece, n, collective_id):
    return col_exchange(piece, n, "rowsum", collective_id)


def local(tensor, first_factor, second_factor):
    frame_count, col_count, row_count = tensor.shape
    components = first_factor.shape[0]
    n = lax.axis_size("col")
    second_values = second_factor.astype(jnp.float32)
    gram_first_part = gram_of(first_factor)
    gram_second_part = gram_of(second_factor)
    block_t = col_gather_t(first_factor.T, n)
    frame_part = frame_pass(tensor, block_t, second_values.T).T
    scaled_second = gram_second_part * (1.0 / lax.axis_size("row"))
    summed = all_reduce(jnp.concatenate([frame_part, gram_first_part, scaled_second], axis=1), n, 3)
    frame_sum = summed[:, :frame_count]
    gram_first = summed[:, frame_count:frame_count + components]
    gram_second = summed[:, frame_count + components:]
    frames = ridge_solve(gram_first * gram_second, frame_sum)
    gram_frames = jnp.dot(frames, frames.T, precision=lax.Precision.HIGHEST)
    full_part = accumulate_pass_t(tensor, frames, second_values)
    inverse = ridge_solve(gram_second * gram_frames, jnp.eye(components, dtype=jnp.float32))
    new_block_t = solve_and_gather_t(full_part, inverse.T, n, 1)
    gram_new_part = lax.dot_general(
        new_block_t, new_block_t, (((0,), (0,)), ((), ())), preferred_element_type=jnp.float32
    )
    second_part_t = second_pass(tensor, new_block_t, frames.T)
    summed_new = row_sum(jnp.concatenate([second_part_t, gram_new_part], axis=0), n, 4)
    second_sum = summed_new[:col_count].T
    gram_new = summed_new[col_count:]
    new_second = ridge_solve(gram_new * gram_frames, second_sum)
    full_next = accumulate_pass_t(tensor, frames, new_second)
    mode_one = col_reduce_scatter(full_next, n, 2)
    return (frames, mode_one)


def solution(mesh):
    return jax.shard_map(
        local,
        mesh=mesh,
        in_specs=(P(None, "col", "row"), P(None, ("row", "col")), P(None, "col")),
        out_specs=(P(), P(None, ("row", "col"))),
        check_vma=False,
    )
```

```python
import functools

import jax
import jax.numpy as jnp
from jax import lax
from jax.experimental import pallas as pl
from jax.experimental.pallas import tpu as pltpu
from jax.sharding import PartitionSpec as P

ridge_weight = 0.05
MESH_ID = pl.DeviceIdType.MESH


def ridge_solve(gram, right_side):
    order_size = gram.shape[0]
    factor_low = jnp.linalg.cholesky(gram + ridge_weight * jnp.eye(order_size, dtype=jnp.float32))
    middle = lax.linalg.triangular_solve(factor_low, right_side, left_side=True, lower=True)
    return lax.linalg.triangular_solve(
        factor_low, middle, left_side=True, lower=True, transpose_a=True
    )


def gram_of(factor):
    return jnp.dot(factor, factor.T, preferred_element_type=jnp.float32)


STREAM_FRAMES = 32
PROJECT_FRAMES = 64


def _frame_kernel(block_t_ref, second_t_ref, slab_ref, out_ref):
    frames, width, rows = slab_ref.shape
    projected = jnp.dot(
        slab_ref[...].reshape(frames * width, rows), block_t_ref[...],
        preferred_element_type=jnp.float32,
    ).reshape(frames, width, block_t_ref.shape[1])
    out_ref[...] = jnp.sum(projected * second_t_ref[...][None], axis=1)


def _second_kernel(block_t_ref, frames_ref, slab_ref, out_ref, frames_t_ref):
    frames, width, rows = slab_ref.shape
    step = pl.program_id(0)

    @pl.when(step == 0)
    def _():
        out_ref[...] = jnp.zeros_like(out_ref)
        frames_t_ref[...] = frames_ref[...].T

    projected = jnp.dot(
        slab_ref[...].reshape(frames * width, rows), block_t_ref[...],
        preferred_element_type=jnp.float32,
    ).reshape(frames, width, block_t_ref.shape[1])
    block_frames = frames_t_ref[pl.ds(pl.multiple_of(step * frames, frames), frames), :]
    out_ref[...] += jnp.sum(projected * block_frames[:, None, :], axis=0)


def _slab_spec(width, rows, frames=STREAM_FRAMES):
    return pl.BlockSpec((frames, width, rows), lambda s: (s, 0, 0))


def _whole(shape):
    return pl.BlockSpec(shape, lambda s: (0,) * len(shape))


def frame_pass(tensor, block_t, second_t):
    frame_count, width, rows = tensor.shape
    components = block_t.shape[1]
    return pl.pallas_call(
        _frame_kernel,
        grid=(frame_count // PROJECT_FRAMES,),
        in_specs=[
            _whole(block_t.shape), _whole(second_t.shape), _slab_spec(width, rows, PROJECT_FRAMES)
        ],
        out_specs=pl.BlockSpec((PROJECT_FRAMES, components), lambda s: (s, 0)),
        out_shape=jax.ShapeDtypeStruct((frame_count, components), jnp.float32),
        cost_estimate=pl.CostEstimate(
            flops=2 * components * frame_count * width * rows, transcendentals=0,
            bytes_accessed=2 * frame_count * width * rows,
        ),
    )(block_t, second_t, tensor)


def second_pass(tensor, block_t, frames):
    frame_count, width, rows = tensor.shape
    components = block_t.shape[1]
    return pl.pallas_call(
        _second_kernel,
        grid=(frame_count // PROJECT_FRAMES,),
        in_specs=[
            _whole(block_t.shape),
            _whole(frames.shape),
            _slab_spec(width, rows, PROJECT_FRAMES),
        ],
        out_specs=_whole((width, components)),
        out_shape=jax.ShapeDtypeStruct((width, components), jnp.float32),
        scratch_shapes=[pltpu.VMEM((frame_count, components), jnp.float32)],
        cost_estimate=pl.CostEstimate(
            flops=2 * components * frame_count * width * rows, transcendentals=0,
            bytes_accessed=2 * frame_count * width * rows,
        ),
    )(block_t, frames, tensor)


def _accumulate_kernel(frames_ref, tiled_ref, slab_ref, out_ref, total_ref):
    frames, width, rows = slab_ref.shape
    step = pl.program_id(0)

    @pl.when(step == 0)
    def _():
        total_ref[...] = jnp.zeros_like(total_ref)

    frame_count = frames_ref.shape[1]
    span = frames * width
    which = lax.broadcasted_iota(jnp.int32, (frame_count, span), 0) - step * frames
    column = lax.broadcasted_iota(jnp.int32, (frame_count, span), 1)
    expand = ((column >= which * width) & (column < which * width + width)).astype(jnp.bfloat16)
    rest = frames_ref[...]
    repeated = jnp.zeros((frames_ref.shape[0], span), jnp.float32)
    for _ in range(3):
        piece = rest.astype(jnp.bfloat16)
        rest = rest - piece.astype(jnp.float32)
        repeated = repeated + jnp.dot(piece, expand, preferred_element_type=jnp.float32)
    weights = (repeated * tiled_ref[...]).astype(jnp.bfloat16)
    total_ref[...] += jnp.dot(
        weights, slab_ref[...].reshape(span, rows), preferred_element_type=jnp.float32
    )

    @pl.when(step == pl.num_programs(0) - 1)
    def _():
        out_ref[...] = total_ref[...].T


def accumulate_pass_t(tensor, frames, second):
    frame_count, width, rows = tensor.shape
    components = frames.shape[0]
    tiled = jnp.tile(second, (1, STREAM_FRAMES))
    return pl.pallas_call(
        _accumulate_kernel,
        grid=(frame_count // STREAM_FRAMES,),
        in_specs=[_whole(frames.shape), _whole(tiled.shape), _slab_spec(width, rows)],
        out_specs=_whole((rows, components)),
        out_shape=jax.ShapeDtypeStruct((rows, components), jnp.float32),
        scratch_shapes=[pltpu.VMEM((components, rows), jnp.float32)],
        cost_estimate=pl.CostEstimate(
            flops=2 * components * frame_count * width * rows, transcendentals=0,
            bytes_accessed=2 * frame_count * width * rows,
        ),
    )(frames, tiled, tensor)


def _split(n):
    inner = next(d for d in (8, 4, 2, 1) if n % d == 0 and d * d <= n)
    return inner, n // inner


def _exchange_kernel(n, rows, mode, *refs):
    if mode == "solve":
        send_ref, op_ref, out_ref = refs[:3]
        scratch = refs[3:]
    else:
        send_ref, out_ref = refs[:2]
        scratch = refs[2:]
    me = lax.axis_index("col")
    row = lax.axis_index("row")
    inner, outer = _split(n)
    low = lax.rem(me, inner)
    high = me // inner

    def in_low(peer):
        return (row, high * inner + peer)

    def in_high(peer):
        return (row, peer * inner + low)

    def in_row(peer):
        return (peer, me)

    def exchange(count, mine, device, source, landing, sends, recvs):
        def descriptor(peer, slot):
            return pltpu.make_async_remote_copy(
                src_ref=source(peer),
                dst_ref=landing.at[slot],
                send_sem=sends.at[peer],
                recv_sem=recvs.at[slot],
                device_id=device(peer),
                device_id_type=MESH_ID,
            )

        def start(t, carry):
            peer = lax.rem(mine + 1 + t, count)
            descriptor(peer, mine).start()
            return carry

        lax.fori_loop(0, count - 1, start, 0)

        def finish(t, carry):
            peer = lax.rem(mine + 1 + t, count)
            copy = descriptor(peer, peer)
            copy.wait_send()
            copy.wait_recv()
            return carry

        lax.fori_loop(0, count - 1, finish, 0)
        landing[mine] = source(mine)[...]

    if mode == "rowsum":
        groups = [(rows, row, in_row)]
    else:
        groups = [(inner, low, in_low), (outer, high, in_high)]
        if mode == "allreduce":
            groups.append((rows, row, in_row))
    barrier = pltpu.get_barrier_semaphore()
    for count, mine, device in groups:
        def greet(t, carry, count=count, mine=mine, device=device):
            peer = lax.rem(mine + 1 + t, count)
            pl.semaphore_signal(barrier, inc=1, device_id=device(peer), device_id_type=MESH_ID)
            return carry

        lax.fori_loop(0, count - 1, greet, 0)
    pl.semaphore_wait(barrier, sum(count - 1 for count, _, _ in groups))

    scratch = list(scratch)

    def take(k):
        taken = scratch[:k]
        del scratch[:k]
        return taken

    def gather(piece_ref):
        bundle, s1, r1 = take(3)
        exchange(inner, low, in_low, lambda peer: piece_ref, bundle, s1, r1)
        everything, s2, r2 = take(3)
        exchange(outer, high, in_high, lambda peer: bundle, everything, s2, r2)
        out_ref[...] = everything[...]

    if mode == "rowsum":
        landing, s1, r1 = take(3)
        exchange(rows, row, in_row, lambda peer: send_ref, landing, s1, r1)
        out_ref[...] = jnp.sum(landing[...], axis=0)
        return
    if mode == "gather":
        gather(send_ref)
        return
    landing, s1, r1, partial = take(4)
    exchange(outer, high, in_high, lambda peer: send_ref.at[peer], landing, s1, r1)
    partial[...] = jnp.sum(landing[...], axis=0)
    if mode == "scatter":
        landing2, s2, r2 = take(3)
        exchange(inner, low, in_low, lambda peer: partial.at[peer], landing2, s2, r2)
        out_ref[...] = jnp.sum(landing2[...], axis=0)
        return
    if mode == "solve":
        landing2, s2, r2, solved = take(4)
        exchange(inner, low, in_low, lambda peer: partial.at[peer], landing2, s2, r2)
        chunk = jnp.sum(landing2[...], axis=0)
        solved[...] = jnp.dot(
            chunk, op_ref[...], precision=lax.Precision.HIGHEST, preferred_element_type=jnp.float32
        ).astype(solved.dtype)
        gather(solved)
        return
    landing2, s2, r2, bundle = take(4)
    exchange(inner, low, in_low, lambda peer: partial, landing2, s2, r2)
    bundle[...] = jnp.sum(landing2[...], axis=0)
    row_landing, s3, r3, total = take(4)
    exchange(rows, row, in_row, lambda peer: bundle, row_landing, s3, r3)
    total[...] = jnp.sum(row_landing[...], axis=0)
    everything, s4, r4 = take(3)
    exchange(outer, high, in_high, lambda peer: total, everything, s4, r4)
    out_ref[...] = everything[...]


def col_exchange(send, n, mode, collective_id, op=None, out_dtype=None):
    rows = lax.axis_size("row")
    inner, outer = _split(n)
    dtype = send.dtype

    def stage(count, piece, kind=dtype):
        return [
            pltpu.VMEM((count,) + piece, kind),
            pltpu.SemaphoreType.DMA((count,)),
            pltpu.SemaphoreType.DMA((count,)),
        ]

    if mode == "rowsum":
        piece = tuple(send.shape)
        out_shape = piece
        scratch = stage(rows, piece)
    elif mode == "gather":
        piece = tuple(send.shape)
        out_shape = (outer, inner) + piece
        scratch = stage(inner, piece) + stage(outer, (inner,) + piece)
    else:
        piece = tuple(send.shape[2:])
        out_shape = piece if mode == "scatter" else (outer, inner) + piece
        bundle = (inner,) + piece
        scratch = stage(outer, bundle) + [pltpu.VMEM(bundle, dtype)]
        if mode == "scatter":
            scratch += stage(inner, piece)
        elif mode == "solve":
            out_shape = (outer, inner) + piece
            scratch += stage(inner, piece) + [pltpu.VMEM(piece, out_dtype)]
            scratch += stage(inner, piece, out_dtype) + stage(outer, (inner,) + piece, out_dtype)
        else:
            scratch += stage(inner, bundle) + [pltpu.VMEM(bundle, dtype)]
            scratch += stage(rows, bundle) + [pltpu.VMEM(bundle, dtype)]
            scratch += stage(outer, bundle)
    operands = (send,) if op is None else (send, op)
    return pl.pallas_call(
        functools.partial(_exchange_kernel, n, rows, mode),
        out_shape=jax.ShapeDtypeStruct(out_shape, out_dtype or dtype),
        in_specs=[pl.BlockSpec(memory_space=pltpu.VMEM)] * len(operands),
        out_specs=pl.BlockSpec(memory_space=pltpu.VMEM),
        scratch_shapes=scratch,
        compiler_params=pltpu.CompilerParams(collective_id=collective_id, has_side_effects=True),
    )(*operands)


def _chunk_order(chunks, n):
    inner, outer = _split(n)
    return chunks.reshape((outer, inner) + chunks.shape[1:])


def _col_order(gathered, n):
    return gathered.reshape((n,) + gathered.shape[2:])


def col_gather_t(piece_t, n):
    gathered = _col_order(col_exchange(piece_t, n, "gather", 0), n)
    return gathered.reshape(n * piece_t.shape[0], piece_t.shape[1])


def col_reduce_scatter(full_t, n, collective_id):
    width = full_t.shape[0] // n
    chunks = _chunk_order(full_t.reshape(n, width, full_t.shape[1]), n)
    return col_exchange(chunks, n, "scatter", collective_id).T


def all_reduce(full, n, collective_id):
    width = full.shape[1] // n
    chunks = _chunk_order(full.T.reshape(n, width, full.shape[0]), n)
    summed_t = _col_order(col_exchange(chunks, n, "allreduce", collective_id), n)
    return summed_t.reshape(n * width, full.shape[0]).T


def solve_and_gather_t(full_t, operator_t, n, collective_id):
    width = full_t.shape[0] // n
    chunks = _chunk_order(full_t.reshape(n, width, full_t.shape[1]), n)
    gathered = col_exchange(
        chunks, n, "solve", collective_id, op=operator_t, out_dtype=jnp.bfloat16
    )
    return gathered.reshape(n * width, full_t.shape[1])


def row_sum(piece, n, collective_id):
    return col_exchange(piece, n, "rowsum", collective_id)


def local(tensor, first_factor, second_factor):
    frame_count, col_count, row_count = tensor.shape
    components = first_factor.shape[0]
    n = lax.axis_size("col")
    second_values = second_factor.astype(jnp.float32)
    gram_first_part = gram_of(first_factor)
    gram_second_part = gram_of(second_factor)
    block_t = col_gather_t(first_factor.T, n)
    frame_part = frame_pass(tensor, block_t, second_values.T).T
    scaled_second = gram_second_part * (1.0 / lax.axis_size("row"))
    summed = all_reduce(jnp.concatenate([frame_part, gram_first_part, scaled_second], axis=1), n, 3)
    frame_sum = summed[:, :frame_count]
    gram_first = summed[:, frame_count:frame_count + components]
    gram_second = summed[:, frame_count + components:]
    frames = ridge_solve(gram_first * gram_second, frame_sum)
    gram_frames = jnp.dot(frames, frames.T, precision=lax.Precision.HIGHEST)
    full_part = accumulate_pass_t(tensor, frames, second_values)
    inverse = ridge_solve(gram_second * gram_frames, jnp.eye(components, dtype=jnp.float32))
    new_block_t = solve_and_gather_t(full_part, inverse.T, n, 1)
    gram_new_part = lax.dot_general(
        new_block_t, new_block_t, (((0,), (0,)), ((), ())), preferred_element_type=jnp.float32
    )
    second_part_t = second_pass(tensor, new_block_t, frames)
    summed_new = row_sum(jnp.concatenate([second_part_t, gram_new_part], axis=0), n, 4)
    second_sum = summed_new[:col_count].T
    gram_new = summed_new[col_count:]
    new_second = ridge_solve(gram_new * gram_frames, second_sum)
    full_next = accumulate_pass_t(tensor, frames, new_second)
    mode_one = col_reduce_scatter(full_next, n, 2)
    return (frames, mode_one)


def solution(mesh):
    return jax.shard_map(
        local,
        mesh=mesh,
        in_specs=(P(None, "col", "row"), P(None, ("row", "col")), P(None, "col")),
        out_specs=(P(), P(None, ("row", "col"))),
        check_vma=False,
    )
```

```python
import functools

import jax
import jax.numpy as jnp
from jax import lax
from jax.experimental import pallas as pl
from jax.experimental.pallas import tpu as pltpu
from jax.sharding import PartitionSpec as P

ridge_weight = 0.05
MESH_ID = pl.DeviceIdType.MESH


def ridge_solve(gram, right_side):
    order_size = gram.shape[0]
    factor_low = jnp.linalg.cholesky(gram + ridge_weight * jnp.eye(order_size, dtype=jnp.float32))
    middle = lax.linalg.triangular_solve(factor_low, right_side, left_side=True, lower=True)
    return lax.linalg.triangular_solve(
        factor_low, middle, left_side=True, lower=True, transpose_a=True
    )


def gram_of(factor):
    return jnp.dot(factor, factor.T, preferred_element_type=jnp.float32)


STREAM_FRAMES = 32
PROJECT_FRAMES = 64


def _frame_kernel(block_t_ref, second_t_ref, slab_ref, out_ref):
    frames, width, rows = slab_ref.shape
    projected = jnp.dot(
        slab_ref[...].reshape(frames * width, rows), block_t_ref[...],
        preferred_element_type=jnp.float32,
    ).reshape(frames, width, block_t_ref.shape[1])
    out_ref[...] = jnp.sum(projected * second_t_ref[...][None], axis=1)


def _second_kernel(block_t_ref, frames_t_ref, slab_ref, out_ref):
    frames, width, rows = slab_ref.shape

    @pl.when(pl.program_id(0) == 0)
    def _():
        out_ref[...] = jnp.zeros_like(out_ref)

    projected = jnp.dot(
        slab_ref[...].reshape(frames * width, rows), block_t_ref[...],
        preferred_element_type=jnp.float32,
    ).reshape(frames, width, block_t_ref.shape[1])
    out_ref[...] += jnp.sum(projected * frames_t_ref[...][:, None, :], axis=0)


def _slab_spec(width, rows, frames=STREAM_FRAMES):
    return pl.BlockSpec((frames, width, rows), lambda s: (s, 0, 0))


def _whole(shape):
    return pl.BlockSpec(shape, lambda s: (0,) * len(shape))


def frame_pass(tensor, block_t, second_t):
    frame_count, width, rows = tensor.shape
    components = block_t.shape[1]
    return pl.pallas_call(
        _frame_kernel,
        grid=(frame_count // PROJECT_FRAMES,),
        in_specs=[
            _whole(block_t.shape), _whole(second_t.shape), _slab_spec(width, rows, PROJECT_FRAMES)
        ],
        out_specs=pl.BlockSpec((PROJECT_FRAMES, components), lambda s: (s, 0)),
        out_shape=jax.ShapeDtypeStruct((frame_count, components), jnp.float32),
        cost_estimate=pl.CostEstimate(
            flops=2 * components * frame_count * width * rows, transcendentals=0,
            bytes_accessed=2 * frame_count * width * rows,
        ),
    )(block_t, second_t, tensor)


def second_pass(tensor, block_t, frames_t):
    frame_count, width, rows = tensor.shape
    components = block_t.shape[1]
    return pl.pallas_call(
        _second_kernel,
        grid=(frame_count // PROJECT_FRAMES,),
        in_specs=[
            _whole(block_t.shape),
            pl.BlockSpec((PROJECT_FRAMES, components), lambda s: (s, 0)),
            _slab_spec(width, rows, PROJECT_FRAMES),
        ],
        out_specs=_whole((width, components)),
        out_shape=jax.ShapeDtypeStruct((width, components), jnp.float32),
        cost_estimate=pl.CostEstimate(
            flops=2 * components * frame_count * width * rows, transcendentals=0,
            bytes_accessed=2 * frame_count * width * rows,
        ),
    )(block_t, frames_t, tensor)


def _accumulate_kernel(frames_ref, tiled_ref, slab_ref, out_ref, total_ref):
    frames, width, rows = slab_ref.shape
    step = pl.program_id(0)

    @pl.when(step == 0)
    def _():
        total_ref[...] = jnp.zeros_like(total_ref)

    frame_count = frames_ref.shape[1]
    span = frames * width
    which = lax.broadcasted_iota(jnp.int32, (frame_count, span), 0) - step * frames
    column = lax.broadcasted_iota(jnp.int32, (frame_count, span), 1)
    expand = ((column >= which * width) & (column < which * width + width)).astype(jnp.bfloat16)
    rest = frames_ref[...]
    repeated = jnp.zeros((frames_ref.shape[0], span), jnp.float32)
    for _ in range(3):
        piece = rest.astype(jnp.bfloat16)
        rest = rest - piece.astype(jnp.float32)
        repeated = repeated + jnp.dot(piece, expand, preferred_element_type=jnp.float32)
    weights = (repeated * tiled_ref[...]).astype(jnp.bfloat16)
    total_ref[...] += jnp.dot(
        weights, slab_ref[...].reshape(span, rows), preferred_element_type=jnp.float32
    )

    @pl.when(step == pl.num_programs(0) - 1)
    def _():
        out_ref[...] = total_ref[...].T


def accumulate_pass_t(tensor, frames, second):
    frame_count, width, rows = tensor.shape
    components = frames.shape[0]
    tiled = jnp.tile(second, (1, STREAM_FRAMES))
    return pl.pallas_call(
        _accumulate_kernel,
        grid=(frame_count // STREAM_FRAMES,),
        in_specs=[_whole(frames.shape), _whole(tiled.shape), _slab_spec(width, rows)],
        out_specs=_whole((rows, components)),
        out_shape=jax.ShapeDtypeStruct((rows, components), jnp.float32),
        scratch_shapes=[pltpu.VMEM((components, rows), jnp.float32)],
        cost_estimate=pl.CostEstimate(
            flops=2 * components * frame_count * width * rows, transcendentals=0,
            bytes_accessed=2 * frame_count * width * rows,
        ),
    )(frames, tiled, tensor)


def _split(n):
    inner = next(d for d in (8, 4, 2, 1) if n % d == 0 and d * d <= n)
    return inner, n // inner


def _exchange_kernel(n, rows, mode, *refs):
    if mode == "solve":
        send_ref, op_ref, out_ref = refs[:3]
        scratch = refs[3:]
    else:
        send_ref, out_ref = refs[:2]
        scratch = refs[2:]
    me = lax.axis_index("col")
    row = lax.axis_index("row")
    inner, outer = _split(n)
    low = lax.rem(me, inner)
    high = me // inner

    def in_low(peer):
        return (row, high * inner + peer)

    def in_high(peer):
        return (row, peer * inner + low)

    def in_row(peer):
        return (peer, me)

    def exchange(count, mine, device, source, landing, sends, recvs):
        def descriptor(peer, slot):
            return pltpu.make_async_remote_copy(
                src_ref=source(peer),
                dst_ref=landing.at[slot],
                send_sem=sends.at[peer],
                recv_sem=recvs.at[slot],
                device_id=device(peer),
                device_id_type=MESH_ID,
            )

        def start(t, carry):
            peer = lax.rem(mine + 1 + t, count)
            descriptor(peer, mine).start()
            return carry

        lax.fori_loop(0, count - 1, start, 0)

        def finish(t, carry):
            peer = lax.rem(mine + 1 + t, count)
            copy = descriptor(peer, peer)
            copy.wait_send()
            copy.wait_recv()
            return carry

        lax.fori_loop(0, count - 1, finish, 0)
        landing[mine] = source(mine)[...]

    if mode == "rowsum":
        groups = [(rows, row, in_row)]
    else:
        groups = [(inner, low, in_low), (outer, high, in_high)]
        if mode == "allreduce":
            groups.append((rows, row, in_row))
    barrier = pltpu.get_barrier_semaphore()
    for count, mine, device in groups:
        def greet(t, carry, count=count, mine=mine, device=device):
            peer = lax.rem(mine + 1 + t, count)
            pl.semaphore_signal(barrier, inc=1, device_id=device(peer), device_id_type=MESH_ID)
            return carry

        lax.fori_loop(0, count - 1, greet, 0)
    pl.semaphore_wait(barrier, sum(count - 1 for count, _, _ in groups))

    scratch = list(scratch)

    def take(k):
        taken = scratch[:k]
        del scratch[:k]
        return taken

    def gather(piece_ref):
        bundle, s1, r1 = take(3)
        exchange(inner, low, in_low, lambda peer: piece_ref, bundle, s1, r1)
        everything, s2, r2 = take(3)
        exchange(outer, high, in_high, lambda peer: bundle, everything, s2, r2)
        out_ref[...] = everything[...]

    if mode == "rowsum":
        landing, s1, r1 = take(3)
        exchange(rows, row, in_row, lambda peer: send_ref, landing, s1, r1)
        out_ref[...] = jnp.sum(landing[...], axis=0)
        return
    if mode == "gather":
        gather(send_ref)
        return
    landing, s1, r1, partial = take(4)
    exchange(outer, high, in_high, lambda peer: send_ref.at[peer], landing, s1, r1)
    partial[...] = jnp.sum(landing[...], axis=0)
    if mode == "scatter":
        landing2, s2, r2 = take(3)
        exchange(inner, low, in_low, lambda peer: partial.at[peer], landing2, s2, r2)
        out_ref[...] = jnp.sum(landing2[...], axis=0)
        return
    if mode == "solve":
        landing2, s2, r2, solved = take(4)
        exchange(inner, low, in_low, lambda peer: partial.at[peer], landing2, s2, r2)
        chunk = jnp.sum(landing2[...], axis=0)
        solved[...] = jnp.dot(
            chunk, op_ref[...], precision=lax.Precision.HIGHEST, preferred_element_type=jnp.float32
        ).astype(solved.dtype)
        gather(solved)
        return
    landing2, s2, r2, bundle = take(4)
    exchange(inner, low, in_low, lambda peer: partial, landing2, s2, r2)
    bundle[...] = jnp.sum(landing2[...], axis=0)
    row_landing, s3, r3, total = take(4)
    exchange(rows, row, in_row, lambda peer: bundle, row_landing, s3, r3)
    total[...] = jnp.sum(row_landing[...], axis=0)
    everything, s4, r4 = take(3)
    exchange(outer, high, in_high, lambda peer: total, everything, s4, r4)
    out_ref[...] = everything[...]


def col_exchange(send, n, mode, collective_id, op=None, out_dtype=None):
    rows = lax.axis_size("row")
    inner, outer = _split(n)
    dtype = send.dtype

    def stage(count, piece, kind=dtype):
        return [
            pltpu.VMEM((count,) + piece, kind),
            pltpu.SemaphoreType.DMA((count,)),
            pltpu.SemaphoreType.DMA((count,)),
        ]

    if mode == "rowsum":
        piece = tuple(send.shape)
        out_shape = piece
        scratch = stage(rows, piece)
    elif mode == "gather":
        piece = tuple(send.shape)
        out_shape = (outer, inner) + piece
        scratch = stage(inner, piece) + stage(outer, (inner,) + piece)
    else:
        piece = tuple(send.shape[2:])
        out_shape = piece if mode == "scatter" else (outer, inner) + piece
        bundle = (inner,) + piece
        scratch = stage(outer, bundle) + [pltpu.VMEM(bundle, dtype)]
        if mode == "scatter":
            scratch += stage(inner, piece)
        elif mode == "solve":
            out_shape = (outer, inner) + piece
            scratch += stage(inner, piece) + [pltpu.VMEM(piece, out_dtype)]
            scratch += stage(inner, piece, out_dtype) + stage(outer, (inner,) + piece, out_dtype)
        else:
            scratch += stage(inner, bundle) + [pltpu.VMEM(bundle, dtype)]
            scratch += stage(rows, bundle) + [pltpu.VMEM(bundle, dtype)]
            scratch += stage(outer, bundle)
    operands = (send,) if op is None else (send, op)
    return pl.pallas_call(
        functools.partial(_exchange_kernel, n, rows, mode),
        out_shape=jax.ShapeDtypeStruct(out_shape, out_dtype or dtype),
        in_specs=[pl.BlockSpec(memory_space=pltpu.VMEM)] * len(operands),
        out_specs=pl.BlockSpec(memory_space=pltpu.VMEM),
        scratch_shapes=scratch,
        compiler_params=pltpu.CompilerParams(collective_id=collective_id, has_side_effects=True),
    )(*operands)


def _chunk_order(chunks, n):
    inner, outer = _split(n)
    return chunks.reshape((outer, inner) + chunks.shape[1:])


def _col_order(gathered, n):
    return gathered.reshape((n,) + gathered.shape[2:])


def col_gather_t(piece_t, n):
    gathered = _col_order(col_exchange(piece_t, n, "gather", 0), n)
    return gathered.reshape(n * piece_t.shape[0], piece_t.shape[1])


def col_reduce_scatter(full_t, n, collective_id):
    width = full_t.shape[0] // n
    chunks = _chunk_order(full_t.reshape(n, width, full_t.shape[1]), n)
    return col_exchange(chunks, n, "scatter", collective_id).T


def all_reduce_t(full_t, n, collective_id):
    width = full_t.shape[0] // n
    chunks = _chunk_order(full_t.reshape(n, width, full_t.shape[1]), n)
    summed_t = _col_order(col_exchange(chunks, n, "allreduce", collective_id), n)
    return summed_t.reshape(full_t.shape)


def solve_and_gather_t(full_t, operator_t, n, collective_id):
    width = full_t.shape[0] // n
    chunks = _chunk_order(full_t.reshape(n, width, full_t.shape[1]), n)
    gathered = col_exchange(
        chunks, n, "solve", collective_id, op=operator_t, out_dtype=jnp.bfloat16
    )
    return gathered.reshape(n * width, full_t.shape[1])


def row_sum(piece, n, collective_id):
    return col_exchange(piece, n, "rowsum", collective_id)


def local(tensor, first_factor, second_factor):
    frame_count, col_count, row_count = tensor.shape
    components = first_factor.shape[0]
    n = lax.axis_size("col")
    second_values = second_factor.astype(jnp.float32)
    gram_first_part = gram_of(first_factor)
    gram_second_part = gram_of(second_factor)
    block_t = col_gather_t(first_factor.T, n)
    frame_part_t = frame_pass(tensor, block_t, second_values.T)
    scaled_second = gram_second_part * (1.0 / lax.axis_size("row"))
    summed_t = all_reduce_t(
        jnp.concatenate([frame_part_t, gram_first_part.T, scaled_second.T], axis=0), n, 3
    )
    frame_sum = summed_t[:frame_count].T
    gram_first = summed_t[frame_count:frame_count + components].T
    gram_second = summed_t[frame_count + components:].T
    frames = ridge_solve(gram_first * gram_second, frame_sum)
    gram_frames = jnp.dot(frames, frames.T, precision=lax.Precision.HIGHEST)
    full_part = accumulate_pass_t(tensor, frames, second_values)
    inverse = ridge_solve(gram_second * gram_frames, jnp.eye(components, dtype=jnp.float32))
    new_block_t = solve_and_gather_t(full_part, inverse.T, n, 1)
    gram_new_part = lax.dot_general(
        new_block_t, new_block_t, (((0,), (0,)), ((), ())), preferred_element_type=jnp.float32
    )
    second_part_t = second_pass(tensor, new_block_t, frames.T)
    summed_new = row_sum(jnp.concatenate([second_part_t, gram_new_part], axis=0), n, 4)
    second_sum = summed_new[:col_count].T
    gram_new = summed_new[col_count:]
    new_second = ridge_solve(gram_new * gram_frames, second_sum)
    full_next = accumulate_pass_t(tensor, frames, new_second)
    mode_one = col_reduce_scatter(full_next, n, 2)
    return (frames, mode_one)


def solution(mesh):
    return jax.shard_map(
        local,
        mesh=mesh,
        in_specs=(P(None, "col", "row"), P(None, ("row", "col")), P(None, "col")),
        out_specs=(P(), P(None, ("row", "col"))),
        check_vma=False,
    )
```

```python
import functools

import jax
import numpy as np
import jax.numpy as jnp
from jax import lax
from jax.experimental import pallas as pl
from jax.experimental.pallas import tpu as pltpu
from jax.sharding import PartitionSpec as P

ridge_weight = 0.05
MESH_ID = pl.DeviceIdType.MESH


def ridge_solve(gram, right_side):
    order_size = gram.shape[0]
    factor_low = jnp.linalg.cholesky(gram + ridge_weight * jnp.eye(order_size, dtype=jnp.float32))
    middle = lax.linalg.triangular_solve(factor_low, right_side, left_side=True, lower=True)
    return lax.linalg.triangular_solve(
        factor_low, middle, left_side=True, lower=True, transpose_a=True
    )


def gram_of(factor):
    return jnp.dot(factor, factor.T, preferred_element_type=jnp.float32)


STREAM_FRAMES = 32
PROJECT_FRAMES = 64


def _frame_kernel(block_t_ref, second_t_ref, slab_ref, out_ref):
    frames, width, rows = slab_ref.shape
    projected = jnp.dot(
        slab_ref[...].reshape(frames * width, rows), block_t_ref[...],
        preferred_element_type=jnp.float32,
    ).reshape(frames, width, block_t_ref.shape[1])
    out_ref[...] = jnp.sum(projected * second_t_ref[...][None], axis=1)


def _second_kernel(block_t_ref, frames_t_ref, slab_ref, out_ref):
    frames, width, rows = slab_ref.shape

    @pl.when(pl.program_id(0) == 0)
    def _():
        out_ref[...] = jnp.zeros_like(out_ref)

    projected = jnp.dot(
        slab_ref[...].reshape(frames * width, rows), block_t_ref[...],
        preferred_element_type=jnp.float32,
    ).reshape(frames, width, block_t_ref.shape[1])
    out_ref[...] += jnp.sum(projected * frames_t_ref[...][:, None, :], axis=0)


def _slab_spec(width, rows, frames=STREAM_FRAMES):
    return pl.BlockSpec((frames, width, rows), lambda s: (s, 0, 0))


def _whole(shape):
    return pl.BlockSpec(shape, lambda s: (0,) * len(shape))


def frame_pass(tensor, block_t, second_t):
    frame_count, width, rows = tensor.shape
    components = block_t.shape[1]
    return pl.pallas_call(
        _frame_kernel,
        grid=(frame_count // PROJECT_FRAMES,),
        in_specs=[
            _whole(block_t.shape), _whole(second_t.shape), _slab_spec(width, rows, PROJECT_FRAMES)
        ],
        out_specs=pl.BlockSpec((PROJECT_FRAMES, components), lambda s: (s, 0)),
        out_shape=jax.ShapeDtypeStruct((frame_count, components), jnp.float32),
        cost_estimate=pl.CostEstimate(
            flops=2 * components * frame_count * width * rows, transcendentals=0,
            bytes_accessed=2 * frame_count * width * rows,
        ),
    )(block_t, second_t, tensor)


def second_pass(tensor, block_t, frames_t):
    frame_count, width, rows = tensor.shape
    components = block_t.shape[1]
    return pl.pallas_call(
        _second_kernel,
        grid=(frame_count // PROJECT_FRAMES,),
        in_specs=[
            _whole(block_t.shape),
            pl.BlockSpec((PROJECT_FRAMES, components), lambda s: (s, 0)),
            _slab_spec(width, rows, PROJECT_FRAMES),
        ],
        out_specs=_whole((width, components)),
        out_shape=jax.ShapeDtypeStruct((width, components), jnp.float32),
        cost_estimate=pl.CostEstimate(
            flops=2 * components * frame_count * width * rows, transcendentals=0,
            bytes_accessed=2 * frame_count * width * rows,
        ),
    )(block_t, frames_t, tensor)


def _accumulate_kernel(frames_ref, tiled_ref, expand_ref, slab_ref, out_ref, total_ref):
    frames, width, rows = slab_ref.shape
    step = pl.program_id(0)

    @pl.when(step == 0)
    def _():
        total_ref[...] = jnp.zeros_like(total_ref)

    span = frames * width
    expand = expand_ref[...]
    rest = frames_ref[...]
    repeated = jnp.zeros((frames_ref.shape[0], span), jnp.float32)
    for _ in range(3):
        piece = rest.astype(jnp.bfloat16)
        rest = rest - piece.astype(jnp.float32)
        repeated = repeated + jnp.dot(piece, expand, preferred_element_type=jnp.float32)
    weights = (repeated * tiled_ref[...]).astype(jnp.bfloat16)
    total_ref[...] += jnp.dot(
        weights, slab_ref[...].reshape(span, rows), preferred_element_type=jnp.float32
    )

    @pl.when(step == pl.num_programs(0) - 1)
    def _():
        out_ref[...] = total_ref[...].T


def accumulate_pass_t(tensor, frames, second):
    frame_count, width, rows = tensor.shape
    components = frames.shape[0]
    tiled = jnp.tile(second, (1, STREAM_FRAMES))
    steps = frame_count // STREAM_FRAMES
    span = STREAM_FRAMES * width
    owner = np.arange(frame_count)[:, None] - np.arange(steps)[:, None, None] * STREAM_FRAMES
    column = np.arange(span)[None, None, :]
    expand = jnp.asarray(
        ((column >= owner * width) & (column < owner * width + width)).astype(np.float32),
        jnp.bfloat16,
    )
    return pl.pallas_call(
        _accumulate_kernel,
        grid=(steps,),
        in_specs=[
            _whole(frames.shape), _whole(tiled.shape),
            pl.BlockSpec((None, frame_count, span), lambda s: (s, 0, 0)),
            _slab_spec(width, rows),
        ],
        out_specs=_whole((rows, components)),
        out_shape=jax.ShapeDtypeStruct((rows, components), jnp.float32),
        scratch_shapes=[pltpu.VMEM((components, rows), jnp.float32)],
        cost_estimate=pl.CostEstimate(
            flops=2 * components * frame_count * width * rows, transcendentals=0,
            bytes_accessed=2 * frame_count * width * rows,
        ),
    )(frames, tiled, expand, tensor)


def _split(n):
    inner = next(d for d in (8, 4, 2, 1) if n % d == 0 and d * d <= n)
    return inner, n // inner


def _exchange_kernel(n, rows, mode, *refs):
    if mode == "solve":
        send_ref, op_ref, out_ref = refs[:3]
        scratch = refs[3:]
    else:
        send_ref, out_ref = refs[:2]
        scratch = refs[2:]
    me = lax.axis_index("col")
    row = lax.axis_index("row")
    inner, outer = _split(n)
    low = lax.rem(me, inner)
    high = me // inner

    def in_low(peer):
        return (row, high * inner + peer)

    def in_high(peer):
        return (row, peer * inner + low)

    def in_row(peer):
        return (peer, me)

    def exchange(count, mine, device, source, landing, sends, recvs):
        def descriptor(peer, slot):
            return pltpu.make_async_remote_copy(
                src_ref=source(peer),
                dst_ref=landing.at[slot],
                send_sem=sends.at[peer],
                recv_sem=recvs.at[slot],
                device_id=device(peer),
                device_id_type=MESH_ID,
            )

        def start(t, carry):
            peer = lax.rem(mine + 1 + t, count)
            descriptor(peer, mine).start()
            return carry

        lax.fori_loop(0, count - 1, start, 0)

        def finish(t, carry):
            peer = lax.rem(mine + 1 + t, count)
            copy = descriptor(peer, peer)
            copy.wait_send()
            copy.wait_recv()
            return carry

        lax.fori_loop(0, count - 1, finish, 0)
        landing[mine] = source(mine)[...]

    if mode == "rowsum":
        groups = [(rows, row, in_row)]
    else:
        groups = [(inner, low, in_low), (outer, high, in_high)]
        if mode == "allreduce":
            groups.append((rows, row, in_row))
    barrier = pltpu.get_barrier_semaphore()
    for count, mine, device in groups:
        def greet(t, carry, count=count, mine=mine, device=device):
            peer = lax.rem(mine + 1 + t, count)
            pl.semaphore_signal(barrier, inc=1, device_id=device(peer), device_id_type=MESH_ID)
            return carry

        lax.fori_loop(0, count - 1, greet, 0)
    pl.semaphore_wait(barrier, sum(count - 1 for count, _, _ in groups))

    scratch = list(scratch)

    def take(k):
        taken = scratch[:k]
        del scratch[:k]
        return taken

    def gather(piece_ref):
        bundle, s1, r1 = take(3)
        exchange(inner, low, in_low, lambda peer: piece_ref, bundle, s1, r1)
        everything, s2, r2 = take(3)
        exchange(outer, high, in_high, lambda peer: bundle, everything, s2, r2)
        out_ref[...] = everything[...]

    if mode == "rowsum":
        landing, s1, r1 = take(3)
        exchange(rows, row, in_row, lambda peer: send_ref, landing, s1, r1)
        out_ref[...] = jnp.sum(landing[...], axis=0)
        return
    if mode == "gather":
        gather(send_ref)
        return
    landing, s1, r1, partial = take(4)
    exchange(outer, high, in_high, lambda peer: send_ref.at[peer], landing, s1, r1)
    partial[...] = jnp.sum(landing[...], axis=0)
    if mode == "scatter":
        landing2, s2, r2 = take(3)
        exchange(inner, low, in_low, lambda peer: partial.at[peer], landing2, s2, r2)
        out_ref[...] = jnp.sum(landing2[...], axis=0)
        return
    if mode == "solve":
        landing2, s2, r2, solved = take(4)
        exchange(inner, low, in_low, lambda peer: partial.at[peer], landing2, s2, r2)
        chunk = jnp.sum(landing2[...], axis=0)
        solved[...] = jnp.dot(
            chunk, op_ref[...], precision=lax.Precision.HIGHEST, preferred_element_type=jnp.float32
        ).astype(solved.dtype)
        gather(solved)
        return
    landing2, s2, r2, bundle = take(4)
    exchange(inner, low, in_low, lambda peer: partial, landing2, s2, r2)
    bundle[...] = jnp.sum(landing2[...], axis=0)
    row_landing, s3, r3, total = take(4)
    exchange(rows, row, in_row, lambda peer: bundle, row_landing, s3, r3)
    total[...] = jnp.sum(row_landing[...], axis=0)
    everything, s4, r4 = take(3)
    exchange(outer, high, in_high, lambda peer: total, everything, s4, r4)
    out_ref[...] = everything[...]


def col_exchange(send, n, mode, collective_id, op=None, out_dtype=None):
    rows = lax.axis_size("row")
    inner, outer = _split(n)
    dtype = send.dtype

    def stage(count, piece, kind=dtype):
        return [
            pltpu.VMEM((count,) + piece, kind),
            pltpu.SemaphoreType.DMA((count,)),
            pltpu.SemaphoreType.DMA((count,)),
        ]

    if mode == "rowsum":
        piece = tuple(send.shape)
        out_shape = piece
        scratch = stage(rows, piece)
    elif mode == "gather":
        piece = tuple(send.shape)
        out_shape = (outer, inner) + piece
        scratch = stage(inner, piece) + stage(outer, (inner,) + piece)
    else:
        piece = tuple(send.shape[2:])
        out_shape = piece if mode == "scatter" else (outer, inner) + piece
        bundle = (inner,) + piece
        scratch = stage(outer, bundle) + [pltpu.VMEM(bundle, dtype)]
        if mode == "scatter":
            scratch += stage(inner, piece)
        elif mode == "solve":
            out_shape = (outer, inner) + piece
            scratch += stage(inner, piece) + [pltpu.VMEM(piece, out_dtype)]
            scratch += stage(inner, piece, out_dtype) + stage(outer, (inner,) + piece, out_dtype)
        else:
            scratch += stage(inner, bundle) + [pltpu.VMEM(bundle, dtype)]
            scratch += stage(rows, bundle) + [pltpu.VMEM(bundle, dtype)]
            scratch += stage(outer, bundle)
    operands = (send,) if op is None else (send, op)
    return pl.pallas_call(
        functools.partial(_exchange_kernel, n, rows, mode),
        out_shape=jax.ShapeDtypeStruct(out_shape, out_dtype or dtype),
        in_specs=[pl.BlockSpec(memory_space=pltpu.VMEM)] * len(operands),
        out_specs=pl.BlockSpec(memory_space=pltpu.VMEM),
        scratch_shapes=scratch,
        compiler_params=pltpu.CompilerParams(collective_id=collective_id, has_side_effects=True),
    )(*operands)


def _chunk_order(chunks, n):
    inner, outer = _split(n)
    return chunks.reshape((outer, inner) + chunks.shape[1:])


def _col_order(gathered, n):
    return gathered.reshape((n,) + gathered.shape[2:])


def col_gather_t(piece_t, n):
    gathered = _col_order(col_exchange(piece_t, n, "gather", 0), n)
    return gathered.reshape(n * piece_t.shape[0], piece_t.shape[1])


def col_reduce_scatter(full_t, n, collective_id):
    width = full_t.shape[0] // n
    chunks = _chunk_order(full_t.reshape(n, width, full_t.shape[1]), n)
    return col_exchange(chunks, n, "scatter", collective_id).T


def all_reduce(full, n, collective_id):
    width = full.shape[1] // n
    chunks = _chunk_order(full.T.reshape(n, width, full.shape[0]), n)
    summed_t = _col_order(col_exchange(chunks, n, "allreduce", collective_id), n)
    return summed_t.reshape(n * width, full.shape[0]).T


def solve_and_gather_t(full_t, operator_t, n, collective_id):
    width = full_t.shape[0] // n
    chunks = _chunk_order(full_t.reshape(n, width, full_t.shape[1]), n)
    gathered = col_exchange(
        chunks, n, "solve", collective_id, op=operator_t, out_dtype=jnp.bfloat16
    )
    return gathered.reshape(n * width, full_t.shape[1])


def row_sum(piece, n, collective_id):
    return col_exchange(piece, n, "rowsum", collective_id)


def local(tensor, first_factor, second_factor):
    frame_count, col_count, row_count = tensor.shape
    components = first_factor.shape[0]
    n = lax.axis_size("col")
    second_values = second_factor.astype(jnp.float32)
    gram_first_part = gram_of(first_factor)
    gram_second_part = gram_of(second_factor)
    block_t = col_gather_t(first_factor.T, n)
    frame_part = frame_pass(tensor, block_t, second_values.T).T
    scaled_second = gram_second_part * (1.0 / lax.axis_size("row"))
    summed = all_reduce(jnp.concatenate([frame_part, gram_first_part, scaled_second], axis=1), n, 3)
    frame_sum = summed[:, :frame_count]
    gram_first = summed[:, frame_count:frame_count + components]
    gram_second = summed[:, frame_count + components:]
    frames = ridge_solve(gram_first * gram_second, frame_sum)
    gram_frames = jnp.dot(frames, frames.T, precision=lax.Precision.HIGHEST)
    full_part = accumulate_pass_t(tensor, frames, second_values)
    inverse = ridge_solve(gram_second * gram_frames, jnp.eye(components, dtype=jnp.float32))
    new_block_t = solve_and_gather_t(full_part, inverse.T, n, 1)
    gram_new_part = lax.dot_general(
        new_block_t, new_block_t, (((0,), (0,)), ((), ())), preferred_element_type=jnp.float32
    )
    second_part_t = second_pass(tensor, new_block_t, frames.T)
    summed_new = row_sum(jnp.concatenate([second_part_t, gram_new_part], axis=0), n, 4)
    second_sum = summed_new[:col_count].T
    gram_new = summed_new[col_count:]
    new_second = ridge_solve(gram_new * gram_frames, second_sum)
    full_next = accumulate_pass_t(tensor, frames, new_second)
    mode_one = col_reduce_scatter(full_next, n, 2)
    return (frames, mode_one)


def solution(mesh):
    return jax.shard_map(
        local,
        mesh=mesh,
        in_specs=(P(None, "col", "row"), P(None, ("row", "col")), P(None, "col")),
        out_specs=(P(), P(None, ("row", "col"))),
        check_vma=False,
    )
```
